32 devices in a mesh: group: 2 (over core), trow: 2 (over y), tcol: 8 (over z, x).
Axes of the slice: x: 2, y: 2, z: 4, core: 2. Of those that a mesh axis runs over, the one named last changes fastest.
Arguments:
- displacement: float32 [3, 128, 64, 256], P(None, ('group', 'trow'), 'tcol'), may hold values from -6 to 6
- velocity: float32 [3, 128, 64, 256], P(None, ('group', 'trow'), 'tcol'), may hold values from -6 to 6
- stiffness: float32 [128, 64], P(('group', 'trow'), 'tcol'), may hold values from 4 to 12
- wet_position: float32 [3, 8192], P(None, ('group', 'trow', 'tcol')), may hold values from -6 to 6
- wet_normal: float32 [3, 8192], P(None, ('group', 'trow', 'tcol')), may hold values from -6 to 6
- wet_area: float32 [8192], P(('group', 'trow', 'tcol')), may hold values from 0.022097087 to 0.22097087
- wet_map: int32 [8192], P(('group', 'trow', 'tcol')), may hold values from 0 to 255
Outputs:
- displacement_out: float32 [3, 128, 64, 256], P(None, ('group', 'trow'), 'tcol')
- velocity_out: float32 [3, 128, 64, 256], P(None, ('group', 'trow'), 'tcol')
The draws below stay inside these ranges and needn't reach their ends.
Inputs may be any that keep to these rules, and one draw needn't show every extreme that they name: Each wet point lies on the patch of nodes of the device that holds it: wet_map gives a * 8 + b for the node (a, b) of that patch.
All inputs are finite; a program needn't handle non-finite values.
Results may differ from the reference program's by a relative error of at most 0.0018.
Values may be sent and summed in bfloat16 or wider, within the bound.
A program may use at most 128 MiB of HBM per device.

```python
import math
import jax
import jax.numpy as jnp
from jax import lax

LOADS = 64
LAYERS = 4
SUBSTEPS = 4
COUPLED = 2
WET_DEV = 256
PA = 32
PB = 8
NA = 128
NB = 64
W = 8192
N_TCOL = 8


def state_field(key, salt):
    key = jax.random.fold_in(key, salt)
    first_key = jax.random.fold_in(key, 0)
    shape = (3, NA, NB, LAYERS * LOADS)
    layer = lax.broadcasted_iota(jnp.int32, shape, 3) // LOADS
    inner = layer < LAYERS - 1
    base = jax.random.normal(first_key, shape, jnp.float32)
    values = base * jnp.where(inner, 2.5, 1.0).astype(jnp.float32)
    return jnp.clip(values, -6.0, 6.0).astype(jnp.float32)


def draw_displacement(key, part):
    return state_field(key, 7001)


def draw_velocity(key, part):
    return state_field(key, 7002)


def place_ends(result, rng, low, largest):
    shape = result.shape
    place = [jax.random.randint(jax.random.fold_in(rng, axis), (), 0, shape[axis]) for axis in range(len(shape))]
    result = result.at[tuple(place)].set(low)
    longest = shape.index(max(shape))
    place[longest] = (place[longest] + 1) % shape[longest]
    return result.at[tuple(place)].set(largest)


def levels(rng, extent, cuts, smallest, top_value):
    level, own = 1.0, jax.random.fold_in(rng, 6)
    for dim, blocks in cuts:
        draws = jnp.exp(jax.random.uniform(jax.random.fold_in(own, dim), (blocks,), jnp.float32, smallest / len(cuts), top_value / len(cuts)))
        level = level * jnp.repeat(draws, extent[dim] // blocks).reshape([-1 if axis == dim else 1 for axis in range(len(extent))])
    return level


def bell_draw(key, shape, deviation, reach, pieces=(), held_as=jnp.bfloat16):
    loudness = levels(key, shape, pieces, -0.22, 0.18) if pieces else 1.0
    values = jax.random.normal(key, shape, jnp.float32) * deviation * loudness
    return jnp.minimum(jnp.maximum(values, -reach), reach).astype(held_as)


def setup_inputs(seed: int = 0) -> dict:
    keys = jax.random.split(jax.random.key(seed), 8)
    displacement = draw_displacement(jax.random.fold_in(keys[7], 71), 0)
    velocity = draw_velocity(jax.random.fold_in(keys[7], 71), 0)
    stiffness = jnp.clip(jnp.exp(math.log(12.0) - 1.0986123 * jax.random.uniform(keys[2], (NA, NB), jnp.float32) ** levels(keys[2], (NA, NB), ((0, 4), (1, 8)), -0.2, 0.2)), 4.0, 12.0)
    wet_position = bell_draw(keys[3], (3, W), 1.0, 6.0, ((1, 32),), jnp.float32)
    wet_normal = bell_draw(keys[4], (3, W), 1.0, 6.0, ((1, 32),), jnp.float32)
    wet_area = jnp.clip(jnp.exp(math.log(0.22097087) - 2.3025851 * jax.random.uniform(keys[5], (W,), jnp.float32) ** levels(keys[5], (W,), ((0, 32),), -0.2, 0.2)), 0.022097087, 0.22097087)
    wet_map = place_ends(jax.random.randint(keys[6], (W,), 0, PA * PB), jax.random.fold_in(keys[6], 1), 0, (PA * PB) - 1).astype(jnp.int32)
    return dict(displacement=displacement, velocity=velocity, stiffness=stiffness, wet_position=wet_position, wet_normal=wet_normal, wet_area=wet_area, wet_map=wet_map)


SPHERE_AREA = 4.0 * math.pi
SMOOTHING = 0.1
TIME_STEP = 0.3
THICKNESS = 0.5
SPLINE_TAPS = (2.0 / 3.0, -1.0 / 12.0, -1.0 / 12.0, -1.0 / 6.0)

def spline_apply(padded, height, breadth, margin):
    middle = padded[:, margin:margin + height, margin:margin + breadth]
    summed = 2.0 * SPLINE_TAPS[0] * middle
    for offset in (1, 2, 3):
        along_rows = padded[:, margin + offset:margin + offset + height, margin:margin + breadth] + padded[:, margin - offset:margin - offset + height, margin:margin + breadth]
        along_cols = padded[:, margin:margin + height, margin + offset:margin + offset + breadth] + padded[:, margin:margin + height, margin - offset:margin - offset + breadth]
        summed = summed + SPLINE_TAPS[offset] * (along_rows + along_cols)
    return summed

def thickness_term(values, stride):
    above_layer = jnp.concatenate([values[..., stride:], values[..., -stride:]], axis=3)
    below_layer = jnp.concatenate([values[..., :stride], values[..., :-stride]], axis=3)
    return 2.0 * values - above_layer - below_layer

def advance(displacement, velocity, stiffness_grid, loading, in_plane):
    acceleration = -(stiffness_grid * in_plane) - THICKNESS * thickness_term(displacement, LOADS)
    outermost = acceleration[..., -LOADS:] + loading
    acceleration = jnp.concatenate([acceleration[..., :-LOADS], outermost], axis=3)
    velocity = velocity + TIME_STEP * acceleration
    displacement = displacement + TIME_STEP * velocity
    return (displacement, velocity)

def kernel_tile(position, normal, area, targets):
    delta_x = targets[0][None, :] - position[0][:, None]
    delta_y = targets[1][None, :] - position[1][:, None]
    delta_z = targets[2][None, :] - position[2][:, None]
    numerator = normal[0][:, None] * delta_x + normal[1][:, None] * delta_y + normal[2][:, None] * delta_z
    squared = delta_x * delta_x + delta_y * delta_y + delta_z * delta_z + SMOOTHING * SMOOTHING
    weighted = area[:, None] * numerator
    return (weighted / (SPHERE_AREA * squared * jnp.sqrt(squared))).astype(jnp.bfloat16)

def reference(displacement, velocity, stiffness, wet_position, wet_normal, wet_area, wet_map):
    wet_index = jnp.arange(W, dtype=jnp.int32)
    device = wet_index // WET_DEV
    node_row = device // N_TCOL * PA + wet_map // PB
    node_col = device % N_TCOL * PB + wet_map % PB
    node = (node_row * NB + node_col).astype(jnp.int32)
    block_size = math.gcd(W, 512)
    block_count = W // block_size
    target_blocks = wet_position.reshape(3, block_count, block_size).transpose(1, 0, 2)
    stiffness_grid = stiffness[None, :, :, None]
    for repeat in range(COUPLED):
        outer_layer = velocity[..., -LOADS:].reshape(3, NA * NB, LOADS)
        picked = jnp.take(outer_layer, node, axis=1)
        speeds = (wet_normal[0][:, None] * picked[0] + wet_normal[1][:, None] * picked[1] + wet_normal[2][:, None] * picked[2]).T
        speed_rounded = lax.optimization_barrier(speeds.astype(jnp.bfloat16)).astype(jnp.float32)

        def block_product(targets):
            tile = lax.optimization_barrier(kernel_tile(wet_position, wet_normal, wet_area, targets)).astype(jnp.float32)
            return jnp.dot(speed_rounded, tile, precision=lax.Precision.HIGHEST)
        products = lax.map(block_product, target_blocks)
        summed = products.transpose(1, 0, 2).reshape(LOADS, W)
        pressure = 0.5 * speeds + summed
        contribution = -(wet_normal[:, :, None] * pressure.T[None, :, :])
        loading = jnp.stack([jax.ops.segment_sum(contribution[component], node, num_segments=NA * NB) for component in range(3)])
        loading = loading.reshape(3, NA, NB, LOADS)

        def evolve(state):
            position_now, speed_now, force_now = state
            for substep in range(SUBSTEPS):
                padded = jnp.pad(position_now, ((0, 0), (3, 3), (3, 3), (0, 0)))
                in_plane = spline_apply(padded, NA, NB, 3)
                position_now, speed_now = advance(position_now, speed_now, stiffness_grid, force_now, in_plane)
            return (position_now, speed_now)
        displacement, velocity = lax.map(evolve, (displacement[:, None], velocity[:, None], loading[:, None]))
        displacement = displacement[:, 0]
        velocity = velocity[:, 0]
    return (displacement, velocity)
```

```python
import functools
import math

import jax
import jax.numpy as jnp
from jax import lax
from jax.experimental import pallas as pl
from jax.experimental.pallas import tpu as pltpu
from jax.sharding import PartitionSpec as P

LOADS = 64
SUBSTEPS = 4
COUPLED = 2

SPHERE_AREA = 4.0 * math.pi
SMOOTHING = 0.1
TIME_STEP = 0.3
THICKNESS = 0.5
SPLINE_TAPS = (2.0 / 3.0, -1.0 / 12.0, -1.0 / 12.0, -1.0 / 6.0)
REACH = 3
PAD = 8
MESH = pl.DeviceIdType.MESH
VMEM = pltpu.VMEM


def row_device(index, trow_count):
    return {"group": index // trow_count, "trow": lax.rem(index, trow_count)}


def whole_spec():
    return pl.BlockSpec(memory_space=pltpu.VMEM)


HIGHEST = lax.Precision.HIGHEST


def coupled_kernel(
    shape, u_in, v_in, stiff_ref, position_ref, normal_ref, area_ref, node_ref, u_out, v_out,
    field, speed_now, work, load, col_out, col_in, row_out, row_in,
    geometry, sources, targets, target_cols, normal_cols, pick, spread,
    own_speeds, packed_out, packed_in, unpacked, tiles, partial_out, partial_in,
    halo_send, halo_recv, geo_send, geo_recv, speed_send, speed_recv, part_send, part_recv,
    all_out, all_in, all_send, all_recv
):
    col_count, row_count, trow_count = shape
    parts, breadth, height, width = speed_now.shape
    half = width // 2
    points = geometry.shape[1]
    count = breadth * height
    col = lax.axis_index("tcol")
    row = lax.axis_index("group") * trow_count + lax.axis_index("trow")
    present = (col > 0, col < col_count - 1, row > 0, row < row_count - 1)
    peers = (
        {"tcol": jnp.maximum(col - 1, 0)},
        {"tcol": jnp.minimum(col + 1, col_count - 1)},
        row_device(jnp.maximum(row - 1, 0), trow_count),
        row_device(jnp.minimum(row + 1, row_count - 1), trow_count),
    )
    middle = pl.ds(PAD, height)

    def col_peer(d):
        return {"tcol": lax.rem(col + d, col_count)}

    def row_peer(d):
        return row_device(lax.rem(row + d, row_count), trow_count)

    barrier = pltpu.get_barrier_semaphore()

    @pl.loop(1, col_count)
    def _(d):
        pl.semaphore_signal(barrier, inc=1, device_id=col_peer(d), device_id_type=MESH)

    @pl.loop(1, row_count)
    def _(d):
        pl.semaphore_signal(barrier, inc=1, device_id=row_peer(d), device_id_type=MESH)

    geometry[0:3, :] = position_ref[...]
    geometry[3:6, :] = normal_ref[...] * (area_ref[...] * (1.0 / SPHERE_AREA))
    geometry[6:8, :] = jnp.zeros((2, points), jnp.float32)

    total = col_count * row_count
    me = row * col_count + col

    def any_device(index):
        r = index // col_count
        return {"group": r // trow_count, "trow": lax.rem(r, trow_count), "tcol": lax.rem(index, col_count)}

    @pl.loop(1, total)
    def _(d):
        pl.semaphore_signal(barrier, inc=1, device_id=any_device(lax.rem(me + d, total)), device_id_type=MESH)

    pl.semaphore_wait(barrier, col_count + row_count - 2 + total - 1)

    def all_copy(k, d):
        to = lax.rem(me + d, total)
        return pltpu.make_async_remote_copy(
            src_ref=all_out.at[k, to], dst_ref=all_in.at[k, me],
            send_sem=all_send.at[k, d], recv_sem=all_recv.at[k, d],
            device_id=any_device(to), device_id_type=MESH)

    def fill(k, carry):
        def one(i, c):
            all_out[k, i] = (all_in[lax.rem(k + 2, 3), i].astype(jnp.float32) + 1.0).astype(all_out.dtype) if False else jnp.zeros(all_out.shape[2:], all_out.dtype)
            return c
        lax.fori_loop(0, total, one, 0)

        @pl.loop(1, total)
        def _(d):
            all_copy(k, d).start()

        @pl.loop(1, total)
        def _(d):
            all_copy(k, d).wait_recv()

        @pl.loop(1, total)
        def _(d):
            all_copy(k, d).wait_send()
        return carry

    lax.fori_loop(0, 1, fill, 0)

    def geo_copy(kind, d):
        return pltpu.make_async_remote_copy(
            src_ref=geometry,
            dst_ref=sources.at[col] if kind == 0 else targets.at[row],
            send_sem=geo_send.at[kind, d],
            recv_sem=geo_recv.at[kind, d],
            device_id=col_peer(d) if kind == 0 else row_peer(d),
            device_id_type=MESH,
        )

    def speed_copy(repeat, d):
        return pltpu.make_async_remote_copy(
            src_ref=packed_out.at[repeat],
            dst_ref=packed_in.at[repeat, col],
            send_sem=speed_send.at[repeat, d],
            recv_sem=speed_recv.at[repeat, d],
            device_id=col_peer(d),
            device_id_type=MESH,
        )

    def part_copy(repeat, d):
        return pltpu.make_async_remote_copy(
            src_ref=partial_out.at[repeat, lax.rem(row + d, row_count)],
            dst_ref=partial_in.at[repeat, d],
            send_sem=part_send.at[repeat, d],
            recv_sem=part_recv.at[repeat, d],
            device_id=row_peer(d),
            device_id_type=MESH,
        )

    for kind, total in ((1, row_count), (0, col_count)):

        @pl.loop(1, total)
        def _(d):
            geo_copy(kind, d).start()

    sources[col] = geometry[...]
    targets[row] = geometry[...]

    field[...] = jnp.zeros_like(field)
    for part in range(parts):
        for j in range(breadth):
            for lanes in range(2):
                lines = pl.ds(lanes * breadth + j, height, stride=2 * breadth)
                cut = pl.ds(lanes * half, half)
                field[part, REACH + j, middle, cut] = u_in[part, lines, :]
                speed_now[part, j, :, cut] = v_in[part, lines, :]
    for side in range(2):

        @pl.when(jnp.logical_not(present[side]))
        def _():
            col_in[:, :, side] = jnp.zeros(col_in.shape[:2] + col_in.shape[3:], col_in.dtype)

    def as_column(line):
        return jnp.broadcast_to(line, (half, line.shape[1])).T

    for part in range(parts):
        normal_cols[part] = as_column(normal_ref[part : part + 1, :])
    spread[...] = (
        lax.broadcasted_iota(jnp.int32, (count, points), 0) == node_ref[...]
    ).astype(jnp.float32)
    pick[...] = spread[...].T

    def halo_copy(step, side, part, arriving):
        out_buffer, in_buffer = (col_out, col_in) if side < 2 else (row_out, row_in)
        own = side % 2
        other = own if arriving else 1 - own
        return pltpu.make_async_remote_copy(
            src_ref=out_buffer.at[step, part, own],
            dst_ref=in_buffer.at[step, part, other],
            send_sem=halo_send.at[step, part, side],
            recv_sem=halo_recv.at[step, part, (side // 2) * 2 + other],
            device_id=peers[side],
            device_id_type=MESH,
        )

    lane = lax.broadcasted_iota(jnp.int32, (height, half), 1)
    low = lane < half // 2
    low_half = lax.broadcasted_iota(jnp.int32, (points // 2, half), 1) < half // 2

    def pack(value):
        turned = pltpu.roll(value[points // 2 :], half // 2, 1)
        return jnp.where(low_half, turned, value[: points // 2])

    def tile(r):
        group = 32

        def block(index, carry):
            source = index // (points // half)
            lanes = pl.ds(pl.multiple_of(lax.rem(index, points // half) * half, half), half)
            line = [sources[source, k : k + 1, lanes] for k in range(6)]

            def rows_of(g, inner):
                rows = pl.ds(pl.multiple_of(g * group, group), group)
                dx = target_cols[r, 0, rows, :] - line[0]
                dy = target_cols[r, 1, rows, :] - line[1]
                dz = target_cols[r, 2, rows, :] - line[2]
                numerator = line[3] * dx + line[4] * dy + line[5] * dz
                squared = dx * dx + dy * dy + dz * dz + SMOOTHING * SMOOTHING
                inverse = lax.rsqrt(squared)
                value = numerator * inverse * (inverse * inverse)
                tiles[r, source, rows, lanes] = value.astype(jnp.bfloat16)
                return inner

            return lax.fori_loop(0, points // group, rows_of, carry, unroll=2)

        lax.fori_loop(0, col_count * (points // half), block, 0)

    def send_halos(step, part):
        for side, first in ((0, REACH), (1, breadth)):

            @pl.when(present[side])
            def _():
                for j in range(REACH):
                    col_out[step, part, side, j] = field[part, first + j, middle, :].astype(
                        col_out.dtype
                    )
                halo_copy(step, side, part, False).start()

        for side, first in ((2, PAD), (3, PAD + height - REACH)):

            @pl.when(present[side])
            def _():
                for j in range(breadth):
                    row_out[
                        step, part, side - 2, j // 2, (j % 2) * 4 : (j % 2) * 4 + REACH, :
                    ] = field[part, REACH + j, first : first + REACH, :]
                halo_copy(step, side, part, False).start()

    def local(part):
        def body(column, carry):
            a = field[part, REACH + column, middle, 0:half]
            b = field[part, REACH + column, middle, half:width]
            turned_a = pltpu.roll(a, half // 2, 1)
            turned_b = pltpu.roll(b, half // 2, 1)
            between = jnp.where(low, turned_a, turned_b)
            edge_a = jnp.where(low, a, turned_a)
            edge_b = jnp.where(low, turned_b, b)
            stiff = stiff_ref[column]
            for lanes, here, edge in ((0, a, edge_a), (1, b, edge_b)):
                cut = pl.ds(lanes * half, half)
                summed = (2.0 * SPLINE_TAPS[0]) * here
                for offset in range(1, REACH + 1):
                    summed = summed + SPLINE_TAPS[offset] * (
                        field[part, REACH + column + offset, middle, cut]
                        + field[part, REACH + column - offset, middle, cut]
                    )
                value = -(stiff * summed) - THICKNESS * (2.0 * here - between - edge)
                if lanes == 1:
                    value = value + load[part, column]
                work[part, column, :, cut] = speed_now[part, column, :, cut] + TIME_STEP * value
            return carry

        lax.fori_loop(0, breadth, body, 0)

    def complete(step, part):
        for side, first in ((2, PAD - REACH), (3, PAD + height)):

            @pl.when(present[side])
            def _():
                halo_copy(step, side, part, True).wait_recv()
                for j in range(breadth):
                    field[part, REACH + j, first : first + REACH, :] = row_in[
                        step, part, side - 2, j // 2, (j % 2) * 4 : (j % 2) * 4 + REACH, :
                    ]

        def along_rows(column, carry):
            stiff = stiff_ref[column] * (-TIME_STEP)
            for lanes in range(2):
                cut = pl.ds(lanes * half, half)
                summed = 0.0
                for offset in range(1, REACH + 1):
                    summed = summed + SPLINE_TAPS[offset] * (
                        field[part, REACH + column, pl.ds(PAD + offset, height), cut]
                        + field[part, REACH + column, pl.ds(PAD - offset, height), cut]
                    )
                work[part, column, :, cut] += stiff * summed
            return carry

        lax.fori_loop(0, breadth, along_rows, 0)

        for side in range(2):

            @pl.when(present[side])
            def _():
                halo_copy(step, side, part, True).wait_recv()

        for column in range(breadth):
            stiff = stiff_ref[column] * (-TIME_STEP)
            for lanes in range(2):
                cut = pl.ds(lanes * half, half)
                value = work[part, column, :, cut]
                summed = None
                for offset in range(1, REACH + 1):
                    for side, j in ((0, column - offset + REACH), (1, column + offset - breadth)):
                        inside = (column - offset < 0) if side == 0 else (column + offset >= breadth)
                        if inside:
                            term = SPLINE_TAPS[offset] * col_in[
                                step, part, side, j, :, cut
                            ].astype(jnp.float32)
                            summed = term if summed is None else summed + term
                if summed is not None:
                    value = value + stiff * summed
                speed_now[part, column, :, cut] = value
                field[part, REACH + column, middle, cut] += TIME_STEP * value

    for repeat in range(COUPLED):
        speeds = jnp.zeros((points, half), jnp.float32)
        for part in range(parts):
            outer = speed_now[part, :, :, half:width].reshape(count, half)
            picked = jnp.dot(
                pick[...], outer, precision=HIGHEST, preferred_element_type=jnp.float32
            )
            speeds = speeds + normal_cols[part] * picked
        own_speeds[...] = speeds
        packed_out[repeat] = pack(speeds).astype(packed_out.dtype)

        @pl.loop(1, col_count)
        def _(d):
            speed_copy(repeat, d).start()

        packed_in[repeat, col] = packed_out[repeat]

        if repeat == 0:

            @pl.loop(1, row_count)
            def _(d):
                geo_copy(1, d).wait_recv()

            @pl.loop(1, col_count)
            def _(d):
                geo_copy(0, d).wait_recv()

            @pl.loop(0, row_count)
            def _(r):
                for k in range(3):
                    target_cols[r, k] = as_column(targets[r, k : k + 1, :])

            tile(lax.rem(row + 1, row_count))

        @pl.loop(1, col_count)
        def _(d):
            speed_copy(repeat, d).wait_recv()

        @pl.loop(0, parts)
        def _(part):
            send_halos(repeat * SUBSTEPS, part)

        @pl.loop(0, col_count)
        def _(c):
            value = packed_in[repeat, c].astype(jnp.float32)
            unpacked[c, 0 : points // 2, :] = value.astype(jnp.bfloat16)
            unpacked[c, points // 2 : points, :] = pltpu.roll(value, half // 2, 1).astype(
                jnp.bfloat16
            )

        @pl.loop(1, row_count + 1)
        def _(d):
            r = lax.rem(row + d, row_count)
            total = jnp.zeros((points, half), jnp.float32)
            for c in range(col_count):
                total = total + jnp.dot(
                    tiles[r, c], unpacked[c], preferred_element_type=jnp.float32
                )
            partial_out[repeat, r] = pack(total)

            @pl.when(d < row_count)
            def _():
                part_copy(repeat, d).start()
                if repeat == 0:
                    tile(lax.rem(r + 1, row_count))

        received = partial_out[repeat, row]
        for d in range(1, row_count):
            part_copy(repeat, d).wait_recv()
            received = received + partial_in[repeat, d]
        low_points = jnp.concatenate([low_half, low_half], axis=0)
        both = jnp.concatenate([received, pltpu.roll(received, half // 2, 1)], axis=0)
        pressure = jnp.where(low_points, 0.0, 0.5 * own_speeds[...] + both)
        for part in range(parts):
            loading = jnp.dot(
                spread[...], -(normal_cols[part] * pressure),
                precision=HIGHEST, preferred_element_type=jnp.float32,
            )
            load[part] = loading.reshape(breadth, height, half)

            local(part)

        last = (repeat + 1) * SUBSTEPS - 1

        @pl.loop(repeat * SUBSTEPS, last + 1)
        def _(step):
            @pl.loop(0, parts)
            def _(part):
                complete(step, part)

                @pl.when(step < last)
                def _():
                    send_halos(step + 1, part)
                    local(part)

    for part in range(parts):
        for j in range(breadth):
            for lanes in range(2):
                lines = pl.ds(lanes * breadth + j, height, stride=2 * breadth)
                cut = pl.ds(lanes * half, half)
                u_out[part, lines, :] = field[part, REACH + j, middle, cut]
                v_out[part, lines, :] = speed_now[part, j, :, cut]

    @pl.loop(0, COUPLED * SUBSTEPS)
    def _(step):
        for side in range(4):

            @pl.when(present[side])
            def _():
                for part in range(parts):
                    halo_copy(step, side, part, False).wait_send()

    @pl.loop(1, col_count)
    def _(d):
        geo_copy(0, d).wait_send()
        for repeat in range(COUPLED):
            speed_copy(repeat, d).wait_send()

    @pl.loop(1, row_count)
    def _(d):
        geo_copy(1, d).wait_send()
        for repeat in range(COUPLED):
            part_copy(repeat, d).wait_send()


def on_device(shape, displacement, velocity, stiffness, wet_position, wet_normal, wet_area, wet_map):
    col_count, row_count, _ = shape
    parts, height, breadth, width = displacement.shape
    half = width // 2
    points = wet_map.shape[0]
    steps = COUPLED * SUBSTEPS
    stiff = jnp.broadcast_to(stiffness.T[:, :, None], (breadth, height, half))
    node = (wet_map % breadth) * height + wet_map // breadth

    def split(state):
        tiled = state.reshape(parts, height, breadth, 2, half).transpose(0, 1, 3, 2, 4)
        return tiled.reshape(parts, height * 2 * breadth, half)

    def joined(state):
        tiled = state.reshape(parts, height, 2, breadth, half).transpose(0, 1, 3, 2, 4)
        return tiled.reshape(parts, height, breadth, width)

    state = jax.ShapeDtypeStruct((parts, height * 2 * breadth, half), jnp.float32)
    cols = (steps, parts, 2, REACH, height, width)
    rows = (steps, parts, 2, breadth // 2, 8, width)
    f32, bf16 = jnp.float32, jnp.bfloat16
    dma = pltpu.SemaphoreType.DMA
    u_new, v_new = pl.pallas_call(
        functools.partial(coupled_kernel, shape),
        out_shape=(state, state),
        in_specs=[whole_spec()] * 7,
        out_specs=(whole_spec(), whole_spec()),
        scratch_shapes=[
            VMEM((parts, breadth + 2 * REACH, height + 2 * PAD, width), f32),
            VMEM((parts, breadth, height, width), f32),
            VMEM((parts, breadth, height, width), f32),
            VMEM((parts, breadth, height, half), f32),
            VMEM(cols, bf16),
            VMEM(cols, bf16),
            VMEM(rows, f32),
            VMEM(rows, f32),
            VMEM((8, points), f32),
            VMEM((col_count, 8, points), f32),
            VMEM((row_count, 8, points), f32),
            VMEM((row_count, 3, points, half), f32),
            VMEM((parts, points, half), f32),
            VMEM((points, height * breadth), f32),
            VMEM((height * breadth, points), f32),
            VMEM((points, half), f32),
            VMEM((COUPLED, points // 2, half), bf16),
            VMEM((COUPLED, col_count, points // 2, half), bf16),
            VMEM((col_count, points, half), bf16),
            VMEM((row_count, col_count, points, points), bf16),
            VMEM((COUPLED, row_count, points // 2, half), f32),
            VMEM((COUPLED, row_count, points // 2, half), f32),
            dma((steps, parts, 4)),
            dma((steps, parts, 4)),
            dma((2, max(col_count, row_count))),
            dma((2, max(col_count, row_count))),
            dma((COUPLED, col_count)),
            dma((COUPLED, col_count)),
            dma((COUPLED, row_count)),
            dma((COUPLED, row_count)),
            VMEM((1, col_count * row_count, 16, 128), jnp.int16),
            VMEM((1, col_count * row_count, 16, 128), jnp.int16),
            dma((1, col_count * row_count)),
            dma((1, col_count * row_count)),
        ],
        compiler_params=pltpu.CompilerParams(
            collective_id=0, has_side_effects=True, vmem_limit_bytes=67043328
        ),
        name="coupled_steps",
    )(
        split(displacement), split(velocity), stiff,
        wet_position, wet_normal, wet_area[None, :], node[None, :],
    )
    return (joined(u_new), joined(v_new))


def solution(mesh):
    sizes = mesh.shape
    shape = (sizes["tcol"], sizes["group"] * sizes["trow"], sizes["trow"])
    state = P(None, ("group", "trow"), "tcol", None)
    wet = ("group", "trow", "tcol")
    return jax.shard_map(
        functools.partial(on_device, shape),
        mesh=mesh,
        in_specs=(
            state,
            state,
            P(("group", "trow"), "tcol"),
            P(None, wet),
            P(None, wet),
            P(wet),
            P(wet),
        ),
        out_specs=(state, state),
        check_vma=False,
    )
```

```python
import functools
import math

import jax
import jax.numpy as jnp
from jax import lax
from jax.experimental import pallas as pl
from jax.experimental.pallas import tpu as pltpu
from jax.sharding import PartitionSpec as P

LOADS = 64
SUBSTEPS = 4
COUPLED = 2

SPHERE_AREA = 4.0 * math.pi
SMOOTHING = 0.1
TIME_STEP = 0.3
THICKNESS = 0.5
SPLINE_TAPS = (2.0 / 3.0, -1.0 / 12.0, -1.0 / 12.0, -1.0 / 6.0)
REACH = 3
PAD = 8
MESH = pl.DeviceIdType.MESH
VMEM = pltpu.VMEM


def row_device(index, trow_count):
    return {"group": index // trow_count, "trow": lax.rem(index, trow_count)}


def whole_spec():
    return pl.BlockSpec(memory_space=pltpu.VMEM)


HIGHEST = lax.Precision.HIGHEST


def coupled_kernel(
    shape, u_in, v_in, stiff_ref, position_ref, normal_ref, area_ref, node_ref, u_out, v_out,
    field, speed_now, work, load, col_out, col_in, row_out, row_in,
    geometry, sources, targets, target_cols, normal_cols, pick, spread,
    own_speeds, packed_out, packed_in, unpacked, tiles, partial_out, partial_in,
    halo_send, halo_recv, geo_send, geo_recv, speed_send, speed_recv, part_send, part_recv
):
    col_count, row_count, trow_count = shape
    parts, breadth, height, width = speed_now.shape
    half = width // 2
    points = geometry.shape[1]
    count = breadth * height
    col = lax.axis_index("tcol")
    row = lax.axis_index("group") * trow_count + lax.axis_index("trow")
    present = (col > 0, col < col_count - 1, row > 0, row < row_count - 1)
    peers = (
        {"tcol": jnp.maximum(col - 1, 0)},
        {"tcol": jnp.minimum(col + 1, col_count - 1)},
        row_device(jnp.maximum(row - 1, 0), trow_count),
        row_device(jnp.minimum(row + 1, row_count - 1), trow_count),
    )
    middle = pl.ds(PAD, height)

    def col_peer(d):
        return {"tcol": lax.rem(col + d, col_count)}

    def row_peer(d):
        return row_device(lax.rem(row + d, row_count), trow_count)

    barrier = pltpu.get_barrier_semaphore()

    @pl.loop(1, col_count)
    def _(d):
        pl.semaphore_signal(barrier, inc=1, device_id=col_peer(d), device_id_type=MESH)

    @pl.loop(1, row_count)
    def _(d):
        pl.semaphore_signal(barrier, inc=1, device_id=row_peer(d), device_id_type=MESH)

    geometry[0:3, :] = position_ref[...]
    geometry[3:6, :] = normal_ref[...] * (area_ref[...] * (1.0 / SPHERE_AREA))
    geometry[6:8, :] = jnp.zeros((2, points), jnp.float32)
    pl.semaphore_wait(barrier, col_count + row_count - 2)

    def geo_copy(kind, d):
        return pltpu.make_async_remote_copy(
            src_ref=geometry,
            dst_ref=sources.at[col] if kind == 0 else targets.at[row],
            send_sem=geo_send.at[kind, d],
            recv_sem=geo_recv.at[kind, d],
            device_id=col_peer(d) if kind == 0 else row_peer(d),
            device_id_type=MESH,
        )

    def speed_copy(repeat, d):
        return pltpu.make_async_remote_copy(
            src_ref=packed_out.at[repeat],
            dst_ref=packed_in.at[repeat, col],
            send_sem=speed_send.at[repeat, d],
            recv_sem=speed_recv.at[repeat, d],
            device_id=col_peer(d),
            device_id_type=MESH,
        )

    def part_copy(repeat, d):
        return pltpu.make_async_remote_copy(
            src_ref=partial_out.at[repeat, lax.rem(row + d, row_count)],
            dst_ref=partial_in.at[repeat, d],
            send_sem=part_send.at[repeat, d],
            recv_sem=part_recv.at[repeat, d],
            device_id=row_peer(d),
            device_id_type=MESH,
        )

    for kind, total in ((1, row_count), (0, col_count)):

        @pl.loop(1, total)
        def _(d):
            geo_copy(kind, d).start()

    sources[col] = geometry[...]
    targets[row] = geometry[...]

    field[...] = jnp.zeros_like(field)
    for part in range(parts):
        for j in range(breadth):
            for lanes in range(2):
                lines = pl.ds(lanes * breadth + j, height, stride=2 * breadth)
                cut = pl.ds(lanes * half, half)
                field[part, REACH + j, middle, cut] = u_in[part, lines, :]
                speed_now[part, j, :, cut] = v_in[part, lines, :]
    for side in range(2):

        @pl.when(jnp.logical_not(present[side]))
        def _():
            col_in[:, :, side] = jnp.zeros(col_in.shape[:2] + col_in.shape[3:], col_in.dtype)

    def as_column(line):
        return jnp.broadcast_to(line, (half, line.shape[1])).T

    for part in range(parts):
        normal_cols[part] = as_column(normal_ref[part : part + 1, :])
    spread[...] = (
        lax.broadcasted_iota(jnp.int32, (count, points), 0) == node_ref[...]
    ).astype(jnp.float32)
    pick[...] = spread[...].T

    def halo_copy(step, side, part, arriving):
        out_buffer, in_buffer = (col_out, col_in) if side < 2 else (row_out, row_in)
        own = side % 2
        other = own if arriving else 1 - own
        return pltpu.make_async_remote_copy(
            src_ref=out_buffer.at[step, part, own],
            dst_ref=in_buffer.at[step, part, other],
            send_sem=halo_send.at[step, part, side],
            recv_sem=halo_recv.at[step, part, (side // 2) * 2 + other],
            device_id=peers[side],
            device_id_type=MESH,
        )

    lane = lax.broadcasted_iota(jnp.int32, (height, half), 1)
    low = lane < half // 2
    low_half = lax.broadcasted_iota(jnp.int32, (points // 2, half), 1) < half // 2

    def pack(value):
        turned = pltpu.roll(value[points // 2 :], half // 2, 1)
        return jnp.where(low_half, turned, value[: points // 2])

    def tile(r):
        group = 32

        def block(index, carry):
            source = index // (points // half)
            lanes = pl.ds(pl.multiple_of(lax.rem(index, points // half) * half, half), half)
            line = [sources[source, k : k + 1, lanes] for k in range(6)]

            def rows_of(g, inner):
                rows = pl.ds(pl.multiple_of(g * group, group), group)
                dx = target_cols[r, 0, rows, :] - line[0]
                dy = target_cols[r, 1, rows, :] - line[1]
                dz = target_cols[r, 2, rows, :] - line[2]
                numerator = line[3] * dx + line[4] * dy + line[5] * dz
                squared = dx * dx + dy * dy + dz * dz + SMOOTHING * SMOOTHING
                inverse = lax.rsqrt(squared)
                value = numerator * inverse * (inverse * inverse)
                tiles[r, source, rows, lanes] = value.astype(jnp.bfloat16)
                return inner

            return lax.fori_loop(0, points // group, rows_of, carry, unroll=2)

        lax.fori_loop(0, col_count * (points // half), block, 0)

    def send_halos(step, part):
        for side, first in ((0, REACH), (1, breadth)):

            @pl.when(present[side])
            def _():
                for j in range(REACH):
                    col_out[step, part, side, j] = field[part, first + j, middle, :].astype(
                        col_out.dtype
                    )
                halo_copy(step, side, part, False).start()

        for side, first in ((2, PAD), (3, PAD + height - REACH)):

            @pl.when(present[side])
            def _():
                for j in range(breadth):
                    row_out[
                        step, part, side - 2, j // 2, (j % 2) * 4 : (j % 2) * 4 + REACH, :
                    ] = field[part, REACH + j, first : first + REACH, :]
                halo_copy(step, side, part, False).start()

    def local(part):
        def body(column, carry):
            a = field[part, REACH + column, middle, 0:half]
            b = field[part, REACH + column, middle, half:width]
            turned_a = pltpu.roll(a, half // 2, 1)
            turned_b = pltpu.roll(b, half // 2, 1)
            between = jnp.where(low, turned_a, turned_b)
            edge_a = jnp.where(low, a, turned_a)
            edge_b = jnp.where(low, turned_b, b)
            stiff = stiff_ref[column]
            for lanes, here, edge in ((0, a, edge_a), (1, b, edge_b)):
                cut = pl.ds(lanes * half, half)
                summed = (2.0 * SPLINE_TAPS[0]) * here
                for offset in range(1, REACH + 1):
                    summed = summed + SPLINE_TAPS[offset] * (
                        field[part, REACH + column + offset, middle, cut]
                        + field[part, REACH + column - offset, middle, cut]
                    )
                value = -(stiff * summed) - THICKNESS * (2.0 * here - between - edge)
                if lanes == 1:
                    value = value + load[part, column]
                work[part, column, :, cut] = speed_now[part, column, :, cut] + TIME_STEP * value
            return carry

        lax.fori_loop(0, breadth, body, 0)

    def complete(step, part):
        for side, first in ((2, PAD - REACH), (3, PAD + height)):

            @pl.when(present[side])
            def _():
                halo_copy(step, side, part, True).wait_recv()
                for j in range(breadth):
                    field[part, REACH + j, first : first + REACH, :] = row_in[
                        step, part, side - 2, j // 2, (j % 2) * 4 : (j % 2) * 4 + REACH, :
                    ]

        def along_rows(column, carry):
            stiff = stiff_ref[column] * (-TIME_STEP)
            for lanes in range(2):
                cut = pl.ds(lanes * half, half)
                summed = 0.0
                for offset in range(1, REACH + 1):
                    summed = summed + SPLINE_TAPS[offset] * (
                        field[part, REACH + column, pl.ds(PAD + offset, height), cut]
                        + field[part, REACH + column, pl.ds(PAD - offset, height), cut]
                    )
                work[part, column, :, cut] += stiff * summed
            return carry

        lax.fori_loop(0, breadth, along_rows, 0)

        for side in range(2):

            @pl.when(present[side])
            def _():
                halo_copy(step, side, part, True).wait_recv()

        for column in range(breadth):
            stiff = stiff_ref[column] * (-TIME_STEP)
            for lanes in range(2):
                cut = pl.ds(lanes * half, half)
                value = work[part, column, :, cut]
                summed = None
                for offset in range(1, REACH + 1):
                    for side, j in ((0, column - offset + REACH), (1, column + offset - breadth)):
                        inside = (column - offset < 0) if side == 0 else (column + offset >= breadth)
                        if inside:
                            term = SPLINE_TAPS[offset] * col_in[
                                step, part, side, j, :, cut
                            ].astype(jnp.float32)
                            summed = term if summed is None else summed + term
                if summed is not None:
                    value = value + stiff * summed
                speed_now[part, column, :, cut] = value
                field[part, REACH + column, middle, cut] += TIME_STEP * value

    for repeat in range(COUPLED):
        speeds = jnp.zeros((points, half), jnp.float32)
        for part in range(parts):
            outer = speed_now[part, :, :, half:width].reshape(count, half)
            picked = jnp.dot(
                pick[...], outer, precision=HIGHEST, preferred_element_type=jnp.float32
            )
            speeds = speeds + normal_cols[part] * picked
        own_speeds[...] = speeds
        packed_out[repeat] = pack(speeds).astype(packed_out.dtype)

        @pl.loop(1, col_count)
        def _(d):
            speed_copy(repeat, d).start()

        packed_in[repeat, col] = packed_out[repeat]

        if repeat == 0:

            @pl.loop(1, row_count)
            def _(d):
                geo_copy(1, d).wait_recv()

            @pl.loop(1, col_count)
            def _(d):
                geo_copy(0, d).wait_recv()

            @pl.loop(0, row_count)
            def _(r):
                for k in range(3):
                    target_cols[r, k] = as_column(targets[r, k : k + 1, :])

            tile(lax.rem(row + 1, row_count))

        @pl.loop(1, col_count)
        def _(d):
            speed_copy(repeat, d).wait_recv()

        @pl.loop(0, parts)
        def _(part):
            send_halos(repeat * SUBSTEPS, part)

        @pl.loop(0, col_count)
        def _(c):
            value = packed_in[repeat, c].astype(jnp.float32)
            unpacked[c, 0 : points // 2, :] = value.astype(jnp.bfloat16)
            unpacked[c, points // 2 : points, :] = pltpu.roll(value, half // 2, 1).astype(
                jnp.bfloat16
            )

        @pl.loop(1, row_count + 1)
        def _(d):
            r = lax.rem(row + d, row_count)
            total = jnp.zeros((points, half), jnp.float32)
            for c in range(col_count):
                total = total + jnp.dot(
                    tiles[r, c], unpacked[c], preferred_element_type=jnp.float32
                )
            partial_out[repeat, r] = pack(total)

            @pl.when(d < row_count)
            def _():
                part_copy(repeat, d).start()
                if repeat == 0:
                    tile(lax.rem(r + 1, row_count))

        received = partial_out[repeat, row]
        for d in range(1, row_count):
            part_copy(repeat, d).wait_recv()
            received = received + partial_in[repeat, d]
        low_points = jnp.concatenate([low_half, low_half], axis=0)
        both = jnp.concatenate([received, pltpu.roll(received, half // 2, 1)], axis=0)
        pressure = jnp.where(low_points, 0.0, 0.5 * own_speeds[...] + both)
        for part in range(parts):
            loading = jnp.dot(
                spread[...], -(normal_cols[part] * pressure),
                precision=HIGHEST, preferred_element_type=jnp.float32,
            )
            load[part] = loading.reshape(breadth, height, half)

            local(part)

        last = (repeat + 1) * SUBSTEPS - 1

        @pl.loop(repeat * SUBSTEPS, last + 1)
        def _(step):
            @pl.loop(0, parts)
            def _(part):
                complete(step, part)

                @pl.when(step < last)
                def _():
                    send_halos(step + 1, part)
                    local(part)

    for part in range(parts):
        for j in range(breadth):
            for lanes in range(2):
                lines = pl.ds(lanes * breadth + j, height, stride=2 * breadth)
                cut = pl.ds(lanes * half, half)
                u_out[part, lines, :] = field[part, REACH + j, middle, cut]
                v_out[part, lines, :] = speed_now[part, j, :, cut]

    @pl.loop(0, COUPLED * SUBSTEPS)
    def _(step):
        for side in range(4):

            @pl.when(present[side])
            def _():
                for part in range(parts):
                    halo_copy(step, side, part, False).wait_send()

    @pl.loop(1, col_count)
    def _(d):
        geo_copy(0, d).wait_send()
        for repeat in range(COUPLED):
            speed_copy(repeat, d).wait_send()

    @pl.loop(1, row_count)
    def _(d):
        geo_copy(1, d).wait_send()
        for repeat in range(COUPLED):
            part_copy(repeat, d).wait_send()


def on_device(shape, displacement, velocity, stiffness, wet_position, wet_normal, wet_area, wet_map):
    col_count, row_count, _ = shape
    parts, height, breadth, width = displacement.shape
    half = width // 2
    points = wet_map.shape[0]
    steps = COUPLED * SUBSTEPS
    stiff = jnp.broadcast_to(stiffness.T[:, :, None], (breadth, height, half))
    node = (wet_map % breadth) * height + wet_map // breadth

    def split(state):
        tiled = state.reshape(parts, height, breadth, 2, half).transpose(0, 1, 3, 2, 4)
        return tiled.reshape(parts, height * 2 * breadth, half)

    def joined(state):
        tiled = state.reshape(parts, height, 2, breadth, half).transpose(0, 1, 3, 2, 4)
        return tiled.reshape(parts, height, breadth, width)

    state = jax.ShapeDtypeStruct((parts, height * 2 * breadth, half), jnp.float32)
    cols = (steps, parts, 2, REACH, height, width)
    rows = (steps, parts, 2, breadth // 2, 8, width)
    f32, bf16 = jnp.float32, jnp.bfloat16
    dma = pltpu.SemaphoreType.DMA
    u_new, v_new = pl.pallas_call(
        functools.partial(coupled_kernel, shape),
        out_shape=(state, state),
        in_specs=[whole_spec()] * 7,
        out_specs=(whole_spec(), whole_spec()),
        scratch_shapes=[
            VMEM((parts, breadth + 2 * REACH, height + 2 * PAD, width), f32),
            VMEM((parts, breadth, height, width), f32),
            VMEM((parts, breadth, height, width), f32),
            VMEM((parts, breadth, height, half), f32),
            VMEM(cols, bf16),
            VMEM(cols, bf16),
            VMEM(rows, f32),
            VMEM(rows, f32),
            VMEM((8, points), f32),
            VMEM((col_count, 8, points), f32),
            VMEM((row_count, 8, points), f32),
            VMEM((row_count, 3, points, half), f32),
            VMEM((parts, points, half), f32),
            VMEM((points, height * breadth), f32),
            VMEM((height * breadth, points), f32),
            VMEM((points, half), f32),
            VMEM((COUPLED, points // 2, half), bf16),
            VMEM((COUPLED, col_count, points // 2, half), bf16),
            VMEM((col_count, points, half), bf16),
            VMEM((row_count, col_count, points, points), bf16),
            VMEM((COUPLED, row_count, points // 2, half), f32),
            VMEM((COUPLED, row_count, points // 2, half), f32),
            dma((steps, parts, 4)),
            dma((steps, parts, 4)),
            dma((2, max(col_count, row_count))),
            dma((2, max(col_count, row_count))),
            dma((COUPLED, col_count)),
            dma((COUPLED, col_count)),
            dma((COUPLED, row_count)),
            dma((COUPLED, row_count)),
        ],
        compiler_params=pltpu.CompilerParams(
            collective_id=0, has_side_effects=True, vmem_limit_bytes=67043328
        ),
        name="coupled_steps",
    )(
        split(displacement), split(velocity), stiff,
        wet_position, wet_normal, wet_area[None, :], node[None, :],
    )
    return (joined(u_new), joined(v_new))


PAIR = 2
LEVELS = 32767.0


def plane_kernel(
    shape, u_hbm, v_hbm, stiff_ref, position_ref, normal_ref, area_ref, map_ref, u_out, v_out,
    u_raw, v_raw, perm, turn, eye, stencil, edges, in_out, in_in, facts_out, facts, places, targets,
    source_cols, first_out, first_in, tiles, part_out, part_in, spoken,
    onehot, onehot_back, u_now, v_now, load, halves, summed, beside, stiff_now, own_speed,
    halo_out, halo_in, speed_out, speed_in, final_out, final_in, scale_out, scale_in,
    load_sem, facts_send, facts_recv, places_send, places_recv, first_send, first_recv,
    in_send, in_recv, part_send, part_recv, halo_send, halo_recv, speed_send, speed_recv,
    final_send, final_recv, scale_send, scale_recv,
):
    col_count, row_count, trow_count = shape
    depth_count = col_count // PAIR
    members = row_count * PAIR
    total = members * depth_count
    parts, _, half = u_raw.shape
    count, points = onehot.shape[1:]
    breadth, height = stiff_ref.shape
    width = perm.shape[1]
    own = LOADS // members
    layers = width // LOADS
    block = own * layers
    last_step = COUPLED * SUBSTEPS - 1
    f32, bf16, i16, i32 = jnp.float32, jnp.bfloat16, jnp.int16, jnp.int32
    col = lax.axis_index("tcol")
    row = lax.axis_index("group") * trow_count + lax.axis_index("trow")
    z = col // PAIR
    me = row * PAIR + lax.rem(col, PAIR)

    def device(depth, member):
        return dict(
            row_device(member // PAIR, trow_count), tcol=depth * PAIR + lax.rem(member, PAIR)
        )

    def member_of(d):
        return lax.rem(me + d, members)

    def depth_of(d):
        return lax.rem(z + d, depth_count)

    def each(first, last, action):
        @pl.loop(first, last)
        def _(d):
            action(d)

    barrier = pltpu.get_barrier_semaphore()

    @pl.loop(1, total)
    def _(d):
        to = device(depth_of(d // members), member_of(lax.rem(d, members)))
        pl.semaphore_signal(barrier, inc=1, device_id=to, device_id_type=MESH)

    v_load = pltpu.make_async_copy(v_hbm, v_raw, load_sem.at[0])
    u_load = pltpu.make_async_copy(u_hbm, u_raw, load_sem.at[1])
    v_load.start()
    u_load.start()

    def iota(size, axis):
        return lax.broadcasted_iota(i32, size, axis)

    def ones_where(mask):
        return jnp.where(mask, 1.0, 0.0).astype(bf16)

    def dot(a, b):
        return jnp.dot(a, b, preferred_element_type=f32)

    def dot_turned(a, b):
        return lax.dot_general(a, b, (((1,), (1,)), ((), ())), preferred_element_type=f32)

    def lane_of(line):
        member, inner = line // block, line % block
        return (inner // own) * LOADS + member * own + inner % own

    square = (width, width)
    line, column = iota(square, 0), iota(square, 1)
    perm[0:width, :] = ones_where(lane_of(line) == column)
    turn[...] = ones_where(lane_of(column) == line)
    outer = (LOADS, width)
    perm[width : width + LOADS, :] = ones_where(
        (layers - 1) * LOADS + iota(outer, 0) == iota(outer, 1)
    )
    eye[...] = ones_where(iota((count, count), 0) == iota((count, count), 1))

    src, dst = iota((count, count), 0), iota((count, count), 1)
    src_a, src_b, dst_a, dst_b = src % height, src // height, dst % height, dst // height

    def taps(distance, mask):
        value = jnp.where(distance == 3, -2.0, jnp.where((distance == 1) | (distance == 2), -1.0, 0.0))
        return jnp.where(mask, value, 0.0)

    same_a, same_b = src_a == dst_a, src_b == dst_b
    stencil[0:count, :] = (
        jnp.where(src == dst, 16.0, 0.0)
        + taps(jnp.abs(src_b - dst_b), same_a)
        + taps(jnp.abs(src_a - dst_a), same_b)
    ).astype(bf16)
    stencil[count : 2 * count, :] = (
        taps(dst_a + height - src_a, same_b) + taps(src_a + height - dst_a, same_b)
    ).astype(bf16)
    stencil[2 * count : 3 * count, :] = (
        taps(dst_b + breadth - src_b, same_a) + taps(src_b + breadth - dst_b, same_a)
    ).astype(bf16)
    node_a = iota((16, count), 1) % height
    edges[0] = ones_where(node_a >= height - REACH)
    edges[1] = ones_where(node_a < REACH)

    spread = ones_where(iota((height, count), 0) == iota((height, count), 1) % height).astype(f32)
    wide = jnp.dot(stiff_ref[...], spread, precision=HIGHEST, preferred_element_type=f32)
    own_b = iota((breadth, count), 0) == iota((breadth, count), 1) // height
    places[0:3, :] = position_ref[...]
    places[3:8, :] = jnp.zeros((5, points), f32)
    facts_out[0:3, :] = position_ref[...]
    facts_out[3:6, :] = normal_ref[...] * (area_ref[...] * (1.0 / SPHERE_AREA))
    facts_out[6:9, :] = normal_ref[...]
    numbers = map_ref[...]
    facts_out[9:10, :] = ((numbers % breadth) * height + numbers // breadth).astype(f32)
    facts_out[10:11, :] = jnp.sum(jnp.where(own_b, wide, 0.0), axis=0, keepdims=True)
    facts_out[13:16, :] = jnp.zeros((3, points), f32)
    targets[z] = places[...]

    halves[:, :, 0] = jnp.zeros((2, parts) + halves.shape[3:], bf16)
    halves[:, :, row_count + 1] = jnp.zeros((2, parts) + halves.shape[3:], bf16)
    beyond = halo_in.shape[:3] + (row_count, block, half)
    halo_in[:, :, :, :, block : 2 * block, :] = jnp.zeros(beyond, bf16)
    present = (z > 0, z < depth_count - 1)
    for side in range(2):

        @pl.when(jnp.logical_not(present[side]))
        def _():
            halo_in[:, :, side, :, 0:block, :] = jnp.zeros(beyond[:2] + beyond[3:], bf16)

    def plane_copy(d, source, target, send, recv):
        return pltpu.make_async_remote_copy(
            src_ref=source, dst_ref=target.at[me], send_sem=send.at[d], recv_sem=recv.at[d],
            device_id=device(z, member_of(d)), device_id_type=MESH,
        )

    def facts_copy(d):
        return plane_copy(d, facts_out, facts, facts_send, facts_recv)

    def places_copy(d):
        return pltpu.make_async_remote_copy(
            src_ref=places, dst_ref=targets.at[z],
            send_sem=places_send.at[d], recv_sem=places_recv.at[d],
            device_id=device(depth_of(d), me), device_id_type=MESH,
        )

    def first_copy(d):
        return plane_copy(d, first_out, first_in, first_send, first_recv)

    def in_copy(d):
        return plane_copy(d, in_out.at[member_of(d)], in_in, in_send, in_recv)

    def speed_copy(d):
        return plane_copy(d, speed_out, speed_in, speed_send, speed_recv)

    def final_copy(part, d):
        return plane_copy(
            d, final_out.at[part, member_of(d)], final_in.at[part],
            final_send.at[part], final_recv.at[part],
        )

    def scale_copy(part, d):
        return plane_copy(
            d, scale_out.at[part], scale_in.at[part], scale_send.at[part], scale_recv.at[part]
        )

    def part_copy(repeat, dz, dj):
        lines = pl.ds(pl.multiple_of(member_of(dj) * own, own), own)
        return pltpu.make_async_remote_copy(
            src_ref=part_out.at[repeat, depth_of(dz), lines, :],
            dst_ref=part_in.at[repeat, z, me],
            send_sem=part_send.at[repeat, dz, dj], recv_sem=part_recv.at[repeat, dz, dj],
            device_id=device(depth_of(dz), member_of(dj)), device_id_type=MESH,
        )

    def halo_copy(step, part, side, arriving):
        there = side if arriving else 1 - side
        step_z = jnp.maximum(z - 1, 0) if side == 0 else jnp.minimum(z + 1, depth_count - 1)
        return pltpu.make_async_remote_copy(
            src_ref=halo_out.at[step, part, side],
            dst_ref=halo_in.at[step, part, there, :, 0:block, :],
            send_sem=halo_send.at[step, part, side], recv_sem=halo_recv.at[step, part, there],
            device_id=device(step_z, me), device_id_type=MESH,
        )

    def as_column(value):
        return jnp.broadcast_to(value, (half, value.shape[1])).T

    def one_hot(s):
        onehot[s] = ones_where(iota((count, points), 0).astype(f32) == facts[s, 9:10, :])

    def one_hot_back(s):
        nodes = as_column(facts[s, 9:10, :])
        for lanes in range(2):
            numbers = (iota((points, half), 1) + lanes * half).astype(f32)
            onehot_back[s, :, lanes * half : (lanes + 1) * half] = ones_where(numbers == nodes)

    facts[me] = facts_out[...]
    one_hot(me)

    def largest(value):
        reduced = jnp.max(jnp.abs(value), axis=0)
        top = jnp.max(jnp.max(reduced, axis=1, keepdims=True), axis=0, keepdims=True)
        return jnp.maximum(top, 1e-30)

    def split(value):
        high = value.astype(bf16).astype(f32)
        return jnp.concatenate([high, value - high], axis=-2).astype(bf16)

    def turned(raw, part, inverse, lines):
        rows = []
        for j in range(breadth):
            picks = [
                raw[part, pl.ds(lanes * breadth + j, height, stride=2 * breadth), :]
                for lanes in range(2)
            ]
            rows.append(jnp.concatenate(picks, axis=1))
        value = jnp.round(jnp.concatenate(rows, axis=0) * inverse)
        high = jnp.round(value * (1.0 / 256.0))
        low = value - 256.0 * high
        return (
            dot_turned(perm[0:lines, :], high.astype(bf16)),
            dot_turned(perm[0:lines, :], low.astype(bf16)),
        )

    def top_of(raw):
        return largest(raw[...].reshape(raw.shape[0] * raw.shape[1] // 8, 8, half))

    v_load.wait()
    v_top = top_of(v_raw)
    v_scale, v_inverse = v_top * (1.0 / LEVELS), LEVELS / v_top
    facts_out[12:13, :] = jnp.broadcast_to(v_scale, (1, points))
    picked_all = jnp.zeros((LOADS, points), f32)
    for part in range(parts):
        high, low = turned(v_raw, part, v_inverse, width + LOADS)
        whole = high[0:width] * 256.0 + low[0:width]
        in_out[:, part, block : 2 * block, :] = (
            whole.reshape(members, block, count).astype(i32).astype(i16)
        )
        rows = jnp.concatenate([high[width:], low[width:]], axis=0).astype(bf16)
        both = dot(rows, onehot[me])
        picked = both[0:LOADS] * 256.0 + both[LOADS:]
        picked_all = picked_all + picked * (normal_ref[part : part + 1, :] * v_scale)
    own_speed[...] = picked_all
    first_out[...] = picked_all.astype(bf16)
    first_in[me] = first_out[...]

    u_load.wait()
    u_top = top_of(u_raw)
    u_scale, u_inverse = u_top * (1.0 / LEVELS), LEVELS / u_top
    facts_out[11:12, :] = jnp.broadcast_to(u_scale, (1, points))
    facts[me] = facts_out[...]
    for part in range(parts):
        high, low = turned(u_raw, part, u_inverse, width)
        whole = high * 256.0 + low
        in_out[:, part, 0:block, :] = whole.reshape(members, block, count).astype(i32).astype(i16)
    in_in[me] = in_out[me]

    pl.semaphore_wait(barrier, total - 1)
    each(1, members, lambda d: facts_copy(d).start())
    each(1, depth_count, lambda d: places_copy(d).start())
    each(1, members, lambda d: first_copy(d).start())
    each(1, members, lambda d: in_copy(d).start())

    each(1, members, lambda d: facts_copy(d).wait_recv())

    @pl.loop(0, members)
    def _(s):
        for k in range(6):
            source_cols[s, k] = as_column(facts[s, k : k + 1, :])

    group = 32

    def tile(depth):
        def blocks(index, carry):
            source = index // (points // half)
            lanes = pl.ds(pl.multiple_of(lax.rem(index, points // half) * half, half), half)
            known = [targets[depth, k : k + 1, lanes] for k in range(3)]

            def rows_of(g, inner):
                start = pl.multiple_of(g * group, group)
                rows = pl.ds(start, group)
                dx = known[0] - source_cols[source, 0, rows, :]
                dy = known[1] - source_cols[source, 1, rows, :]
                dz = known[2] - source_cols[source, 2, rows, :]
                numerator = (
                    source_cols[source, 3, rows, :] * dx
                    + source_cols[source, 4, rows, :] * dy
                    + source_cols[source, 5, rows, :] * dz
                )
                squared = dx * dx + dy * dy + dz * dz + SMOOTHING * SMOOTHING
                inverse = lax.rsqrt(squared)
                value = numerator * inverse * (inverse * inverse)
                deep = pl.ds(pl.multiple_of(source * points + start, group), group)
                tiles[depth, deep, lanes] = value.astype(bf16)
                return inner

            return lax.fori_loop(0, points // group, rows_of, carry, unroll=2)

        lax.fori_loop(0, members * (points // half), blocks, 0)

    def send_pressures(repeat, speeds):
        @pl.loop(1, depth_count + 1)
        def _(d):
            depth = depth_of(d)
            if repeat == 0:

                @pl.when(d < depth_count)
                def _():
                    places_copy(depth_count - d).wait_recv()

                tile(depth)

                @pl.when(d == 1)
                def _():
                    each(1, members, lambda d: first_copy(d).wait_recv())

            value = dot(speeds(), tiles[depth])
            if repeat == 0:
                value = value + jnp.where(depth == z, 0.5, 0.0) * own_speed[...]
            part_out[repeat, depth] = value

            @pl.when(d < depth_count)
            def _():
                each(0, members, lambda dj: part_copy(repeat, d, dj).start())

            @pl.when(d == depth_count)
            def _():
                each(1, members, lambda dj: part_copy(repeat, 0, dj).start())

        part_in[repeat, z, me] = part_out[
            repeat, z, pl.ds(pl.multiple_of(me * own, own), own), :
        ]

    def parts_taken(repeat, action):
        each(1, members, lambda dj: action(part_copy(repeat, 0, dj)))

        @pl.loop(1, depth_count)
        def _(d):
            each(0, members, lambda dj: action(part_copy(repeat, d, dj)))

    def interior(part, now):
        def view(dr):
            return halves[now, part, pl.ds(1 + dr, row_count)]

        def rows16(value):
            return value.reshape(members * 2 * block // 16, 16, count)

        down = rows16(view(-1)) * edges[0] + rows16(view(1)) * edges[1]
        flat = (members * 2 * block, count)
        lines = jnp.concatenate([view(0).reshape(flat), down.reshape(flat)], axis=1)
        summed[part] = dot(lines, stencil[0 : 2 * count, :])

    def send_halos(step, part):
        for side in range(2):

            @pl.when(present[side])
            def _():
                halo_copy(step, part, side, False).start()

    def place_halo(step, part, r, x, value):
        lanes = x * half
        halo_out[step, part, x, r] = value[:, lanes : lanes + half].astype(bf16)

    send_pressures(
        0, lambda: jnp.concatenate([first_in[s] for s in range(members)], axis=1)
    )

    @pl.loop(0, members, unroll=2)
    def _(s):
        one_hot(s)
        one_hot_back(s)
        stiff_now[s] = jnp.broadcast_to(facts[s, 10:11, :] * (-TIME_STEP / 12.0), (8, count))

    each(1, members, lambda d: in_copy(d).wait_recv())

    @pl.loop(0, parts)
    def _(part):
        @pl.loop(0, row_count)
        def _(r):
            for x in range(PAIR):
                s = r * PAIR + x
                value = in_in[s, part].astype(i32).astype(f32)
                u_new = value[0:block] * facts[s, 11:12, :]
                u_now[part, s] = u_new
                v_now[part, s] = value[block : 2 * block] * facts[s, 12:13, :]
                halves[0, part, 1 + r, x] = split(u_new)
                place_halo(0, part, r, x, u_new)

        send_halos(0, part)
        interior(part, 0)

    def take_pressures(repeat):
        parts_taken(repeat, lambda copy: copy.wait_recv())

        @pl.loop(0, members, unroll=4)
        def _(s):
            value = part_in[repeat, 0, s]
            for d in range(1, depth_count):
                value = value + part_in[repeat, d, s]
            if repeat > 0:
                value = value + 0.5 * spoken[s]
            pieces = [
                split(value * (facts[s, 6 + k : 7 + k, :] * (-TIME_STEP))) for k in range(parts)
            ]
            both = dot(jnp.concatenate(pieces, axis=0), onehot_back[s])
            for k in range(parts):
                load[k, s] = both[16 * k : 16 * k + 8] + both[16 * k + 8 : 16 * k + 16]

    def advance(part, step, final):
        now = lax.rem(step, 2)
        later = 1 - now
        for side in range(2):

            @pl.when(present[side])
            def _():
                halo_copy(step, part, side, True).wait_recv()

        inner = pl.ds(1, row_count)
        flat = (members * 2 * block, half)
        low = jnp.stack(
            [halves[now, part, inner, 1, :, 0:half], halo_in[step, part, 1]], axis=1
        ).reshape(flat)
        high = jnp.stack(
            [halo_in[step, part, 0], halves[now, part, inner, 0, :, half : 2 * half]], axis=1
        ).reshape(flat)
        beside[...] = dot(jnp.concatenate([low, high], axis=1), stencil[2 * count : 3 * count, :])

        @pl.loop(0, row_count)
        def _(r):
            for x in range(PAIR):
                s = r * PAIR + x
                band = pl.ds(pl.multiple_of(s * 2 * block, 2 * block), 2 * block)
                both = summed[part, band, :] + beside[band, :]
                plane = (both[0:block] + both[block : 2 * block]).reshape(layers, own, count)
                u_old = u_now[part, s].reshape(layers, own, count)
                under = jnp.concatenate([u_old[0:1], u_old[: layers - 1]], axis=0)
                above = jnp.concatenate([u_old[1:], u_old[layers - 1 :]], axis=0)
                v_new = (
                    v_now[part, s].reshape(layers, own, count)
                    + stiff_now[s] * plane
                    - (TIME_STEP * THICKNESS) * (2.0 * u_old - under - above)
                )
                v_new = jnp.concatenate(
                    [v_new[: layers - 1], v_new[layers - 1 :] + load[part, s]], axis=0
                )
                u_new = (u_old + TIME_STEP * v_new).reshape(block, count)
                v_now[part, s] = v_new.reshape(block, count)
                u_now[part, s] = u_new
                if not final:
                    halves[later, part, 1 + r, x] = split(u_new)
                    place_halo(step + 1, part, r, x, u_new)

        if not final:
            send_halos(step + 1, part)
            interior(part, later)

    take_pressures(0)

    @pl.loop(0, SUBSTEPS)
    def _(step):
        @pl.loop(0, parts)
        def _(part):
            advance(part, step, False)

    spoken_rows = []
    for s in range(members):
        pieces = [split(v_now[k, s, block - own : block]) for k in range(parts)]
        both = dot(jnp.concatenate(pieces, axis=0), onehot[s])
        value = jnp.zeros((own, points), f32)
        for k in range(parts):
            value = value + facts[s, 6 + k : 7 + k, :] * (
                both[16 * k : 16 * k + 8] + both[16 * k + 8 : 16 * k + 16]
            )
        spoken[s] = value
        spoken_rows.append(value)
    pairs = members // 2
    speed_out[...] = jnp.concatenate(
        [
            jnp.concatenate(spoken_rows[:pairs], axis=1),
            jnp.concatenate(spoken_rows[pairs:], axis=1),
        ], axis=0
    ).astype(bf16)
    each(1, members, lambda d: speed_copy(d).start())
    speed_in[me] = speed_out[...]
    each(1, members, lambda d: speed_copy(d).wait_recv())

    def gathered():
        arrived = [speed_in[s].astype(f32) for s in range(members)]
        lower = jnp.concatenate([value[0:own] for value in arrived], axis=0)
        upper = jnp.concatenate([value[own : 2 * own] for value in arrived], axis=0)
        return jnp.concatenate([lower, upper], axis=1).astype(bf16)

    send_pressures(1, gathered)
    take_pressures(1)

    @pl.loop(SUBSTEPS, last_step)
    def _(step):
        @pl.loop(0, parts)
        def _(part):
            advance(part, step, False)

    @pl.loop(0, parts)
    def _(part):
        advance(part, last_step, True)
        for f, state in enumerate((u_now, v_now)):
            value = state[part]
            high = largest(value.reshape(members * layers, own, count))
            scale_out[part, :, f * (half // 2) : (f + 1) * (half // 2)] = jnp.broadcast_to(
                high * (1.0 / LEVELS), (1, half // 2)
            )
            whole = jnp.round(value * (LEVELS / high))
            final_out[part, :, f * block : (f + 1) * block, :] = whole.astype(i32).astype(i16)
        each(1, members, lambda d: final_copy(part, d).start())
        each(1, members, lambda d: scale_copy(part, d).start())
        final_in[part, me] = final_out[part, me]
        scale_in[part, me] = scale_out[part]

    @pl.loop(0, parts)
    def _(part):
        each(1, members, lambda d: final_copy(part, d).wait_recv())
        each(1, members, lambda d: scale_copy(part, d).wait_recv())
        value = final_in[part].astype(i32).astype(f32)
        for f, result in enumerate((u_out, v_out)):
            scale = scale_in[part, :, :, f * (half // 2) : f * (half // 2) + 1]
            rows = (value[:, f * block : (f + 1) * block] * scale).reshape(width, count)
            high = rows.astype(bf16)
            low = (rows - high.astype(f32)).astype(bf16)
            ordered = [dot(turn[...], piece).astype(bf16) for piece in (high, low)]
            back = dot_turned(eye[...], ordered[0]) + dot_turned(eye[...], ordered[1])
            for j in range(breadth):
                for lanes in range(2):
                    lines = pl.ds(lanes * breadth + j, height, stride=2 * breadth)
                    result[part, lines, :] = back[
                        j * height : (j + 1) * height, lanes * half : (lanes + 1) * half
                    ]

    each(1, members, lambda d: facts_copy(d).wait_send())
    each(1, depth_count, lambda d: places_copy(d).wait_send())
    each(1, members, lambda d: first_copy(d).wait_send())
    each(1, members, lambda d: in_copy(d).wait_send())
    each(1, members, lambda d: speed_copy(d).wait_send())
    for repeat in range(COUPLED):
        parts_taken(repeat, lambda copy: copy.wait_send())

    @pl.loop(0, parts)
    def _(part):
        each(1, members, lambda d: final_copy(part, d).wait_send())
        each(1, members, lambda d: scale_copy(part, d).wait_send())

        @pl.loop(0, last_step + 1)
        def _(step):
            for side in range(2):

                @pl.when(present[side])
                def _():
                    halo_copy(step, part, side, False).wait_send()


def plane_on_device(shape, displacement, velocity, stiffness, wet_position, wet_normal, wet_area, wet_map):
    col_count, row_count, _ = shape
    depth_count = col_count // PAIR
    members = row_count * PAIR
    parts, height, breadth, width = displacement.shape
    half = width // 2
    points = wet_map.shape[0]
    count = height * breadth
    own = LOADS // members
    block = own * (width // LOADS)
    steps = COUPLED * SUBSTEPS
    f32, bf16, i16 = jnp.float32, jnp.bfloat16, jnp.int16
    dma = pltpu.SemaphoreType.DMA

    def separated(state):
        tiled = state.reshape(parts, height, breadth, 2, half).transpose(0, 1, 3, 2, 4)
        return tiled.reshape(parts, height * 2 * breadth, half)

    def joined(state):
        tiled = state.reshape(parts, height, 2, breadth, half).transpose(0, 1, 3, 2, 4)
        return tiled.reshape(parts, height, breadth, width)

    raw = (parts, height * 2 * breadth, half)
    state = jax.ShapeDtypeStruct(raw, f32)
    field = VMEM((parts, members, block, count), f32)
    anywhere = pl.BlockSpec(memory_space=pl.ANY)
    slab = (members, parts, 2 * block, count)
    final = (parts, members, 2 * block, count)
    u_new, v_new = pl.pallas_call(
        functools.partial(plane_kernel, shape),
        out_shape=(state, state),
        in_specs=[anywhere] * 2 + [whole_spec()] * 5,
        out_specs=(whole_spec(), whole_spec()),
        scratch_shapes=[
            VMEM(raw, f32),
            VMEM(raw, f32),
            VMEM((width + LOADS, width), bf16),
            VMEM((width, width), bf16),
            VMEM((count, count), bf16),
            VMEM((3 * count, count), bf16),
            VMEM((2, 16, count), bf16),
            VMEM(slab, i16),
            VMEM(slab, i16),
            VMEM((16, points), f32),
            VMEM((members, 16, points), f32),
            VMEM((8, points), f32),
            VMEM((depth_count, 8, points), f32),
            VMEM((members, 6, points, half), f32),
            VMEM((LOADS, points), bf16),
            VMEM((members, LOADS, points), bf16),
            VMEM((depth_count, members * points, points), bf16),
            VMEM((COUPLED, depth_count, LOADS, points), f32),
            VMEM((COUPLED, depth_count, members, own, points), f32),
            VMEM((members, own, points), f32),
            VMEM((members, count, points), bf16),
            VMEM((members, points, count), bf16),
            field,
            field,
            VMEM((parts, members, own, count), f32),
            VMEM((2, parts, row_count + 2, PAIR, 2 * block, count), bf16),
            VMEM((parts, members * 2 * block, count), f32),
            VMEM((members * 2 * block, count), f32),
            VMEM((members, 8, count), f32),
            VMEM((LOADS, points), f32),
            VMEM((steps, parts, 2, row_count, block, half), bf16),
            VMEM((steps, parts, 2, row_count, 2 * block, half), bf16),
            VMEM((2 * own, members // 2 * points), bf16),
            VMEM((members, 2 * own, members // 2 * points), bf16),
            VMEM(final, i16),
            VMEM(final, i16),
            VMEM((parts, 1, half), f32),
            VMEM((parts, members, 1, half), f32),
            dma((2,)),
            dma((members,)),
            dma((members,)),
            dma((depth_count,)),
            dma((depth_count,)),
            dma((members,)),
            dma((members,)),
            dma((members,)),
            dma((members,)),
            dma((COUPLED, depth_count, members)),
            dma((COUPLED, depth_count, members)),
            dma((steps, parts, 2)),
            dma((steps, parts, 2)),
            dma((members,)),
            dma((members,)),
            dma((parts, members)),
            dma((parts, members)),
            dma((parts, members)),
            dma((parts, members)),
        ],
        compiler_params=pltpu.CompilerParams(
            collective_id=0, has_side_effects=True, vmem_limit_bytes=67043328
        ),
        name="plane_steps",
    )(
        separated(displacement), separated(velocity), stiffness.T, wet_position, wet_normal,
        wet_area[None, :], wet_map[None, :],
    )
    return (joined(u_new), joined(v_new))


def by_planes(shape, displacement, wet_map):
    col_count, row_count, _ = shape
    _, height, breadth, width = displacement.shape
    members = row_count * PAIR
    return (
        col_count % PAIR == 0
        and LOADS % members == 0
        and LOADS // members == 8
        and height * breadth == wet_map.shape[0] == width == 256
    )


def either(shape, *arrays):
    chosen = plane_on_device if by_planes(shape, arrays[0], arrays[-1]) else on_device
    return chosen(shape, *arrays)


def solution(mesh):
    sizes = mesh.shape
    shape = (sizes["tcol"], sizes["group"] * sizes["trow"], sizes["trow"])
    state = P(None, ("group", "trow"), "tcol", None)
    wet = ("group", "trow", "tcol")
    return jax.shard_map(
        functools.partial(either, shape),
        mesh=mesh,
        in_specs=(
            state,
            state,
            P(("group", "trow"), "tcol"),
            P(None, wet),
            P(None, wet),
            P(wet),
            P(wet),
        ),
        out_specs=(state, state),
        check_vma=False,
    )
```

```python
import functools
import math

import jax
import jax.numpy as jnp
from jax import lax
from jax.experimental import pallas as pl
from jax.experimental.pallas import tpu as pltpu
from jax.sharding import PartitionSpec as P

LOADS = 64
SUBSTEPS = 4
COUPLED = 2

SPHERE_AREA = 4.0 * math.pi
SMOOTHING = 0.1
TIME_STEP = 0.3
THICKNESS = 0.5
SPLINE_TAPS = (2.0 / 3.0, -1.0 / 12.0, -1.0 / 12.0, -1.0 / 6.0)
REACH = 3
PAD = 8
MESH = pl.DeviceIdType.MESH
VMEM = pltpu.VMEM


def row_device(index, trow_count):
    return {"group": index // trow_count, "trow": lax.rem(index, trow_count)}


def whole_spec():
    return pl.BlockSpec(memory_space=pltpu.VMEM)


HIGHEST = lax.Precision.HIGHEST


def coupled_kernel(
    shape, u_in, v_in, stiff_ref, position_ref, normal_ref, area_ref, node_ref, u_out, v_out,
    field, speed_now, work, load, col_out, col_in, row_out, row_in,
    geometry, sources, targets, target_cols, normal_cols, pick, spread,
    own_speeds, packed_out, packed_in, unpacked, tiles, partial_out, partial_in,
    halo_send, halo_recv, geo_send, geo_recv, speed_send, speed_recv, part_send, part_recv
):
    col_count, row_count, trow_count = shape
    parts, breadth, height, width = speed_now.shape
    half = width // 2
    points = geometry.shape[1]
    count = breadth * height
    col = lax.axis_index("tcol")
    row = lax.axis_index("group") * trow_count + lax.axis_index("trow")
    present = (col > 0, col < col_count - 1, row > 0, row < row_count - 1)
    peers = (
        {"tcol": jnp.maximum(col - 1, 0)},
        {"tcol": jnp.minimum(col + 1, col_count - 1)},
        row_device(jnp.maximum(row - 1, 0), trow_count),
        row_device(jnp.minimum(row + 1, row_count - 1), trow_count),
    )
    middle = pl.ds(PAD, height)

    def col_peer(d):
        return {"tcol": lax.rem(col + d, col_count)}

    def row_peer(d):
        return row_device(lax.rem(row + d, row_count), trow_count)

    barrier = pltpu.get_barrier_semaphore()

    @pl.loop(1, col_count)
    def _(d):
        pl.semaphore_signal(barrier, inc=1, device_id=col_peer(d), device_id_type=MESH)

    @pl.loop(1, row_count)
    def _(d):
        pl.semaphore_signal(barrier, inc=1, device_id=row_peer(d), device_id_type=MESH)

    geometry[0:3, :] = position_ref[...]
    geometry[3:6, :] = normal_ref[...] * (area_ref[...] * (1.0 / SPHERE_AREA))
    geometry[6:8, :] = jnp.zeros((2, points), jnp.float32)
    pl.semaphore_wait(barrier, col_count + row_count - 2)

    def geo_copy(kind, d):
        return pltpu.make_async_remote_copy(
            src_ref=geometry,
            dst_ref=sources.at[col] if kind == 0 else targets.at[row],
            send_sem=geo_send.at[kind, d],
            recv_sem=geo_recv.at[kind, d],
            device_id=col_peer(d) if kind == 0 else row_peer(d),
            device_id_type=MESH,
        )

    def speed_copy(repeat, d):
        return pltpu.make_async_remote_copy(
            src_ref=packed_out.at[repeat],
            dst_ref=packed_in.at[repeat, col],
            send_sem=speed_send.at[repeat, d],
            recv_sem=speed_recv.at[repeat, d],
            device_id=col_peer(d),
            device_id_type=MESH,
        )

    def part_copy(repeat, d):
        return pltpu.make_async_remote_copy(
            src_ref=partial_out.at[repeat, lax.rem(row + d, row_count)],
            dst_ref=partial_in.at[repeat, d],
            send_sem=part_send.at[repeat, d],
            recv_sem=part_recv.at[repeat, d],
            device_id=row_peer(d),
            device_id_type=MESH,
        )

    for kind, total in ((1, row_count), (0, col_count)):

        @pl.loop(1, total)
        def _(d):
            geo_copy(kind, d).start()

    sources[col] = geometry[...]
    targets[row] = geometry[...]

    field[...] = jnp.zeros_like(field)
    for part in range(parts):
        for j in range(breadth):
            for lanes in range(2):
                lines = pl.ds(lanes * breadth + j, height, stride=2 * breadth)
                cut = pl.ds(lanes * half, half)
                field[part, REACH + j, middle, cut] = u_in[part, lines, :]
                speed_now[part, j, :, cut] = v_in[part, lines, :]
    for side in range(2):

        @pl.when(jnp.logical_not(present[side]))
        def _():
            col_in[:, :, side] = jnp.zeros(col_in.shape[:2] + col_in.shape[3:], col_in.dtype)

    def as_column(line):
        return jnp.broadcast_to(line, (half, line.shape[1])).T

    for part in range(parts):
        normal_cols[part] = as_column(normal_ref[part : part + 1, :])
    spread[...] = (
        lax.broadcasted_iota(jnp.int32, (count, points), 0) == node_ref[...]
    ).astype(jnp.float32)
    pick[...] = spread[...].T

    def halo_copy(step, side, part, arriving):
        out_buffer, in_buffer = (col_out, col_in) if side < 2 else (row_out, row_in)
        own = side % 2
        other = own if arriving else 1 - own
        return pltpu.make_async_remote_copy(
            src_ref=out_buffer.at[step, part, own],
            dst_ref=in_buffer.at[step, part, other],
            send_sem=halo_send.at[step, part, side],
            recv_sem=halo_recv.at[step, part, (side // 2) * 2 + other],
            device_id=peers[side],
            device_id_type=MESH,
        )

    lane = lax.broadcasted_iota(jnp.int32, (height, half), 1)
    low = lane < half // 2
    low_half = lax.broadcasted_iota(jnp.int32, (points // 2, half), 1) < half // 2

    def pack(value):
        turned = pltpu.roll(value[points // 2 :], half // 2, 1)
        return jnp.where(low_half, turned, value[: points // 2])

    def tile(r):
        group = 32

        def block(index, carry):
            source = index // (points // half)
            lanes = pl.ds(pl.multiple_of(lax.rem(index, points // half) * half, half), half)
            line = [sources[source, k : k + 1, lanes] for k in range(6)]

            def rows_of(g, inner):
                rows = pl.ds(pl.multiple_of(g * group, group), group)
                dx = target_cols[r, 0, rows, :] - line[0]
                dy = target_cols[r, 1, rows, :] - line[1]
                dz = target_cols[r, 2, rows, :] - line[2]
                numerator = line[3] * dx + line[4] * dy + line[5] * dz
                squared = dx * dx + dy * dy + dz * dz + SMOOTHING * SMOOTHING
                inverse = lax.rsqrt(squared)
                value = numerator * inverse * (inverse * inverse)
                tiles[r, source, rows, lanes] = value.astype(jnp.bfloat16)
                return inner

            return lax.fori_loop(0, points // group, rows_of, carry, unroll=2)

        lax.fori_loop(0, col_count * (points // half), block, 0)

    def send_halos(step, part):
        for side, first in ((0, REACH), (1, breadth)):

            @pl.when(present[side])
            def _():
                for j in range(REACH):
                    col_out[step, part, side, j] = field[part, first + j, middle, :].astype(
                        col_out.dtype
                    )
                halo_copy(step, side, part, False).start()

        for side, first in ((2, PAD), (3, PAD + height - REACH)):

            @pl.when(present[side])
            def _():
                for j in range(breadth):
                    row_out[
                        step, part, side - 2, j // 2, (j % 2) * 4 : (j % 2) * 4 + REACH, :
                    ] = field[part, REACH + j, first : first + REACH, :]
                halo_copy(step, side, part, False).start()

    def local(part):
        def body(column, carry):
            a = field[part, REACH + column, middle, 0:half]
            b = field[part, REACH + column, middle, half:width]
            turned_a = pltpu.roll(a, half // 2, 1)
            turned_b = pltpu.roll(b, half // 2, 1)
            between = jnp.where(low, turned_a, turned_b)
            edge_a = jnp.where(low, a, turned_a)
            edge_b = jnp.where(low, turned_b, b)
            stiff = stiff_ref[column]
            for lanes, here, edge in ((0, a, edge_a), (1, b, edge_b)):
                cut = pl.ds(lanes * half, half)
                summed = (2.0 * SPLINE_TAPS[0]) * here
                for offset in range(1, REACH + 1):
                    summed = summed + SPLINE_TAPS[offset] * (
                        field[part, REACH + column + offset, middle, cut]
                        + field[part, REACH + column - offset, middle, cut]
                    )
                value = -(stiff * summed) - THICKNESS * (2.0 * here - between - edge)
                if lanes == 1:
                    value = value + load[part, column]
                work[part, column, :, cut] = speed_now[part, column, :, cut] + TIME_STEP * value
            return carry

        lax.fori_loop(0, breadth, body, 0)

    def complete(step, part):
        for side, first in ((2, PAD - REACH), (3, PAD + height)):

            @pl.when(present[side])
            def _():
                halo_copy(step, side, part, True).wait_recv()
                for j in range(breadth):
                    field[part, REACH + j, first : first + REACH, :] = row_in[
                        step, part, side - 2, j // 2, (j % 2) * 4 : (j % 2) * 4 + REACH, :
                    ]

        def along_rows(column, carry):
            stiff = stiff_ref[column] * (-TIME_STEP)
            for lanes in range(2):
                cut = pl.ds(lanes * half, half)
                summed = 0.0
                for offset in range(1, REACH + 1):
                    summed = summed + SPLINE_TAPS[offset] * (
                        field[part, REACH + column, pl.ds(PAD + offset, height), cut]
                        + field[part, REACH + column, pl.ds(PAD - offset, height), cut]
                    )
                work[part, column, :, cut] += stiff * summed
            return carry

        lax.fori_loop(0, breadth, along_rows, 0)

        for side in range(2):

            @pl.when(present[side])
            def _():
                halo_copy(step, side, part, True).wait_recv()

        for column in range(breadth):
            stiff = stiff_ref[column] * (-TIME_STEP)
            for lanes in range(2):
                cut = pl.ds(lanes * half, half)
                value = work[part, column, :, cut]
                summed = None
                for offset in range(1, REACH + 1):
                    for side, j in ((0, column - offset + REACH), (1, column + offset - breadth)):
                        inside = (column - offset < 0) if side == 0 else (column + offset >= breadth)
                        if inside:
                            term = SPLINE_TAPS[offset] * col_in[
                                step, part, side, j, :, cut
                            ].astype(jnp.float32)
                            summed = term if summed is None else summed + term
                if summed is not None:
                    value = value + stiff * summed
                speed_now[part, column, :, cut] = value
                field[part, REACH + column, middle, cut] += TIME_STEP * value

    for repeat in range(COUPLED):
        speeds = jnp.zeros((points, half), jnp.float32)
        for part in range(parts):
            outer = speed_now[part, :, :, half:width].reshape(count, half)
            picked = jnp.dot(
                pick[...], outer, precision=HIGHEST, preferred_element_type=jnp.float32
            )
            speeds = speeds + normal_cols[part] * picked
        own_speeds[...] = speeds
        packed_out[repeat] = pack(speeds).astype(packed_out.dtype)

        @pl.loop(1, col_count)
        def _(d):
            speed_copy(repeat, d).start()

        packed_in[repeat, col] = packed_out[repeat]

        if repeat == 0:

            @pl.loop(1, row_count)
            def _(d):
                geo_copy(1, d).wait_recv()

            @pl.loop(1, col_count)
            def _(d):
                geo_copy(0, d).wait_recv()

            @pl.loop(0, row_count)
            def _(r):
                for k in range(3):
                    target_cols[r, k] = as_column(targets[r, k : k + 1, :])

            tile(lax.rem(row + 1, row_count))

        @pl.loop(1, col_count)
        def _(d):
            speed_copy(repeat, d).wait_recv()

        @pl.loop(0, parts)
        def _(part):
            send_halos(repeat * SUBSTEPS, part)

        @pl.loop(0, col_count)
        def _(c):
            value = packed_in[repeat, c].astype(jnp.float32)
            unpacked[c, 0 : points // 2, :] = value.astype(jnp.bfloat16)
            unpacked[c, points // 2 : points, :] = pltpu.roll(value, half // 2, 1).astype(
                jnp.bfloat16
            )

        @pl.loop(1, row_count + 1)
        def _(d):
            r = lax.rem(row + d, row_count)
            total = jnp.zeros((points, half), jnp.float32)
            for c in range(col_count):
                total = total + jnp.dot(
                    tiles[r, c], unpacked[c], preferred_element_type=jnp.float32
                )
            partial_out[repeat, r] = pack(total)

            @pl.when(d < row_count)
            def _():
                part_copy(repeat, d).start()
                if repeat == 0:
                    tile(lax.rem(r + 1, row_count))

        received = partial_out[repeat, row]
        for d in range(1, row_count):
            part_copy(repeat, d).wait_recv()
            received = received + partial_in[repeat, d]
        low_points = jnp.concatenate([low_half, low_half], axis=0)
        both = jnp.concatenate([received, pltpu.roll(received, half // 2, 1)], axis=0)
        pressure = jnp.where(low_points, 0.0, 0.5 * own_speeds[...] + both)
        for part in range(parts):
            loading = jnp.dot(
                spread[...], -(normal_cols[part] * pressure),
                precision=HIGHEST, preferred_element_type=jnp.float32,
            )
            load[part] = loading.reshape(breadth, height, half)

            local(part)

        last = (repeat + 1) * SUBSTEPS - 1

        @pl.loop(repeat * SUBSTEPS, last + 1)
        def _(step):
            @pl.loop(0, parts)
            def _(part):
                complete(step, part)

                @pl.when(step < last)
                def _():
                    send_halos(step + 1, part)
                    local(part)

    for part in range(parts):
        for j in range(breadth):
            for lanes in range(2):
                lines = pl.ds(lanes * breadth + j, height, stride=2 * breadth)
                cut = pl.ds(lanes * half, half)
                u_out[part, lines, :] = field[part, REACH + j, middle, cut]
                v_out[part, lines, :] = speed_now[part, j, :, cut]

    @pl.loop(0, COUPLED * SUBSTEPS)
    def _(step):
        for side in range(4):

            @pl.when(present[side])
            def _():
                for part in range(parts):
                    halo_copy(step, side, part, False).wait_send()

    @pl.loop(1, col_count)
    def _(d):
        geo_copy(0, d).wait_send()
        for repeat in range(COUPLED):
            speed_copy(repeat, d).wait_send()

    @pl.loop(1, row_count)
    def _(d):
        geo_copy(1, d).wait_send()
        for repeat in range(COUPLED):
            part_copy(repeat, d).wait_send()


def on_device(shape, displacement, velocity, stiffness, wet_position, wet_normal, wet_area, wet_map):
    col_count, row_count, _ = shape
    parts, height, breadth, width = displacement.shape
    half = width // 2
    points = wet_map.shape[0]
    steps = COUPLED * SUBSTEPS
    stiff = jnp.broadcast_to(stiffness.T[:, :, None], (breadth, height, half))
    node = (wet_map % breadth) * height + wet_map // breadth

    def split(state):
        tiled = state.reshape(parts, height, breadth, 2, half).transpose(0, 1, 3, 2, 4)
        return tiled.reshape(parts, height * 2 * breadth, half)

    def joined(state):
        tiled = state.reshape(parts, height, 2, breadth, half).transpose(0, 1, 3, 2, 4)
        return tiled.reshape(parts, height, breadth, width)

    state = jax.ShapeDtypeStruct((parts, height * 2 * breadth, half), jnp.float32)
    cols = (steps, parts, 2, REACH, height, width)
    rows = (steps, parts, 2, breadth // 2, 8, width)
    f32, bf16 = jnp.float32, jnp.bfloat16
    dma = pltpu.SemaphoreType.DMA
    u_new, v_new = pl.pallas_call(
        functools.partial(coupled_kernel, shape),
        out_shape=(state, state),
        in_specs=[whole_spec()] * 7,
        out_specs=(whole_spec(), whole_spec()),
        scratch_shapes=[
            VMEM((parts, breadth + 2 * REACH, height + 2 * PAD, width), f32),
            VMEM((parts, breadth, height, width), f32),
            VMEM((parts, breadth, height, width), f32),
            VMEM((parts, breadth, height, half), f32),
            VMEM(cols, bf16),
            VMEM(cols, bf16),
            VMEM(rows, f32),
            VMEM(rows, f32),
            VMEM((8, points), f32),
            VMEM((col_count, 8, points), f32),
            VMEM((row_count, 8, points), f32),
            VMEM((row_count, 3, points, half), f32),
            VMEM((parts, points, half), f32),
            VMEM((points, height * breadth), f32),
            VMEM((height * breadth, points), f32),
            VMEM((points, half), f32),
            VMEM((COUPLED, points // 2, half), bf16),
            VMEM((COUPLED, col_count, points // 2, half), bf16),
            VMEM((col_count, points, half), bf16),
            VMEM((row_count, col_count, points, points), bf16),
            VMEM((COUPLED, row_count, points // 2, half), f32),
            VMEM((COUPLED, row_count, points // 2, half), f32),
            dma((steps, parts, 4)),
            dma((steps, parts, 4)),
            dma((2, max(col_count, row_count))),
            dma((2, max(col_count, row_count))),
            dma((COUPLED, col_count)),
            dma((COUPLED, col_count)),
            dma((COUPLED, row_count)),
            dma((COUPLED, row_count)),
        ],
        compiler_params=pltpu.CompilerParams(
            collective_id=0, has_side_effects=True, vmem_limit_bytes=67043328
        ),
        name="coupled_steps",
    )(
        split(displacement), split(velocity), stiff,
        wet_position, wet_normal, wet_area[None, :], node[None, :],
    )
    return (joined(u_new), joined(v_new))


PAIR = 2
LEVELS = 32767.0


def plane_kernel(
    shape, u_hbm, v_hbm, stiff_ref, position_ref, normal_ref, area_ref, map_ref, u_out, v_out,
    u_raw, v_raw, perm, turn, eye, stencil, in_out, in_in, facts_out, facts, places, targets,
    source_cols, first_out, first_in, tiles, part_out, part_in, spoken,
    onehot, onehot_back, u_now, v_now, load, halves, summed, patched, stiff_now, own_speed,
    halo_out, halo_in, speed_out, speed_in, final_out, final_in, scale_out, scale_in,
    load_sem, facts_send, facts_recv, places_send, places_recv, first_send, first_recv,
    in_send, in_recv, part_send, part_recv, halo_send, halo_recv, speed_send, speed_recv,
    final_send, final_recv, scale_send, scale_recv,
):
    col_count, row_count, trow_count = shape
    depth_count = col_count // PAIR
    members = row_count * PAIR
    total = members * depth_count
    parts, _, half = u_raw.shape
    count, points = onehot.shape[1:]
    breadth, height = stiff_ref.shape
    width = perm.shape[1]
    own = LOADS // members
    layers = width // LOADS
    block = own * layers
    columns = PAIR * breadth
    last_step = COUPLED * SUBSTEPS - 1
    f32, bf16, i16, i32 = jnp.float32, jnp.bfloat16, jnp.int16, jnp.int32
    col = lax.axis_index("tcol")
    row = lax.axis_index("group") * trow_count + lax.axis_index("trow")
    z = col // PAIR
    me = row * PAIR + lax.rem(col, PAIR)

    def device(depth, member):
        return dict(
            row_device(member // PAIR, trow_count), tcol=depth * PAIR + lax.rem(member, PAIR)
        )

    def member_of(d):
        return lax.rem(me + d, members)

    def depth_of(d):
        return lax.rem(z + d, depth_count)

    def each(first, last, action):
        @pl.loop(first, last)
        def _(d):
            action(d)

    barrier = pltpu.get_barrier_semaphore()

    @pl.loop(1, total)
    def _(d):
        to = device(depth_of(d // members), member_of(lax.rem(d, members)))
        pl.semaphore_signal(barrier, inc=1, device_id=to, device_id_type=MESH)

    v_load = pltpu.make_async_copy(v_hbm, v_raw, load_sem.at[0])
    u_load = pltpu.make_async_copy(u_hbm, u_raw, load_sem.at[1])
    v_load.start()
    u_load.start()

    def iota(size, axis):
        return lax.broadcasted_iota(i32, size, axis)

    def ones_where(mask):
        return jnp.where(mask, 1.0, 0.0).astype(bf16)

    def dot(a, b):
        return jnp.dot(a, b, preferred_element_type=f32)

    def dot_turned(a, b):
        return lax.dot_general(a, b, (((1,), (1,)), ((), ())), preferred_element_type=f32)

    def lane_of(line):
        member, inner = line // block, line % block
        return (inner // own) * LOADS + member * own + inner % own

    square = (width, width)
    line, column = iota(square, 0), iota(square, 1)
    perm[0:width, :] = ones_where(lane_of(line) == column)
    turn[...] = ones_where(lane_of(column) == line)
    outer = (LOADS, width)
    perm[width : width + LOADS, :] = ones_where(
        (layers - 1) * LOADS + iota(outer, 0) == iota(outer, 1)
    )
    eye[...] = ones_where(iota((count, count), 0) == iota((count, count), 1))

    src, dst = iota((count, count), 0), iota((count, count), 1)
    distance = jnp.abs(src - dst)
    taps = jnp.where(distance == 3, -2.0, jnp.where(distance < 3, -1.0, 0.0))
    taps = jnp.where(distance == 0, 16.0, taps)
    stencil[...] = jnp.where(src // half == dst // half, taps, 0.0).astype(bf16)

    spread = ones_where(iota((height, count), 0) == iota((height, count), 1) % height).astype(f32)
    wide = jnp.dot(stiff_ref[...], spread, precision=HIGHEST, preferred_element_type=f32)
    own_b = iota((breadth, count), 0) == iota((breadth, count), 1) // height
    places[0:3, :] = position_ref[...]
    places[3:8, :] = jnp.zeros((5, points), f32)
    facts_out[0:3, :] = position_ref[...]
    facts_out[3:6, :] = normal_ref[...] * (area_ref[...] * (1.0 / SPHERE_AREA))
    facts_out[6:9, :] = normal_ref[...]
    numbers = map_ref[...]
    facts_out[9:10, :] = ((numbers % breadth) * height + numbers // breadth).astype(f32)
    facts_out[10:11, :] = jnp.sum(jnp.where(own_b, wide, 0.0), axis=0, keepdims=True)
    facts_out[13:16, :] = jnp.zeros((3, points), f32)
    targets[z] = places[...]

    present = (z > 0, z < depth_count - 1)
    for side, first in ((0, 0), (1, columns + REACH)):

        @pl.when(jnp.logical_not(present[side]))
        def _():
            u_now[:, :, first : first + REACH] = jnp.zeros((2, parts, REACH, block, half), f32)

    def plane_copy(d, source, target, send, recv):
        return pltpu.make_async_remote_copy(
            src_ref=source, dst_ref=target.at[me], send_sem=send.at[d], recv_sem=recv.at[d],
            device_id=device(z, member_of(d)), device_id_type=MESH,
        )

    def facts_copy(d):
        return plane_copy(d, facts_out, facts, facts_send, facts_recv)

    def places_copy(d):
        return pltpu.make_async_remote_copy(
            src_ref=places, dst_ref=targets.at[z],
            send_sem=places_send.at[d], recv_sem=places_recv.at[d],
            device_id=device(depth_of(d), me), device_id_type=MESH,
        )

    def first_copy(d):
        return plane_copy(d, first_out, first_in, first_send, first_recv)

    def in_copy(d):
        return plane_copy(d, in_out.at[member_of(d)], in_in, in_send, in_recv)

    def speed_copy(d):
        return plane_copy(d, speed_out, speed_in, speed_send, speed_recv)

    def final_copy(part, d):
        return plane_copy(
            d, final_out.at[part, member_of(d)], final_in.at[part],
            final_send.at[part], final_recv.at[part],
        )

    def scale_copy(part, d):
        return plane_copy(
            d, scale_out.at[part], scale_in.at[part], scale_send.at[part], scale_recv.at[part]
        )

    def part_copy(repeat, dz, dj):
        lines = pl.ds(pl.multiple_of(member_of(dj) * own, own), own)
        return pltpu.make_async_remote_copy(
            src_ref=part_out.at[repeat, depth_of(dz), lines, :],
            dst_ref=part_in.at[repeat, z, me],
            send_sem=part_send.at[repeat, dz, dj], recv_sem=part_recv.at[repeat, dz, dj],
            device_id=device(depth_of(dz), member_of(dj)), device_id_type=MESH,
        )

    def halo_copy(step, part, side, arriving):
        there = side if arriving else 1 - side
        step_z = jnp.maximum(z - 1, 0) if side == 0 else jnp.minimum(z + 1, depth_count - 1)
        return pltpu.make_async_remote_copy(
            src_ref=halo_out.at[step, part, side],
            dst_ref=halo_in.at[step, part, there],
            send_sem=halo_send.at[step, part, side], recv_sem=halo_recv.at[step, part, there],
            device_id=device(step_z, me), device_id_type=MESH,
        )

    def as_column(value):
        return jnp.broadcast_to(value, (half, value.shape[1])).T

    bunch = iota((8, half), 1) // height
    upper_half, odd = bunch >= 2, bunch % 2 == 1

    def exchange(values):
        rows = values[0].shape[0]

        def choose(mask, a, b):
            shape3 = (rows // 8, 8, half)
            return jnp.where(mask, b.reshape(shape3), a.reshape(shape3)).reshape(rows, half)

        def rolled(value, bunches):
            return pltpu.roll(value, bunches * height, 1)

        lows = [choose(upper_half, values[i], rolled(values[i + 2], 2)) for i in range(2)]
        highs = [choose(upper_half, rolled(values[i], 2), values[i + 2]) for i in range(2)]
        result = []
        for first, second in (lows, highs):
            result.append(choose(odd, first, rolled(second, 1)))
            result.append(choose(odd, rolled(first, 3), second))
        return result

    def tile_lanes(t):
        return slice(t * half, (t + 1) * half)

    def one_hot(s):
        onehot[s] = ones_where(iota((count, points), 0).astype(f32) == facts[s, 9:10, :])

    def one_hot_back(s):
        nodes = as_column(facts[s, 9:10, :])
        for lanes in range(2):
            numbers = (iota((points, half), 1) + lanes * half).astype(f32)
            onehot_back[s, :, lanes * half : (lanes + 1) * half] = ones_where(numbers == nodes)

    facts[me] = facts_out[...]
    one_hot(me)

    def largest(value):
        reduced = jnp.max(jnp.abs(value), axis=0)
        top = jnp.max(jnp.max(reduced, axis=1, keepdims=True), axis=0, keepdims=True)
        return jnp.maximum(top, 1e-30)

    def split(value):
        high = value.astype(bf16).astype(f32)
        return jnp.concatenate([high, value - high], axis=-2).astype(bf16)

    def turned(raw, part, inverse, lines):
        rows = []
        for j in range(breadth):
            picks = [
                raw[part, pl.ds(lanes * breadth + j, height, stride=2 * breadth), :]
                for lanes in range(2)
            ]
            rows.append(jnp.concatenate(picks, axis=1))
        value = jnp.round(jnp.concatenate(rows, axis=0) * inverse)
        high = jnp.round(value * (1.0 / 256.0))
        low = value - 256.0 * high
        return (
            dot_turned(perm[0:lines, :], high.astype(bf16)),
            dot_turned(perm[0:lines, :], low.astype(bf16)),
        )

    def top_of(raw):
        return largest(raw[...].reshape(raw.shape[0] * raw.shape[1] // 8, 8, half))

    v_load.wait()
    v_top = top_of(v_raw)
    v_scale, v_inverse = v_top * (1.0 / LEVELS), LEVELS / v_top
    facts_out[12:13, :] = jnp.broadcast_to(v_scale, (1, points))
    picked_all = jnp.zeros((LOADS, points), f32)
    for part in range(parts):
        high, low = turned(v_raw, part, v_inverse, width + LOADS)
        whole = high[0:width] * 256.0 + low[0:width]
        in_out[:, part, block : 2 * block, :] = (
            whole.reshape(members, block, count).astype(i32).astype(i16)
        )
        rows = jnp.concatenate([high[width:], low[width:]], axis=0).astype(bf16)
        both = dot(rows, onehot[me])
        picked = both[0:LOADS] * 256.0 + both[LOADS:]
        picked_all = picked_all + picked * (normal_ref[part : part + 1, :] * v_scale)
    own_speed[...] = picked_all
    first_out[...] = picked_all.astype(bf16)
    first_in[me] = first_out[...]

    u_load.wait()
    u_top = top_of(u_raw)
    u_scale, u_inverse = u_top * (1.0 / LEVELS), LEVELS / u_top
    facts_out[11:12, :] = jnp.broadcast_to(u_scale, (1, points))
    facts[me] = facts_out[...]
    for part in range(parts):
        high, low = turned(u_raw, part, u_inverse, width)
        whole = high * 256.0 + low
        in_out[:, part, 0:block, :] = whole.reshape(members, block, count).astype(i32).astype(i16)
    in_in[me] = in_out[me]

    pl.semaphore_wait(barrier, total - 1)
    each(1, members, lambda d: facts_copy(d).start())
    each(1, depth_count, lambda d: places_copy(d).start())
    each(1, members, lambda d: first_copy(d).start())
    each(1, members, lambda d: in_copy(d).start())

    each(1, members, lambda d: facts_copy(d).wait_recv())

    @pl.loop(0, members)
    def _(s):
        for k in range(6):
            source_cols[s, k] = as_column(facts[s, k : k + 1, :])

    group = 32

    def tile(depth):
        def blocks(index, carry):
            source = index // (points // half)
            lanes = pl.ds(pl.multiple_of(lax.rem(index, points // half) * half, half), half)
            known = [targets[depth, k : k + 1, lanes] for k in range(3)]

            def rows_of(g, inner):
                start = pl.multiple_of(g * group, group)
                rows = pl.ds(start, group)
                dx = known[0] - source_cols[source, 0, rows, :]
                dy = known[1] - source_cols[source, 1, rows, :]
                dz = known[2] - source_cols[source, 2, rows, :]
                numerator = (
                    source_cols[source, 3, rows, :] * dx
                    + source_cols[source, 4, rows, :] * dy
                    + source_cols[source, 5, rows, :] * dz
                )
                squared = dx * dx + dy * dy + dz * dz + SMOOTHING * SMOOTHING
                inverse = lax.rsqrt(squared)
                value = numerator * inverse * (inverse * inverse)
                deep = pl.ds(pl.multiple_of(source * points + start, group), group)
                tiles[depth, deep, lanes] = value.astype(bf16)
                return inner

            return lax.fori_loop(0, points // group, rows_of, carry, unroll=2)

        lax.fori_loop(0, members * (points // half), blocks, 0)

    def send_pressures(repeat, speeds):
        @pl.loop(1, depth_count + 1)
        def _(d):
            depth = depth_of(d)
            if repeat == 0:

                @pl.when(d < depth_count)
                def _():
                    places_copy(depth_count - d).wait_recv()

                tile(depth)

                @pl.when(d == 1)
                def _():
                    each(1, members, lambda d: first_copy(d).wait_recv())

            value = dot(speeds(), tiles[depth])
            if repeat == 0:
                value = value + jnp.where(depth == z, 0.5, 0.0) * own_speed[...]
            part_out[repeat, depth] = value

            @pl.when(d < depth_count)
            def _():
                each(0, members, lambda dj: part_copy(repeat, d, dj).start())

            @pl.when(d == depth_count)
            def _():
                each(1, members, lambda dj: part_copy(repeat, 0, dj).start())

        part_in[repeat, z, me] = part_out[
            repeat, z, pl.ds(pl.multiple_of(me * own, own), own), :
        ]

    def parts_taken(repeat, action):
        each(1, members, lambda dj: action(part_copy(repeat, 0, dj)))

        @pl.loop(1, depth_count)
        def _(d):
            each(0, members, lambda dj: action(part_copy(repeat, d, dj)))

    def interior(part, now):
        lines = halves[now, part].reshape(columns // 2 * 2 * block, 2 * half)
        summed[part] = dot(lines, stencil[...])

    def send_halos(step, part):
        for side in range(2):

            @pl.when(present[side])
            def _():
                halo_copy(step, part, side, False).start()

    def place(step, part, later, pair, j, value):
        c = pair * 2 + j
        u_now[later, part, REACH + c] = value
        high = value.astype(bf16)
        halves[later, part, pair, 0:block, tile_lanes(j)] = high
        halves[later, part, pair, block : 2 * block, tile_lanes(j)] = (
            value - high.astype(f32)
        ).astype(bf16)
        if isinstance(c, int):
            for side, first in ((0, 0), (1, columns - REACH)):
                if first <= c < first + REACH:
                    halo_out[step, part, side, c - first] = high

    send_pressures(
        0, lambda: jnp.concatenate([first_in[s] for s in range(members)], axis=1)
    )

    @pl.loop(0, members, unroll=2)
    def _(s):
        one_hot(s)
        one_hot_back(s)

    for x in range(PAIR):
        for t in range(breadth // 4):
            given = [
                jnp.broadcast_to(facts[r * PAIR + x, 10:11, tile_lanes(t)], (8, half))
                for r in range(row_count)
            ]
            for g, value in enumerate(exchange(given)):
                stiff_now[x * breadth + t * 4 + g] = value * (-TIME_STEP / 12.0)

    each(1, members, lambda d: in_copy(d).wait_recv())

    @pl.loop(0, parts)
    def _(part):
        for x in range(PAIR):
            for t in range(breadth // 4):
                given = []
                for r in range(row_count):
                    value = in_in[r * PAIR + x, part, :, tile_lanes(t)].astype(i32).astype(f32)
                    scales = facts[r * PAIR + x, 11:13, tile_lanes(t)]
                    given.append(jnp.concatenate(
                        [value[0:block] * scales[0:1], value[block:] * scales[1:2]], axis=0
                    ))
                for g, value in enumerate(exchange(given)):
                    c = x * breadth + t * 4 + g
                    v_now[part, c] = value[block:]
                    place(0, part, 0, c // 2, c % 2, value[0:block])
        send_halos(0, part)
        interior(part, 0)

    def take_pressures(repeat):
        parts_taken(repeat, lambda copy: copy.wait_recv())

        @pl.loop(0, members, unroll=4)
        def _(s):
            value = part_in[repeat, 0, s]
            for d in range(1, depth_count):
                value = value + part_in[repeat, d, s]
            if repeat > 0:
                value = value + 0.5 * spoken[s]
            pieces = [
                split(value * (facts[s, 6 + k : 7 + k, :] * (-TIME_STEP))) for k in range(parts)
            ]
            both = dot(jnp.concatenate(pieces, axis=0), onehot_back[s])
            patched[s] = jnp.concatenate(
                [
                    both[16 * k : 16 * k + 8] + both[16 * k + 8 : 16 * k + 16]
                    for k in range(parts)
                ], axis=0
            )

        for x in range(PAIR):
            for t in range(breadth // 4):
                given = [patched[r * PAIR + x, :, tile_lanes(t)] for r in range(row_count)]
                for g, value in enumerate(exchange(given)):
                    for k in range(parts):
                        load[k, x * breadth + t * 4 + g] = value[own * k : own * (k + 1)]

    def advance(part, step, final):
        now = lax.rem(step, 2)
        later = 1 - now
        for side, first in ((0, 0), (1, columns + REACH)):

            @pl.when(present[side])
            def _():
                halo_copy(step, part, side, True).wait_recv()
                u_now[now, part, first : first + REACH] = halo_in[step, part, side].astype(f32)

        def update(pair, start):
            for j in range(2):
                c = pair * 2 + j
                both = summed[part, pl.ds(start, 2 * block), tile_lanes(j)]
                plane = both[0:block] + both[block : 2 * block]

                def near(offset):
                    return u_now[now, part, REACH + c + offset]

                beside = (near(-1) + near(1)) + (near(-2) + near(2))
                beside = beside + 2.0 * (near(-3) + near(3))
                plane = (plane - beside).reshape(layers, own, half)
                u_old = near(0).reshape(layers, own, half)
                under = jnp.concatenate([u_old[0:1], u_old[: layers - 1]], axis=0)
                above = jnp.concatenate([u_old[1:], u_old[layers - 1 :]], axis=0)
                v_new = (
                    v_now[part, c].reshape(layers, own, half)
                    + stiff_now[c] * plane
                    - (TIME_STEP * THICKNESS) * (2.0 * u_old - under - above)
                )
                v_new = jnp.concatenate(
                    [v_new[: layers - 1], v_new[layers - 1 :] + load[part, c]], axis=0
                )
                u_new = (u_old + TIME_STEP * v_new).reshape(block, half)
                v_now[part, c] = v_new.reshape(block, half)
                if final:
                    u_now[later, part, REACH + c] = u_new
                else:
                    place(step + 1, part, later, pair, j, u_new)

        edge = (REACH + 1) // 2
        for pair in list(range(edge)) + list(range(columns // 2 - edge, columns // 2)):
            update(pair, pair * 2 * block)
        if not final:
            send_halos(step + 1, part)

        @pl.loop(edge, columns // 2 - edge, unroll=2)
        def _(pair):
            update(pair, pl.multiple_of(pair * 2 * block, 2 * block))

        if not final:
            interior(part, later)

    take_pressures(0)

    @pl.loop(0, SUBSTEPS)
    def _(step):
        @pl.loop(0, parts)
        def _(part):
            advance(part, step, False)

    for x in range(PAIR):
        for t in range(breadth // 4):
            given = []
            for g in range(4):
                c = x * breadth + t * 4 + g
                given.append(jnp.concatenate(
                    [v_now[k, c, block - own : block] for k in range(parts)], axis=0
                ))
            for r, value in enumerate(exchange(given)):
                patched[r * PAIR + x, :, tile_lanes(t)] = value

    spoken_rows = []
    for s in range(members):
        pieces = [split(patched[s, own * k : own * (k + 1)]) for k in range(parts)]
        both = dot(jnp.concatenate(pieces, axis=0), onehot[s])
        value = jnp.zeros((own, points), f32)
        for k in range(parts):
            value = value + facts[s, 6 + k : 7 + k, :] * (
                both[16 * k : 16 * k + 8] + both[16 * k + 8 : 16 * k + 16]
            )
        spoken[s] = value
        spoken_rows.append(value)
    pairs = members // 2
    speed_out[...] = jnp.concatenate(
        [
            jnp.concatenate(spoken_rows[:pairs], axis=1),
            jnp.concatenate(spoken_rows[pairs:], axis=1),
        ], axis=0
    ).astype(bf16)
    each(1, members, lambda d: speed_copy(d).start())
    speed_in[me] = speed_out[...]
    each(1, members, lambda d: speed_copy(d).wait_recv())

    def gathered():
        arrived = [speed_in[s].astype(f32) for s in range(members)]
        lower = jnp.concatenate([value[0:own] for value in arrived], axis=0)
        upper = jnp.concatenate([value[own : 2 * own] for value in arrived], axis=0)
        return jnp.concatenate([lower, upper], axis=1).astype(bf16)

    send_pressures(1, gathered)
    take_pressures(1)

    @pl.loop(SUBSTEPS, last_step)
    def _(step):
        @pl.loop(0, parts)
        def _(part):
            advance(part, step, False)

    @pl.loop(0, parts)
    def _(part):
        advance(part, last_step, True)
        done = 1 - last_step % 2
        for f, state in enumerate((u_now.at[done, part, pl.ds(REACH, columns)], v_now.at[part])):
            high = largest(state[...].reshape(columns * layers, own, half))
            scale_out[part, :, f * (half // 2) : (f + 1) * (half // 2)] = jnp.broadcast_to(
                high * (1.0 / LEVELS), (1, half // 2)
            )
            inverse = LEVELS / high
            for x in range(PAIR):
                for t in range(breadth // 4):
                    given = [state[x * breadth + t * 4 + g] * inverse for g in range(4)]
                    for r, value in enumerate(exchange(given)):
                        final_out[
                            part, r * PAIR + x, f * block : (f + 1) * block, tile_lanes(t)
                        ] = jnp.round(value).astype(i32).astype(i16)
        each(1, members, lambda d: final_copy(part, d).start())
        each(1, members, lambda d: scale_copy(part, d).start())
        final_in[part, me] = final_out[part, me]
        scale_in[part, me] = scale_out[part]

    @pl.loop(0, parts)
    def _(part):
        each(1, members, lambda d: final_copy(part, d).wait_recv())
        each(1, members, lambda d: scale_copy(part, d).wait_recv())
        value = final_in[part].astype(i32).astype(f32)
        for f, result in enumerate((u_out, v_out)):
            scale = scale_in[part, :, :, f * (half // 2) : f * (half // 2) + 1]
            rows = (value[:, f * block : (f + 1) * block] * scale).reshape(width, count)
            high = rows.astype(bf16)
            low = (rows - high.astype(f32)).astype(bf16)
            ordered = [dot(turn[...], piece).astype(bf16) for piece in (high, low)]
            back = dot_turned(eye[...], ordered[0]) + dot_turned(eye[...], ordered[1])
            for j in range(breadth):
                for lanes in range(2):
                    lines = pl.ds(lanes * breadth + j, height, stride=2 * breadth)
                    result[part, lines, :] = back[
                        j * height : (j + 1) * height, lanes * half : (lanes + 1) * half
                    ]

    each(1, members, lambda d: facts_copy(d).wait_send())
    each(1, depth_count, lambda d: places_copy(d).wait_send())
    each(1, members, lambda d: first_copy(d).wait_send())
    each(1, members, lambda d: in_copy(d).wait_send())
    each(1, members, lambda d: speed_copy(d).wait_send())
    for repeat in range(COUPLED):
        parts_taken(repeat, lambda copy: copy.wait_send())

    @pl.loop(0, parts)
    def _(part):
        each(1, members, lambda d: final_copy(part, d).wait_send())
        each(1, members, lambda d: scale_copy(part, d).wait_send())

        @pl.loop(0, last_step + 1)
        def _(step):
            for side in range(2):

                @pl.when(present[side])
                def _():
                    halo_copy(step, part, side, False).wait_send()


def plane_on_device(shape, displacement, velocity, stiffness, wet_position, wet_normal, wet_area, wet_map):
    col_count, row_count, _ = shape
    depth_count = col_count // PAIR
    members = row_count * PAIR
    parts, height, breadth, width = displacement.shape
    half = width // 2
    points = wet_map.shape[0]
    count = height * breadth
    own = LOADS // members
    block = own * (width // LOADS)
    steps = COUPLED * SUBSTEPS
    f32, bf16, i16 = jnp.float32, jnp.bfloat16, jnp.int16
    dma = pltpu.SemaphoreType.DMA

    def separated(state):
        tiled = state.reshape(parts, height, breadth, 2, half).transpose(0, 1, 3, 2, 4)
        return tiled.reshape(parts, height * 2 * breadth, half)

    def joined(state):
        tiled = state.reshape(parts, height, 2, breadth, half).transpose(0, 1, 3, 2, 4)
        return tiled.reshape(parts, height, breadth, width)

    raw = (parts, height * 2 * breadth, half)
    state = jax.ShapeDtypeStruct(raw, f32)
    columns = PAIR * breadth
    anywhere = pl.BlockSpec(memory_space=pl.ANY)
    slab = (members, parts, 2 * block, count)
    final = (parts, members, 2 * block, count)
    u_new, v_new = pl.pallas_call(
        functools.partial(plane_kernel, shape),
        out_shape=(state, state),
        in_specs=[anywhere] * 2 + [whole_spec()] * 5,
        out_specs=(whole_spec(), whole_spec()),
        scratch_shapes=[
            VMEM(raw, f32),
            VMEM(raw, f32),
            VMEM((width + LOADS, width), bf16),
            VMEM((width, width), bf16),
            VMEM((count, count), bf16),
            VMEM((count, count), bf16),
            VMEM(slab, i16),
            VMEM(slab, i16),
            VMEM((16, points), f32),
            VMEM((members, 16, points), f32),
            VMEM((8, points), f32),
            VMEM((depth_count, 8, points), f32),
            VMEM((members, 6, points, half), f32),
            VMEM((LOADS, points), bf16),
            VMEM((members, LOADS, points), bf16),
            VMEM((depth_count, members * points, points), bf16),
            VMEM((COUPLED, depth_count, LOADS, points), f32),
            VMEM((COUPLED, depth_count, members, own, points), f32),
            VMEM((members, own, points), f32),
            VMEM((members, count, points), bf16),
            VMEM((members, points, count), bf16),
            VMEM((2, parts, columns + 2 * REACH, block, half), f32),
            VMEM((parts, columns, block, half), f32),
            VMEM((parts, columns, own, half), f32),
            VMEM((2, parts, columns // 2, 2 * block, 2 * half), bf16),
            VMEM((parts, columns * block, 2 * half), f32),
            VMEM((members, parts * own, count), f32),
            VMEM((columns, 8, half), f32),
            VMEM((LOADS, points), f32),
            VMEM((steps, parts, 2, REACH, block, half), bf16),
            VMEM((steps, parts, 2, REACH, block, half), bf16),
            VMEM((2 * own, members // 2 * points), bf16),
            VMEM((members, 2 * own, members // 2 * points), bf16),
            VMEM(final, i16),
            VMEM(final, i16),
            VMEM((parts, 1, half), f32),
            VMEM((parts, members, 1, half), f32),
            dma((2,)),
            dma((members,)),
            dma((members,)),
            dma((depth_count,)),
            dma((depth_count,)),
            dma((members,)),
            dma((members,)),
            dma((members,)),
            dma((members,)),
            dma((COUPLED, depth_count, members)),
            dma((COUPLED, depth_count, members)),
            dma((steps, parts, 2)),
            dma((steps, parts, 2)),
            dma((members,)),
            dma((members,)),
            dma((parts, members)),
            dma((parts, members)),
            dma((parts, members)),
            dma((parts, members)),
        ],
        compiler_params=pltpu.CompilerParams(
            collective_id=0, has_side_effects=True, vmem_limit_bytes=48000000
        ),
        name="plane_steps",
    )(
        pltpu.with_memory_space_constraint(separated(displacement), pltpu.HBM),
        pltpu.with_memory_space_constraint(separated(velocity), pltpu.HBM),
        stiffness.T, wet_position, wet_normal,
        wet_area[None, :], wet_map[None, :],
    )
    return (joined(u_new), joined(v_new))


def by_planes(shape, displacement, wet_map):
    col_count, row_count, _ = shape
    _, height, breadth, width = displacement.shape
    members = row_count * PAIR
    return (
        col_count % PAIR == 0
        and LOADS % members == 0
        and LOADS // members == 8
        and height * breadth == wet_map.shape[0] == width == 256
        and row_count == 4
        and height == 32
    )


def either(shape, *arrays):
    chosen = plane_on_device if by_planes(shape, arrays[0], arrays[-1]) else on_device
    return chosen(shape, *arrays)


def solution(mesh):
    sizes = mesh.shape
    shape = (sizes["tcol"], sizes["group"] * sizes["trow"], sizes["trow"])
    state = P(None, ("group", "trow"), "tcol", None)
    wet = ("group", "trow", "tcol")
    return jax.shard_map(
        functools.partial(either, shape),
        mesh=mesh,
        in_specs=(
            state,
            state,
            P(("group", "trow"), "tcol"),
            P(None, wet),
            P(None, wet),
            P(wet),
            P(wet),
        ),
        out_specs=(state, state),
        check_vma=False,
    )
```

```python
import functools
import math

import jax
import jax.numpy as jnp
from jax import lax
from jax.experimental import pallas as pl
from jax.experimental.pallas import tpu as pltpu
from jax.sharding import PartitionSpec as P

LOADS = 64
SUBSTEPS = 4
COUPLED = 2

SPHERE_AREA = 4.0 * math.pi
SMOOTHING = 0.1
TIME_STEP = 0.3
THICKNESS = 0.5
SPLINE_TAPS = (2.0 / 3.0, -1.0 / 12.0, -1.0 / 12.0, -1.0 / 6.0)
REACH = 3
PAD = 8
MESH = pl.DeviceIdType.MESH
VMEM = pltpu.VMEM


def row_device(index, trow_count):
    return {"group": index // trow_count, "trow": lax.rem(index, trow_count)}


def whole_spec():
    return pl.BlockSpec(memory_space=pltpu.VMEM)


HIGHEST = lax.Precision.HIGHEST


def coupled_kernel(
    shape, u_in, v_in, stiff_ref, position_ref, normal_ref, area_ref, node_ref, u_out, v_out,
    field, speed_now, work, load, col_out, col_in, row_out, row_in,
    geometry, sources, targets, target_cols, normal_cols, pick, spread,
    own_speeds, packed_out, packed_in, unpacked, tiles, partial_out, partial_in,
    halo_send, halo_recv, geo_send, geo_recv, speed_send, speed_recv, part_send, part_recv
):
    col_count, row_count, trow_count = shape
    parts, breadth, height, width = speed_now.shape
    half = width // 2
    points = geometry.shape[1]
    count = breadth * height
    col = lax.axis_index("tcol")
    row = lax.axis_index("group") * trow_count + lax.axis_index("trow")
    present = (col > 0, col < col_count - 1, row > 0, row < row_count - 1)
    peers = (
        {"tcol": jnp.maximum(col - 1, 0)},
        {"tcol": jnp.minimum(col + 1, col_count - 1)},
        row_device(jnp.maximum(row - 1, 0), trow_count),
        row_device(jnp.minimum(row + 1, row_count - 1), trow_count),
    )
    middle = pl.ds(PAD, height)

    def col_peer(d):
        return {"tcol": lax.rem(col + d, col_count)}

    def row_peer(d):
        return row_device(lax.rem(row + d, row_count), trow_count)

    barrier = pltpu.get_barrier_semaphore()

    @pl.loop(1, col_count)
    def _(d):
        pl.semaphore_signal(barrier, inc=1, device_id=col_peer(d), device_id_type=MESH)

    @pl.loop(1, row_count)
    def _(d):
        pl.semaphore_signal(barrier, inc=1, device_id=row_peer(d), device_id_type=MESH)

    geometry[0:3, :] = position_ref[...]
    geometry[3:6, :] = normal_ref[...] * (area_ref[...] * (1.0 / SPHERE_AREA))
    geometry[6:8, :] = jnp.zeros((2, points), jnp.float32)
    pl.semaphore_wait(barrier, col_count + row_count - 2)

    def geo_copy(kind, d):
        return pltpu.make_async_remote_copy(
            src_ref=geometry,
            dst_ref=sources.at[col] if kind == 0 else targets.at[row],
            send_sem=geo_send.at[kind, d],
            recv_sem=geo_recv.at[kind, d],
            device_id=col_peer(d) if kind == 0 else row_peer(d),
            device_id_type=MESH,
        )

    def speed_copy(repeat, d):
        return pltpu.make_async_remote_copy(
            src_ref=packed_out.at[repeat],
            dst_ref=packed_in.at[repeat, col],
            send_sem=speed_send.at[repeat, d],
            recv_sem=speed_recv.at[repeat, d],
            device_id=col_peer(d),
            device_id_type=MESH,
        )

    def part_copy(repeat, d):
        return pltpu.make_async_remote_copy(
            src_ref=partial_out.at[repeat, lax.rem(row + d, row_count)],
            dst_ref=partial_in.at[repeat, d],
            send_sem=part_send.at[repeat, d],
            recv_sem=part_recv.at[repeat, d],
            device_id=row_peer(d),
            device_id_type=MESH,
        )

    for kind, total in ((1, row_count), (0, col_count)):

        @pl.loop(1, total)
        def _(d):
            geo_copy(kind, d).start()

    sources[col] = geometry[...]
    targets[row] = geometry[...]

    field[...] = jnp.zeros_like(field)
    for part in range(parts):
        for j in range(breadth):
            for lanes in range(2):
                lines = pl.ds(lanes * breadth + j, height, stride=2 * breadth)
                cut = pl.ds(lanes * half, half)
                field[part, REACH + j, middle, cut] = u_in[part, lines, :]
                speed_now[part, j, :, cut] = v_in[part, lines, :]
    for side in range(2):

        @pl.when(jnp.logical_not(present[side]))
        def _():
            col_in[:, :, side] = jnp.zeros(col_in.shape[:2] + col_in.shape[3:], col_in.dtype)

    def as_column(line):
        return jnp.broadcast_to(line, (half, line.shape[1])).T

    for part in range(parts):
        normal_cols[part] = as_column(normal_ref[part : part + 1, :])
    spread[...] = (
        lax.broadcasted_iota(jnp.int32, (count, points), 0) == node_ref[...]
    ).astype(jnp.float32)
    pick[...] = spread[...].T

    def halo_copy(step, side, part, arriving):
        out_buffer, in_buffer = (col_out, col_in) if side < 2 else (row_out, row_in)
        own = side % 2
        other = own if arriving else 1 - own
        return pltpu.make_async_remote_copy(
            src_ref=out_buffer.at[step, part, own],
            dst_ref=in_buffer.at[step, part, other],
            send_sem=halo_send.at[step, part, side],
            recv_sem=halo_recv.at[step, part, (side // 2) * 2 + other],
            device_id=peers[side],
            device_id_type=MESH,
        )

    lane = lax.broadcasted_iota(jnp.int32, (height, half), 1)
    low = lane < half // 2
    low_half = lax.broadcasted_iota(jnp.int32, (points // 2, half), 1) < half // 2

    def pack(value):
        turned = pltpu.roll(value[points // 2 :], half // 2, 1)
        return jnp.where(low_half, turned, value[: points // 2])

    def tile(r):
        group = 32

        def block(index, carry):
            source = index // (points // half)
            lanes = pl.ds(pl.multiple_of(lax.rem(index, points // half) * half, half), half)
            line = [sources[source, k : k + 1, lanes] for k in range(6)]

            def rows_of(g, inner):
                rows = pl.ds(pl.multiple_of(g * group, group), group)
                dx = target_cols[r, 0, rows, :] - line[0]
                dy = target_cols[r, 1, rows, :] - line[1]
                dz = target_cols[r, 2, rows, :] - line[2]
                numerator = line[3] * dx + line[4] * dy + line[5] * dz
                squared = dx * dx + dy * dy + dz * dz + SMOOTHING * SMOOTHING
                inverse = lax.rsqrt(squared)
                value = numerator * inverse * (inverse * inverse)
                tiles[r, source, rows, lanes] = value.astype(jnp.bfloat16)
                return inner

            return lax.fori_loop(0, points // group, rows_of, carry, unroll=2)

        lax.fori_loop(0, col_count * (points // half), block, 0)

    def send_halos(step, part):
        for side, first in ((0, REACH), (1, breadth)):

            @pl.when(present[side])
            def _():
                for j in range(REACH):
                    col_out[step, part, side, j] = field[part, first + j, middle, :].astype(
                        col_out.dtype
                    )
                halo_copy(step, side, part, False).start()

        for side, first in ((2, PAD), (3, PAD + height - REACH)):

            @pl.when(present[side])
            def _():
                for j in range(breadth):
                    row_out[
                        step, part, side - 2, j // 2, (j % 2) * 4 : (j % 2) * 4 + REACH, :
                    ] = field[part, REACH + j, first : first + REACH, :]
                halo_copy(step, side, part, False).start()

    def local(part):
        def body(column, carry):
            a = field[part, REACH + column, middle, 0:half]
            b = field[part, REACH + column, middle, half:width]
            turned_a = pltpu.roll(a, half // 2, 1)
            turned_b = pltpu.roll(b, half // 2, 1)
            between = jnp.where(low, turned_a, turned_b)
            edge_a = jnp.where(low, a, turned_a)
            edge_b = jnp.where(low, turned_b, b)
            stiff = stiff_ref[column]
            for lanes, here, edge in ((0, a, edge_a), (1, b, edge_b)):
                cut = pl.ds(lanes * half, half)
                summed = (2.0 * SPLINE_TAPS[0]) * here
                for offset in range(1, REACH + 1):
                    summed = summed + SPLINE_TAPS[offset] * (
                        field[part, REACH + column + offset, middle, cut]
                        + field[part, REACH + column - offset, middle, cut]
                    )
                value = -(stiff * summed) - THICKNESS * (2.0 * here - between - edge)
                if lanes == 1:
                    value = value + load[part, column]
                work[part, column, :, cut] = speed_now[part, column, :, cut] + TIME_STEP * value
            return carry

        lax.fori_loop(0, breadth, body, 0)

    def complete(step, part):
        for side, first in ((2, PAD - REACH), (3, PAD + height)):

            @pl.when(present[side])
            def _():
                halo_copy(step, side, part, True).wait_recv()
                for j in range(breadth):
                    field[part, REACH + j, first : first + REACH, :] = row_in[
                        step, part, side - 2, j // 2, (j % 2) * 4 : (j % 2) * 4 + REACH, :
                    ]

        def along_rows(column, carry):
            stiff = stiff_ref[column] * (-TIME_STEP)
            for lanes in range(2):
                cut = pl.ds(lanes * half, half)
                summed = 0.0
                for offset in range(1, REACH + 1):
                    summed = summed + SPLINE_TAPS[offset] * (
                        field[part, REACH + column, pl.ds(PAD + offset, height), cut]
                        + field[part, REACH + column, pl.ds(PAD - offset, height), cut]
                    )
                work[part, column, :, cut] += stiff * summed
            return carry

        lax.fori_loop(0, breadth, along_rows, 0)

        for side in range(2):

            @pl.when(present[side])
            def _():
                halo_copy(step, side, part, True).wait_recv()

        for column in range(breadth):
            stiff = stiff_ref[column] * (-TIME_STEP)
            for lanes in range(2):
                cut = pl.ds(lanes * half, half)
                value = work[part, column, :, cut]
                summed = None
                for offset in range(1, REACH + 1):
                    for side, j in ((0, column - offset + REACH), (1, column + offset - breadth)):
                        inside = (column - offset < 0) if side == 0 else (column + offset >= breadth)
                        if inside:
                            term = SPLINE_TAPS[offset] * col_in[
                                step, part, side, j, :, cut
                            ].astype(jnp.float32)
                            summed = term if summed is None else summed + term
                if summed is not None:
                    value = value + stiff * summed
                speed_now[part, column, :, cut] = value
                field[part, REACH + column, middle, cut] += TIME_STEP * value

    for repeat in range(COUPLED):
        speeds = jnp.zeros((points, half), jnp.float32)
        for part in range(parts):
            outer = speed_now[part, :, :, half:width].reshape(count, half)
            picked = jnp.dot(
                pick[...], outer, precision=HIGHEST, preferred_element_type=jnp.float32
            )
            speeds = speeds + normal_cols[part] * picked
        own_speeds[...] = speeds
        packed_out[repeat] = pack(speeds).astype(packed_out.dtype)

        @pl.loop(1, col_count)
        def _(d):
            speed_copy(repeat, d).start()

        packed_in[repeat, col] = packed_out[repeat]

        if repeat == 0:

            @pl.loop(1, row_count)
            def _(d):
                geo_copy(1, d).wait_recv()

            @pl.loop(1, col_count)
            def _(d):
                geo_copy(0, d).wait_recv()

            @pl.loop(0, row_count)
            def _(r):
                for k in range(3):
                    target_cols[r, k] = as_column(targets[r, k : k + 1, :])

            tile(lax.rem(row + 1, row_count))

        @pl.loop(1, col_count)
        def _(d):
            speed_copy(repeat, d).wait_recv()

        @pl.loop(0, parts)
        def _(part):
            send_halos(repeat * SUBSTEPS, part)

        @pl.loop(0, col_count)
        def _(c):
            value = packed_in[repeat, c].astype(jnp.float32)
            unpacked[c, 0 : points // 2, :] = value.astype(jnp.bfloat16)
            unpacked[c, points // 2 : points, :] = pltpu.roll(value, half // 2, 1).astype(
                jnp.bfloat16
            )

        @pl.loop(1, row_count + 1)
        def _(d):
            r = lax.rem(row + d, row_count)
            total = jnp.zeros((points, half), jnp.float32)
            for c in range(col_count):
                total = total + jnp.dot(
                    tiles[r, c], unpacked[c], preferred_element_type=jnp.float32
                )
            partial_out[repeat, r] = pack(total)

            @pl.when(d < row_count)
            def _():
                part_copy(repeat, d).start()
                if repeat == 0:
                    tile(lax.rem(r + 1, row_count))

        received = partial_out[repeat, row]
        for d in range(1, row_count):
            part_copy(repeat, d).wait_recv()
            received = received + partial_in[repeat, d]
        low_points = jnp.concatenate([low_half, low_half], axis=0)
        both = jnp.concatenate([received, pltpu.roll(received, half // 2, 1)], axis=0)
        pressure = jnp.where(low_points, 0.0, 0.5 * own_speeds[...] + both)
        for part in range(parts):
            loading = jnp.dot(
                spread[...], -(normal_cols[part] * pressure),
                precision=HIGHEST, preferred_element_type=jnp.float32,
            )
            load[part] = loading.reshape(breadth, height, half)

            local(part)

        last = (repeat + 1) * SUBSTEPS - 1

        @pl.loop(repeat * SUBSTEPS, last + 1)
        def _(step):
            @pl.loop(0, parts)
            def _(part):
                complete(step, part)

                @pl.when(step < last)
                def _():
                    send_halos(step + 1, part)
                    local(part)

    for part in range(parts):
        for j in range(breadth):
            for lanes in range(2):
                lines = pl.ds(lanes * breadth + j, height, stride=2 * breadth)
                cut = pl.ds(lanes * half, half)
                u_out[part, lines, :] = field[part, REACH + j, middle, cut]
                v_out[part, lines, :] = speed_now[part, j, :, cut]

    @pl.loop(0, COUPLED * SUBSTEPS)
    def _(step):
        for side in range(4):

            @pl.when(present[side])
            def _():
                for part in range(parts):
                    halo_copy(step, side, part, False).wait_send()

    @pl.loop(1, col_count)
    def _(d):
        geo_copy(0, d).wait_send()
        for repeat in range(COUPLED):
            speed_copy(repeat, d).wait_send()

    @pl.loop(1, row_count)
    def _(d):
        geo_copy(1, d).wait_send()
        for repeat in range(COUPLED):
            part_copy(repeat, d).wait_send()


def on_device(shape, displacement, velocity, stiffness, wet_position, wet_normal, wet_area, wet_map):
    col_count, row_count, _ = shape
    parts, height, breadth, width = displacement.shape
    half = width // 2
    points = wet_map.shape[0]
    steps = COUPLED * SUBSTEPS
    stiff = jnp.broadcast_to(stiffness.T[:, :, None], (breadth, height, half))
    node = (wet_map % breadth) * height + wet_map // breadth

    def split(state):
        tiled = state.reshape(parts, height, breadth, 2, half).transpose(0, 1, 3, 2, 4)
        return tiled.reshape(parts, height * 2 * breadth, half)

    def joined(state):
        tiled = state.reshape(parts, height, 2, breadth, half).transpose(0, 1, 3, 2, 4)
        return tiled.reshape(parts, height, breadth, width)

    state = jax.ShapeDtypeStruct((parts, height * 2 * breadth, half), jnp.float32)
    cols = (steps, parts, 2, REACH, height, width)
    rows = (steps, parts, 2, breadth // 2, 8, width)
    f32, bf16 = jnp.float32, jnp.bfloat16
    dma = pltpu.SemaphoreType.DMA
    u_new, v_new = pl.pallas_call(
        functools.partial(coupled_kernel, shape),
        out_shape=(state, state),
        in_specs=[whole_spec()] * 7,
        out_specs=(whole_spec(), whole_spec()),
        scratch_shapes=[
            VMEM((parts, breadth + 2 * REACH, height + 2 * PAD, width), f32),
            VMEM((parts, breadth, height, width), f32),
            VMEM((parts, breadth, height, width), f32),
            VMEM((parts, breadth, height, half), f32),
            VMEM(cols, bf16),
            VMEM(cols, bf16),
            VMEM(rows, f32),
            VMEM(rows, f32),
            VMEM((8, points), f32),
            VMEM((col_count, 8, points), f32),
            VMEM((row_count, 8, points), f32),
            VMEM((row_count, 3, points, half), f32),
            VMEM((parts, points, half), f32),
            VMEM((points, height * breadth), f32),
            VMEM((height * breadth, points), f32),
            VMEM((points, half), f32),
            VMEM((COUPLED, points // 2, half), bf16),
            VMEM((COUPLED, col_count, points // 2, half), bf16),
            VMEM((col_count, points, half), bf16),
            VMEM((row_count, col_count, points, points), bf16),
            VMEM((COUPLED, row_count, points // 2, half), f32),
            VMEM((COUPLED, row_count, points // 2, half), f32),
            dma((steps, parts, 4)),
            dma((steps, parts, 4)),
            dma((2, max(col_count, row_count))),
            dma((2, max(col_count, row_count))),
            dma((COUPLED, col_count)),
            dma((COUPLED, col_count)),
            dma((COUPLED, row_count)),
            dma((COUPLED, row_count)),
        ],
        compiler_params=pltpu.CompilerParams(
            collective_id=0, has_side_effects=True, vmem_limit_bytes=67043328
        ),
        name="coupled_steps",
    )(
        split(displacement), split(velocity), stiff,
        wet_position, wet_normal, wet_area[None, :], node[None, :],
    )
    return (joined(u_new), joined(v_new))


PAIR = 2
LEVELS = 32767.0


def plane_kernel(
    shape, u_hbm, v_hbm, stiff_ref, position_ref, normal_ref, area_ref, map_ref, u_out, v_out,
    u_raw, v_raw, perm, turn, eye, stencil, in_out, in_in, facts_out, facts, places, targets,
    source_cols, first_out, first_in, tiles, part_out, part_in, spoken,
    onehot, onehot_back, u_now, v_now, load, halves, summed, patched, stiff_now, own_speed,
    gathered_speeds, halo_out, halo_in, speed_out, speed_in, final_out, final_in, scale_out, scale_in,
    load_sem, facts_send, facts_recv, places_send, places_recv, first_send, first_recv,
    in_send, in_recv, part_send, part_recv, halo_send, halo_recv, speed_send, speed_recv,
    final_send, final_recv, scale_send, scale_recv,
):
    col_count, row_count, trow_count = shape
    depth_count = col_count // PAIR
    members = row_count * PAIR
    total = members * depth_count
    parts, _, half = u_raw.shape
    count, points = onehot.shape[1:]
    breadth, height = stiff_ref.shape
    width = perm.shape[1]
    own = LOADS // members
    layers = width // LOADS
    block = own * layers
    columns = PAIR * breadth
    last_step = COUPLED * SUBSTEPS - 1
    f32, bf16, i16, i32 = jnp.float32, jnp.bfloat16, jnp.int16, jnp.int32
    col = lax.axis_index("tcol")
    row = lax.axis_index("group") * trow_count + lax.axis_index("trow")
    z = col // PAIR
    me = row * PAIR + lax.rem(col, PAIR)

    def device(depth, member):
        return dict(
            row_device(member // PAIR, trow_count), tcol=depth * PAIR + lax.rem(member, PAIR)
        )

    def member_of(d):
        return lax.rem(me + d, members)

    def depth_of(d):
        return lax.rem(z + d, depth_count)

    def each(first, last, action):
        @pl.loop(first, last)
        def _(d):
            action(d)

    barrier = pltpu.get_barrier_semaphore()

    @pl.loop(1, total)
    def _(d):
        to = device(depth_of(d // members), member_of(lax.rem(d, members)))
        pl.semaphore_signal(barrier, inc=1, device_id=to, device_id_type=MESH)

    v_load = pltpu.make_async_copy(v_hbm, v_raw, load_sem.at[0])
    u_load = pltpu.make_async_copy(u_hbm, u_raw, load_sem.at[1])
    v_load.start()
    u_load.start()

    def iota(size, axis):
        return lax.broadcasted_iota(i32, size, axis)

    def ones_where(mask):
        return jnp.where(mask, 1.0, 0.0).astype(bf16)

    def dot(a, b):
        return jnp.dot(a, b, preferred_element_type=f32)

    def dot_turned(a, b):
        return lax.dot_general(a, b, (((1,), (1,)), ((), ())), preferred_element_type=f32)

    def lane_of(line):
        member, inner = line // block, line % block
        return (inner // own) * LOADS + member * own + inner % own

    square = (width, width)
    line, column = iota(square, 0), iota(square, 1)
    perm[0:width, :] = ones_where(lane_of(line) == column)
    turn[...] = ones_where(lane_of(column) == line)
    outer = (LOADS, width)
    perm[width : width + LOADS, :] = ones_where(
        (layers - 1) * LOADS + iota(outer, 0) == iota(outer, 1)
    )
    eye[...] = ones_where(iota((count, count), 0) == iota((count, count), 1))

    src, dst = iota((count, count), 0), iota((count, count), 1)
    distance = jnp.abs(src - dst)
    taps = jnp.where(distance == 3, -2.0, jnp.where(distance < 3, -1.0, 0.0))
    taps = jnp.where(distance == 0, 16.0, taps)
    stencil[...] = jnp.where(src // half == dst // half, taps, 0.0).astype(bf16)

    spread = ones_where(iota((height, count), 0) == iota((height, count), 1) % height).astype(f32)
    wide = jnp.dot(stiff_ref[...], spread, precision=HIGHEST, preferred_element_type=f32)
    own_b = iota((breadth, count), 0) == iota((breadth, count), 1) // height
    places[0:3, :] = position_ref[...]
    places[3:8, :] = jnp.zeros((5, points), f32)
    facts_out[0:3, :] = position_ref[...]
    facts_out[3:6, :] = normal_ref[...] * (area_ref[...] * (1.0 / SPHERE_AREA))
    facts_out[6:9, :] = normal_ref[...]
    numbers = map_ref[...]
    facts_out[9:10, :] = ((numbers % breadth) * height + numbers // breadth).astype(f32)
    facts_out[10:11, :] = jnp.sum(jnp.where(own_b, wide, 0.0), axis=0, keepdims=True)
    facts_out[13:16, :] = jnp.zeros((3, points), f32)
    targets[z] = places[...]

    present = (z > 0, z < depth_count - 1)
    for side, first in ((0, 0), (1, columns + REACH)):

        @pl.when(jnp.logical_not(present[side]))
        def _():
            u_now[:, :, first : first + REACH] = jnp.zeros((2, parts, REACH, block, half), f32)

    def plane_copy(d, source, target, send, recv):
        return pltpu.make_async_remote_copy(
            src_ref=source, dst_ref=target.at[me], send_sem=send.at[d], recv_sem=recv.at[d],
            device_id=device(z, member_of(d)), device_id_type=MESH,
        )

    def facts_copy(d):
        return plane_copy(d, facts_out, facts, facts_send, facts_recv)

    def places_copy(d):
        return pltpu.make_async_remote_copy(
            src_ref=places, dst_ref=targets.at[z],
            send_sem=places_send.at[d], recv_sem=places_recv.at[d],
            device_id=device(depth_of(d), me), device_id_type=MESH,
        )

    def first_copy(d):
        return plane_copy(d, first_out, first_in, first_send, first_recv)

    def in_copy(d):
        return plane_copy(d, in_out.at[member_of(d)], in_in, in_send, in_recv)

    def speed_copy(d):
        return plane_copy(d, speed_out, speed_in, speed_send, speed_recv)

    def final_copy(part, d):
        return plane_copy(
            d, final_out.at[part, member_of(d)], final_in.at[part],
            final_send.at[part], final_recv.at[part],
        )

    def scale_copy(part, d):
        return plane_copy(
            d, scale_out.at[part], scale_in.at[part], scale_send.at[part], scale_recv.at[part]
        )

    def part_copy(repeat, dz, dj):
        lines = pl.ds(pl.multiple_of(member_of(dj) * own, own), own)
        return pltpu.make_async_remote_copy(
            src_ref=part_out.at[repeat, depth_of(dz), lines, :],
            dst_ref=part_in.at[repeat, z, me],
            send_sem=part_send.at[repeat, dz, dj], recv_sem=part_recv.at[repeat, dz, dj],
            device_id=device(depth_of(dz), member_of(dj)), device_id_type=MESH,
        )

    def halo_copy(step, part, side, arriving):
        there = side if arriving else 1 - side
        step_z = jnp.maximum(z - 1, 0) if side == 0 else jnp.minimum(z + 1, depth_count - 1)
        return pltpu.make_async_remote_copy(
            src_ref=halo_out.at[step, part, side],
            dst_ref=halo_in.at[step, part, there],
            send_sem=halo_send.at[step, part, side], recv_sem=halo_recv.at[step, part, there],
            device_id=device(step_z, me), device_id_type=MESH,
        )

    def as_column(value):
        return jnp.broadcast_to(value, (half, value.shape[1])).T

    bunch = iota((8, half), 1) // height
    upper_half, odd = bunch >= 2, bunch % 2 == 1

    def exchange(values):
        rows = values[0].shape[0]

        def choose(mask, a, b):
            shape3 = (rows // 8, 8, half)
            return jnp.where(mask, b.reshape(shape3), a.reshape(shape3)).reshape(rows, half)

        def rolled(value, bunches):
            return pltpu.roll(value, bunches * height, 1)

        lows = [choose(upper_half, values[i], rolled(values[i + 2], 2)) for i in range(2)]
        highs = [choose(upper_half, rolled(values[i], 2), values[i + 2]) for i in range(2)]
        result = []
        for first, second in (lows, highs):
            result.append(choose(odd, first, rolled(second, 1)))
            result.append(choose(odd, rolled(first, 3), second))
        return result

    def tile_lanes(t):
        return slice(t * half, (t + 1) * half)

    def one_hot(s):
        onehot[s] = ones_where(iota((count, points), 0).astype(f32) == facts[s, 9:10, :])

    def one_hot_back(s):
        nodes = as_column(facts[s, 9:10, :])
        for lanes in range(2):
            numbers = (iota((points, half), 1) + lanes * half).astype(f32)
            onehot_back[s, :, lanes * half : (lanes + 1) * half] = ones_where(numbers == nodes)

    facts[me] = facts_out[...]
    one_hot(me)

    def largest(value):
        reduced = jnp.max(jnp.abs(value), axis=0)
        top = jnp.max(jnp.max(reduced, axis=1, keepdims=True), axis=0, keepdims=True)
        return jnp.maximum(top, 1e-30)

    def split(value):
        high = value.astype(bf16).astype(f32)
        return jnp.concatenate([high, value - high], axis=-2).astype(bf16)

    def turned(raw, part, inverse, lines):
        rows = []
        for j in range(breadth):
            picks = [
                raw[part, pl.ds(lanes * breadth + j, height, stride=2 * breadth), :]
                for lanes in range(2)
            ]
            rows.append(jnp.concatenate(picks, axis=1))
        value = jnp.round(jnp.concatenate(rows, axis=0) * inverse)
        high = jnp.round(value * (1.0 / 256.0))
        low = value - 256.0 * high
        return (
            dot_turned(perm[0:lines, :], high.astype(bf16)),
            dot_turned(perm[0:lines, :], low.astype(bf16)),
        )

    def top_of(raw):
        return largest(raw[...].reshape(raw.shape[0] * raw.shape[1] // 8, 8, half))

    v_load.wait()
    v_top = top_of(v_raw)
    v_scale, v_inverse = v_top * (1.0 / LEVELS), LEVELS / v_top
    facts_out[12:13, :] = jnp.broadcast_to(v_scale, (1, points))
    picked_all = jnp.zeros((LOADS, points), f32)
    for part in range(parts):
        high, low = turned(v_raw, part, v_inverse, width + LOADS)
        whole = high[0:width] * 256.0 + low[0:width]
        in_out[:, part, block : 2 * block, :] = (
            whole.reshape(members, block, count).astype(i32).astype(i16)
        )
        rows = jnp.concatenate([high[width:], low[width:]], axis=0).astype(bf16)
        both = dot(rows, onehot[me])
        picked = both[0:LOADS] * 256.0 + both[LOADS:]
        picked_all = picked_all + picked * (normal_ref[part : part + 1, :] * v_scale)
    own_speed[...] = picked_all
    first_out[...] = picked_all.astype(bf16)
    first_in[me] = first_out[...]

    u_load.wait()
    u_top = top_of(u_raw)
    u_scale, u_inverse = u_top * (1.0 / LEVELS), LEVELS / u_top
    facts_out[11:12, :] = jnp.broadcast_to(u_scale, (1, points))
    facts[me] = facts_out[...]
    for part in range(parts):
        high, low = turned(u_raw, part, u_inverse, width)
        whole = high * 256.0 + low
        in_out[:, part, 0:block, :] = whole.reshape(members, block, count).astype(i32).astype(i16)
    in_in[me] = in_out[me]

    pl.semaphore_wait(barrier, total - 1)
    each(1, members, lambda d: facts_copy(d).start())
    each(1, depth_count, lambda d: places_copy(d).start())
    each(1, members, lambda d: first_copy(d).start())
    each(1, members, lambda d: in_copy(d).start())

    each(1, members, lambda d: facts_copy(d).wait_recv())

    @pl.loop(0, members)
    def _(s):
        for k in range(6):
            source_cols[s, k] = as_column(facts[s, k : k + 1, :])

    group = 32

    def tile(depth):
        known = [
            [targets[depth, k : k + 1, lanes * half : (lanes + 1) * half] for k in range(3)]
            for lanes in range(2)
        ]

        def blocks(source, carry):
            def rows_of(g, inner):
                start = pl.multiple_of(g * group, group)
                rows = pl.ds(start, group)
                place_x, place_y, place_z, normal_x, normal_y, normal_z = [
                    source_cols[source, k, rows, :] for k in range(6)
                ]
                deep = pl.ds(pl.multiple_of(source * points + start, group), group)
                for lanes in range(2):
                    dx = known[lanes][0] - place_x
                    dy = known[lanes][1] - place_y
                    dz = known[lanes][2] - place_z
                    numerator = normal_x * dx + normal_y * dy + normal_z * dz
                    squared = dx * dx + dy * dy + dz * dz + SMOOTHING * SMOOTHING
                    inverse = lax.rsqrt(squared)
                    value = numerator * inverse * (inverse * inverse)
                    tiles[depth, deep, tile_lanes(lanes)] = value.astype(bf16)
                return inner

            return lax.fori_loop(0, points // group, rows_of, carry, unroll=2)

        lax.fori_loop(0, members, blocks, 0)

    def send_pressures(repeat, speeds):
        @pl.loop(1, depth_count + 1)
        def _(d):
            depth = depth_of(d)
            if repeat == 0:

                @pl.when(d < depth_count)
                def _():
                    places_copy(depth_count - d).wait_recv()

                tile(depth)

                @pl.when(d == 1)
                def _():
                    each(1, members, lambda d: first_copy(d).wait_recv())
                    for s in range(members):
                        speeds[:, s * points : (s + 1) * points] = first_in[s]

            value = dot(speeds[...], tiles[depth])
            if repeat == 0:
                value = value + jnp.where(depth == z, 0.5, 0.0) * own_speed[...]
            part_out[repeat, depth] = value

            @pl.when(d < depth_count)
            def _():
                each(0, members, lambda dj: part_copy(repeat, d, dj).start())

            @pl.when(d == depth_count)
            def _():
                each(1, members, lambda dj: part_copy(repeat, 0, dj).start())

        part_in[repeat, z, me] = part_out[
            repeat, z, pl.ds(pl.multiple_of(me * own, own), own), :
        ]

    def parts_taken(repeat, action):
        each(1, members, lambda dj: action(part_copy(repeat, 0, dj)))

        @pl.loop(1, depth_count)
        def _(d):
            each(0, members, lambda dj: action(part_copy(repeat, d, dj)))

    def interior(part, now):
        lines = halves[now, part].reshape(columns // 2 * 2 * block, 2 * half)
        summed[part] = dot(lines, stencil[...])

    def send_halos(step, part):
        for side in range(2):

            @pl.when(present[side])
            def _():
                halo_copy(step, part, side, False).start()

    def place(step, part, later, pair, j, value):
        c = pair * 2 + j
        u_now[later, part, REACH + c] = value
        high = value.astype(bf16)
        halves[later, part, pair, 0:block, tile_lanes(j)] = high
        halves[later, part, pair, block : 2 * block, tile_lanes(j)] = (
            value - high.astype(f32)
        ).astype(bf16)
        if isinstance(c, int):
            for side, first in ((0, 0), (1, columns - REACH)):
                if first <= c < first + REACH:
                    halo_out[step, part, side, c - first] = high

    send_pressures(0, gathered_speeds)

    @pl.loop(0, members, unroll=2)
    def _(s):
        one_hot(s)
        one_hot_back(s)

    for x in range(PAIR):
        for t in range(breadth // 4):
            given = [
                jnp.broadcast_to(facts[r * PAIR + x, 10:11, tile_lanes(t)], (8, half))
                for r in range(row_count)
            ]
            for g, value in enumerate(exchange(given)):
                stiff_now[x * breadth + t * 4 + g] = value * (-TIME_STEP / 12.0)

    each(1, members, lambda d: in_copy(d).wait_recv())

    @pl.loop(0, parts)
    def _(part):
        for x in range(PAIR):
            for t in range(breadth // 4):
                given = []
                for r in range(row_count):
                    value = in_in[r * PAIR + x, part, :, tile_lanes(t)].astype(i32).astype(f32)
                    scales = facts[r * PAIR + x, 11:13, tile_lanes(t)]
                    given.append(jnp.concatenate(
                        [value[0:block] * scales[0:1], value[block:] * scales[1:2]], axis=0
                    ))
                for g, value in enumerate(exchange(given)):
                    c = x * breadth + t * 4 + g
                    v_now[part, c] = value[block:]
                    place(0, part, 0, c // 2, c % 2, value[0:block])
        send_halos(0, part)
        interior(part, 0)

    def take_pressures(repeat):
        parts_taken(repeat, lambda copy: copy.wait_recv())

        @pl.loop(0, members, unroll=4)
        def _(s):
            value = part_in[repeat, 0, s]
            for d in range(1, depth_count):
                value = value + part_in[repeat, d, s]
            if repeat > 0:
                value = value + 0.5 * spoken[s]
            pieces = [
                split(value * (facts[s, 6 + k : 7 + k, :] * (-TIME_STEP))) for k in range(parts)
            ]
            both = dot(jnp.concatenate(pieces, axis=0), onehot_back[s])
            patched[s] = jnp.concatenate(
                [
                    both[16 * k : 16 * k + 8] + both[16 * k + 8 : 16 * k + 16]
                    for k in range(parts)
                ], axis=0
            )

        for x in range(PAIR):
            for t in range(breadth // 4):
                given = [patched[r * PAIR + x, :, tile_lanes(t)] for r in range(row_count)]
                for g, value in enumerate(exchange(given)):
                    for k in range(parts):
                        load[k, x * breadth + t * 4 + g] = value[own * k : own * (k + 1)]

    def advance(part, step, final, later_interior=False):
        now = lax.rem(step, 2)
        later = 1 - now
        for side, first in ((0, 0), (1, columns + REACH)):

            @pl.when(present[side])
            def _():
                halo_copy(step, part, side, True).wait_recv()
                u_now[now, part, first : first + REACH] = halo_in[step, part, side].astype(f32)

        def update(pair, start):
            for j in range(2):
                c = pair * 2 + j
                both = summed[part, pl.ds(start, 2 * block), tile_lanes(j)]
                plane = both[0:block] + both[block : 2 * block]

                def near(offset):
                    return u_now[now, part, REACH + c + offset]

                beside = (near(-1) + near(1)) + (near(-2) + near(2))
                beside = beside + 2.0 * (near(-3) + near(3))
                plane = (plane - beside).reshape(layers, own, half)
                u_old = near(0).reshape(layers, own, half)
                under = jnp.concatenate([u_old[0:1], u_old[: layers - 1]], axis=0)
                above = jnp.concatenate([u_old[1:], u_old[layers - 1 :]], axis=0)
                v_new = (
                    v_now[part, c].reshape(layers, own, half)
                    + stiff_now[c] * plane
                    - (TIME_STEP * THICKNESS) * (2.0 * u_old - under - above)
                )
                v_new = jnp.concatenate(
                    [v_new[: layers - 1], v_new[layers - 1 :] + load[part, c]], axis=0
                )
                u_new = (u_old + TIME_STEP * v_new).reshape(block, half)
                v_now[part, c] = v_new.reshape(block, half)
                if final:
                    u_now[later, part, REACH + c] = u_new
                else:
                    place(step + 1, part, later, pair, j, u_new)

        edge = (REACH + 1) // 2
        for pair in list(range(edge)) + list(range(columns // 2 - edge, columns // 2)):
            update(pair, pair * 2 * block)
        if not final:
            send_halos(step + 1, part)

        @pl.loop(edge, columns // 2 - edge, unroll=2)
        def _(pair):
            update(pair, pl.multiple_of(pair * 2 * block, 2 * block))

        if not final and not later_interior:
            interior(part, later)

    take_pressures(0)

    @pl.loop(0, SUBSTEPS - 1)
    def _(step):
        @pl.loop(0, parts)
        def _(part):
            advance(part, step, False)

    @pl.loop(0, parts)
    def _(part):
        advance(part, SUBSTEPS - 1, False, True)

    for x in range(PAIR):
        for t in range(breadth // 4):
            given = []
            for g in range(4):
                c = x * breadth + t * 4 + g
                given.append(jnp.concatenate(
                    [v_now[k, c, block - own : block] for k in range(parts)], axis=0
                ))
            for r, value in enumerate(exchange(given)):
                patched[r * PAIR + x, :, tile_lanes(t)] = value

    spoken_rows = []
    for s in range(members):
        pieces = [split(patched[s, own * k : own * (k + 1)]) for k in range(parts)]
        both = dot(jnp.concatenate(pieces, axis=0), onehot[s])
        value = jnp.zeros((own, points), f32)
        for k in range(parts):
            value = value + facts[s, 6 + k : 7 + k, :] * (
                both[16 * k : 16 * k + 8] + both[16 * k + 8 : 16 * k + 16]
            )
        spoken[s] = value
        spoken_rows.append(value)
    pairs = members // 2
    speed_out[...] = jnp.concatenate(
        [
            jnp.concatenate(spoken_rows[:pairs], axis=1),
            jnp.concatenate(spoken_rows[pairs:], axis=1),
        ], axis=0
    ).astype(bf16)
    each(1, members, lambda d: speed_copy(d).start())
    speed_in[me] = speed_out[...]

    @pl.loop(0, parts)
    def _(part):
        interior(part, SUBSTEPS % 2)

    each(1, members, lambda d: speed_copy(d).wait_recv())

    arrived = [speed_in[s].astype(f32) for s in range(members)]
    for part in range(2):
        pieces = [value[part * own : (part + 1) * own] for value in arrived]
        gathered_speeds[:, part * pairs * points : (part + 1) * pairs * points] = (
            jnp.concatenate(pieces, axis=0).astype(bf16)
        )
    send_pressures(1, gathered_speeds)
    take_pressures(1)

    @pl.loop(SUBSTEPS, last_step)
    def _(step):
        @pl.loop(0, parts)
        def _(part):
            advance(part, step, False)

    @pl.loop(0, parts)
    def _(part):
        advance(part, last_step, True)
        done = 1 - last_step % 2
        for f, state in enumerate((u_now.at[done, part, pl.ds(REACH, columns)], v_now.at[part])):
            high = largest(state[...].reshape(columns * layers, own, half))
            scale_out[part, :, f * (half // 2) : (f + 1) * (half // 2)] = jnp.broadcast_to(
                high * (1.0 / LEVELS), (1, half // 2)
            )
            inverse = LEVELS / high
            for x in range(PAIR):
                for t in range(breadth // 4):
                    given = [state[x * breadth + t * 4 + g] * inverse for g in range(4)]
                    for r, value in enumerate(exchange(given)):
                        final_out[
                            part, r * PAIR + x, f * block : (f + 1) * block, tile_lanes(t)
                        ] = jnp.round(value).astype(i32).astype(i16)
        each(1, members, lambda d: final_copy(part, d).start())
        each(1, members, lambda d: scale_copy(part, d).start())
        final_in[part, me] = final_out[part, me]
        scale_in[part, me] = scale_out[part]

    @pl.loop(0, parts)
    def _(part):
        each(1, members, lambda d: final_copy(part, d).wait_recv())
        each(1, members, lambda d: scale_copy(part, d).wait_recv())
        value = final_in[part].astype(i32).astype(f32)
        for f, result in enumerate((u_out, v_out)):
            scale = scale_in[part, :, :, f * (half // 2) : f * (half // 2) + 1]
            rows = (value[:, f * block : (f + 1) * block] * scale).reshape(width, count)
            high = rows.astype(bf16)
            low = (rows - high.astype(f32)).astype(bf16)
            ordered = [dot(turn[...], piece).astype(bf16) for piece in (high, low)]
            back = dot_turned(eye[...], ordered[0]) + dot_turned(eye[...], ordered[1])
            for j in range(breadth):
                for lanes in range(2):
                    lines = pl.ds(lanes * breadth + j, height, stride=2 * breadth)
                    result[part, lines, :] = back[
                        j * height : (j + 1) * height, lanes * half : (lanes + 1) * half
                    ]

    each(1, members, lambda d: facts_copy(d).wait_send())
    each(1, depth_count, lambda d: places_copy(d).wait_send())
    each(1, members, lambda d: first_copy(d).wait_send())
    each(1, members, lambda d: in_copy(d).wait_send())
    each(1, members, lambda d: speed_copy(d).wait_send())
    for repeat in range(COUPLED):
        parts_taken(repeat, lambda copy: copy.wait_send())

    @pl.loop(0, parts)
    def _(part):
        each(1, members, lambda d: final_copy(part, d).wait_send())
        each(1, members, lambda d: scale_copy(part, d).wait_send())

        @pl.loop(0, last_step + 1)
        def _(step):
            for side in range(2):

                @pl.when(present[side])
                def _():
                    halo_copy(step, part, side, False).wait_send()


def plane_on_device(shape, displacement, velocity, stiffness, wet_position, wet_normal, wet_area, wet_map):
    col_count, row_count, _ = shape
    depth_count = col_count // PAIR
    members = row_count * PAIR
    parts, height, breadth, width = displacement.shape
    half = width // 2
    points = wet_map.shape[0]
    count = height * breadth
    own = LOADS // members
    block = own * (width // LOADS)
    steps = COUPLED * SUBSTEPS
    f32, bf16, i16 = jnp.float32, jnp.bfloat16, jnp.int16
    dma = pltpu.SemaphoreType.DMA

    def separated(state):
        tiled = state.reshape(parts, height, breadth, 2, half).transpose(0, 1, 3, 2, 4)
        return tiled.reshape(parts, height * 2 * breadth, half)

    def joined(state):
        tiled = state.reshape(parts, height, 2, breadth, half).transpose(0, 1, 3, 2, 4)
        return tiled.reshape(parts, height, breadth, width)

    raw = (parts, height * 2 * breadth, half)
    state = jax.ShapeDtypeStruct(raw, f32)
    columns = PAIR * breadth
    anywhere = pl.BlockSpec(memory_space=pl.ANY)
    slab = (members, parts, 2 * block, count)
    final = (parts, members, 2 * block, count)
    u_new, v_new = pl.pallas_call(
        functools.partial(plane_kernel, shape),
        out_shape=(state, state),
        in_specs=[anywhere] * 2 + [whole_spec()] * 5,
        out_specs=(whole_spec(), whole_spec()),
        scratch_shapes=[
            VMEM(raw, f32),
            VMEM(raw, f32),
            VMEM((width + LOADS, width), bf16),
            VMEM((width, width), bf16),
            VMEM((count, count), bf16),
            VMEM((count, count), bf16),
            VMEM(slab, i16),
            VMEM(slab, i16),
            VMEM((16, points), f32),
            VMEM((members, 16, points), f32),
            VMEM((8, points), f32),
            VMEM((depth_count, 8, points), f32),
            VMEM((members, 6, points, half), f32),
            VMEM((LOADS, points), bf16),
            VMEM((members, LOADS, points), bf16),
            VMEM((depth_count, members * points, points), bf16),
            VMEM((COUPLED, depth_count, LOADS, points), f32),
            VMEM((COUPLED, depth_count, members, own, points), f32),
            VMEM((members, own, points), f32),
            VMEM((members, count, points), bf16),
            VMEM((members, points, count), bf16),
            VMEM((2, parts, columns + 2 * REACH, block, half), f32),
            VMEM((parts, columns, block, half), f32),
            VMEM((parts, columns, own, half), f32),
            VMEM((2, parts, columns // 2, 2 * block, 2 * half), bf16),
            VMEM((parts, columns * block, 2 * half), f32),
            VMEM((members, parts * own, count), f32),
            VMEM((columns, 8, half), f32),
            VMEM((LOADS, points), f32),
            VMEM((LOADS, members * points), bf16),
            VMEM((steps, parts, 2, REACH, block, half), bf16),
            VMEM((steps, parts, 2, REACH, block, half), bf16),
            VMEM((2 * own, members // 2 * points), bf16),
            VMEM((members, 2 * own, members // 2 * points), bf16),
            VMEM(final, i16),
            VMEM(final, i16),
            VMEM((parts, 1, half), f32),
            VMEM((parts, members, 1, half), f32),
            dma((2,)),
            dma((members,)),
            dma((members,)),
            dma((depth_count,)),
            dma((depth_count,)),
            dma((members,)),
            dma((members,)),
            dma((members,)),
            dma((members,)),
            dma((COUPLED, depth_count, members)),
            dma((COUPLED, depth_count, members)),
            dma((steps, parts, 2)),
            dma((steps, parts, 2)),
            dma((members,)),
            dma((members,)),
            dma((parts, members)),
            dma((parts, members)),
            dma((parts, members)),
            dma((parts, members)),
        ],
        compiler_params=pltpu.CompilerParams(
            collective_id=0, has_side_effects=True, vmem_limit_bytes=48000000
        ),
        name="plane_steps",
    )(
        pltpu.with_memory_space_constraint(separated(displacement), pltpu.HBM),
        pltpu.with_memory_space_constraint(separated(velocity), pltpu.HBM),
        stiffness.T, wet_position, wet_normal,
        wet_area[None, :], wet_map[None, :],
    )
    return (joined(u_new), joined(v_new))


def by_planes(shape, displacement, wet_map):
    col_count, row_count, _ = shape
    _, height, breadth, width = displacement.shape
    members = row_count * PAIR
    return (
        col_count % PAIR == 0
        and LOADS % members == 0
        and LOADS // members == 8
        and height * breadth == wet_map.shape[0] == width == 256
        and row_count == 4
        and height == 32
    )


def either(shape, *arrays):
    chosen = plane_on_device if by_planes(shape, arrays[0], arrays[-1]) else on_device
    return chosen(shape, *arrays)


def solution(mesh):
    sizes = mesh.shape
    shape = (sizes["tcol"], sizes["group"] * sizes["trow"], sizes["trow"])
    state = P(None, ("group", "trow"), "tcol", None)
    wet = ("group", "trow", "tcol")
    return jax.shard_map(
        functools.partial(either, shape),
        mesh=mesh,
        in_specs=(
            state,
            state,
            P(("group", "trow"), "tcol"),
            P(None, wet),
            P(None, wet),
            P(wet),
            P(wet),
        ),
        out_specs=(state, state),
        check_vma=False,
    )
```

```python
import functools
import math

import jax
import jax.numpy as jnp
from jax import lax
from jax.experimental import pallas as pl
from jax.experimental.pallas import tpu as pltpu
from jax.sharding import PartitionSpec as P

LOADS = 64
SUBSTEPS = 4
COUPLED = 2

SPHERE_AREA = 4.0 * math.pi
SMOOTHING = 0.1
TIME_STEP = 0.3
THICKNESS = 0.5
SPLINE_TAPS = (2.0 / 3.0, -1.0 / 12.0, -1.0 / 12.0, -1.0 / 6.0)
REACH = 3
PAD = 8
MESH = pl.DeviceIdType.MESH
VMEM = pltpu.VMEM


def row_device(index, trow_count):
    return {"group": index // trow_count, "trow": lax.rem(index, trow_count)}


def whole_spec():
    return pl.BlockSpec(memory_space=pltpu.VMEM)


HIGHEST = lax.Precision.HIGHEST


def coupled_kernel(
    shape, u_in, v_in, stiff_ref, position_ref, normal_ref, area_ref, node_ref, u_out, v_out,
    field, speed_now, work, load, col_out, col_in, row_out, row_in,
    geometry, sources, targets, target_cols, normal_cols, pick, spread,
    own_speeds, packed_out, packed_in, unpacked, tiles, partial_out, partial_in,
    halo_send, halo_recv, geo_send, geo_recv, speed_send, speed_recv, part_send, part_recv
):
    col_count, row_count, trow_count = shape
    parts, breadth, height, width = speed_now.shape
    half = width // 2
    points = geometry.shape[1]
    count = breadth * height
    col = lax.axis_index("tcol")
    row = lax.axis_index("group") * trow_count + lax.axis_index("trow")
    present = (col > 0, col < col_count - 1, row > 0, row < row_count - 1)
    peers = (
        {"tcol": jnp.maximum(col - 1, 0)},
        {"tcol": jnp.minimum(col + 1, col_count - 1)},
        row_device(jnp.maximum(row - 1, 0), trow_count),
        row_device(jnp.minimum(row + 1, row_count - 1), trow_count),
    )
    middle = pl.ds(PAD, height)

    def col_peer(d):
        return {"tcol": lax.rem(col + d, col_count)}

    def row_peer(d):
        return row_device(lax.rem(row + d, row_count), trow_count)

    barrier = pltpu.get_barrier_semaphore()

    @pl.loop(1, col_count)
    def _(d):
        pl.semaphore_signal(barrier, inc=1, device_id=col_peer(d), device_id_type=MESH)

    @pl.loop(1, row_count)
    def _(d):
        pl.semaphore_signal(barrier, inc=1, device_id=row_peer(d), device_id_type=MESH)

    geometry[0:3, :] = position_ref[...]
    geometry[3:6, :] = normal_ref[...] * (area_ref[...] * (1.0 / SPHERE_AREA))
    geometry[6:8, :] = jnp.zeros((2, points), jnp.float32)
    pl.semaphore_wait(barrier, col_count + row_count - 2)

    def geo_copy(kind, d):
        return pltpu.make_async_remote_copy(
            src_ref=geometry,
            dst_ref=sources.at[col] if kind == 0 else targets.at[row],
            send_sem=geo_send.at[kind, d],
            recv_sem=geo_recv.at[kind, d],
            device_id=col_peer(d) if kind == 0 else row_peer(d),
            device_id_type=MESH,
        )

    def speed_copy(repeat, d):
        return pltpu.make_async_remote_copy(
            src_ref=packed_out.at[repeat],
            dst_ref=packed_in.at[repeat, col],
            send_sem=speed_send.at[repeat, d],
            recv_sem=speed_recv.at[repeat, d],
            device_id=col_peer(d),
            device_id_type=MESH,
        )

    def part_copy(repeat, d):
        return pltpu.make_async_remote_copy(
            src_ref=partial_out.at[repeat, lax.rem(row + d, row_count)],
            dst_ref=partial_in.at[repeat, d],
            send_sem=part_send.at[repeat, d],
            recv_sem=part_recv.at[repeat, d],
            device_id=row_peer(d),
            device_id_type=MESH,
        )

    for kind, total in ((1, row_count), (0, col_count)):

        @pl.loop(1, total)
        def _(d):
            geo_copy(kind, d).start()

    sources[col] = geometry[...]
    targets[row] = geometry[...]

    field[...] = jnp.zeros_like(field)
    for part in range(parts):
        for j in range(breadth):
            for lanes in range(2):
                lines = pl.ds(lanes * breadth + j, height, stride=2 * breadth)
                cut = pl.ds(lanes * half, half)
                field[part, REACH + j, middle, cut] = u_in[part, lines, :]
                speed_now[part, j, :, cut] = v_in[part, lines, :]
    for side in range(2):

        @pl.when(jnp.logical_not(present[side]))
        def _():
            col_in[:, :, side] = jnp.zeros(col_in.shape[:2] + col_in.shape[3:], col_in.dtype)

    def as_column(line):
        return jnp.broadcast_to(line, (half, line.shape[1])).T

    for part in range(parts):
        normal_cols[part] = as_column(normal_ref[part : part + 1, :])
    spread[...] = (
        lax.broadcasted_iota(jnp.int32, (count, points), 0) == node_ref[...]
    ).astype(jnp.float32)
    pick[...] = spread[...].T

    def halo_copy(step, side, part, arriving):
        out_buffer, in_buffer = (col_out, col_in) if side < 2 else (row_out, row_in)
        own = side % 2
        other = own if arriving else 1 - own
        return pltpu.make_async_remote_copy(
            src_ref=out_buffer.at[step, part, own],
            dst_ref=in_buffer.at[step, part, other],
            send_sem=halo_send.at[step, part, side],
            recv_sem=halo_recv.at[step, part, (side // 2) * 2 + other],
            device_id=peers[side],
            device_id_type=MESH,
        )

    lane = lax.broadcasted_iota(jnp.int32, (height, half), 1)
    low = lane < half // 2
    low_half = lax.broadcasted_iota(jnp.int32, (points // 2, half), 1) < half // 2

    def pack(value):
        turned = pltpu.roll(value[points // 2 :], half // 2, 1)
        return jnp.where(low_half, turned, value[: points // 2])

    def tile(r):
        group = 32

        def block(index, carry):
            source = index // (points // half)
            lanes = pl.ds(pl.multiple_of(lax.rem(index, points // half) * half, half), half)
            line = [sources[source, k : k + 1, lanes] for k in range(6)]

            def rows_of(g, inner):
                rows = pl.ds(pl.multiple_of(g * group, group), group)
                dx = target_cols[r, 0, rows, :] - line[0]
                dy = target_cols[r, 1, rows, :] - line[1]
                dz = target_cols[r, 2, rows, :] - line[2]
                numerator = line[3] * dx + line[4] * dy + line[5] * dz
                squared = dx * dx + dy * dy + dz * dz + SMOOTHING * SMOOTHING
                inverse = lax.rsqrt(squared)
                value = numerator * inverse * (inverse * inverse)
                tiles[r, source, rows, lanes] = value.astype(jnp.bfloat16)
                return inner

            return lax.fori_loop(0, points // group, rows_of, carry, unroll=2)

        lax.fori_loop(0, col_count * (points // half), block, 0)

    def send_halos(step, part):
        for side, first in ((0, REACH), (1, breadth)):

            @pl.when(present[side])
            def _():
                for j in range(REACH):
                    col_out[step, part, side, j] = field[part, first + j, middle, :].astype(
                        col_out.dtype
                    )
                halo_copy(step, side, part, False).start()

        for side, first in ((2, PAD), (3, PAD + height - REACH)):

            @pl.when(present[side])
            def _():
                for j in range(breadth):
                    row_out[
                        step, part, side - 2, j // 2, (j % 2) * 4 : (j % 2) * 4 + REACH, :
                    ] = field[part, REACH + j, first : first + REACH, :]
                halo_copy(step, side, part, False).start()

    def local(part):
        def body(column, carry):
            a = field[part, REACH + column, middle, 0:half]
            b = field[part, REACH + column, middle, half:width]
            turned_a = pltpu.roll(a, half // 2, 1)
            turned_b = pltpu.roll(b, half // 2, 1)
            between = jnp.where(low, turned_a, turned_b)
            edge_a = jnp.where(low, a, turned_a)
            edge_b = jnp.where(low, turned_b, b)
            stiff = stiff_ref[column]
            for lanes, here, edge in ((0, a, edge_a), (1, b, edge_b)):
                cut = pl.ds(lanes * half, half)
                summed = (2.0 * SPLINE_TAPS[0]) * here
                for offset in range(1, REACH + 1):
                    summed = summed + SPLINE_TAPS[offset] * (
                        field[part, REACH + column + offset, middle, cut]
                        + field[part, REACH + column - offset, middle, cut]
                    )
                value = -(stiff * summed) - THICKNESS * (2.0 * here - between - edge)
                if lanes == 1:
                    value = value + load[part, column]
                work[part, column, :, cut] = speed_now[part, column, :, cut] + TIME_STEP * value
            return carry

        lax.fori_loop(0, breadth, body, 0)

    def complete(step, part):
        for side, first in ((2, PAD - REACH), (3, PAD + height)):

            @pl.when(present[side])
            def _():
                halo_copy(step, side, part, True).wait_recv()
                for j in range(breadth):
                    field[part, REACH + j, first : first + REACH, :] = row_in[
                        step, part, side - 2, j // 2, (j % 2) * 4 : (j % 2) * 4 + REACH, :
                    ]

        def along_rows(column, carry):
            stiff = stiff_ref[column] * (-TIME_STEP)
            for lanes in range(2):
                cut = pl.ds(lanes * half, half)
                summed = 0.0
                for offset in range(1, REACH + 1):
                    summed = summed + SPLINE_TAPS[offset] * (
                        field[part, REACH + column, pl.ds(PAD + offset, height), cut]
                        + field[part, REACH + column, pl.ds(PAD - offset, height), cut]
                    )
                work[part, column, :, cut] += stiff * summed
            return carry

        lax.fori_loop(0, breadth, along_rows, 0)

        for side in range(2):

            @pl.when(present[side])
            def _():
                halo_copy(step, side, part, True).wait_recv()

        for column in range(breadth):
            stiff = stiff_ref[column] * (-TIME_STEP)
            for lanes in range(2):
                cut = pl.ds(lanes * half, half)
                value = work[part, column, :, cut]
                summed = None
                for offset in range(1, REACH + 1):
                    for side, j in ((0, column - offset + REACH), (1, column + offset - breadth)):
                        inside = (column - offset < 0) if side == 0 else (column + offset >= breadth)
                        if inside:
                            term = SPLINE_TAPS[offset] * col_in[
                                step, part, side, j, :, cut
                            ].astype(jnp.float32)
                            summed = term if summed is None else summed + term
                if summed is not None:
                    value = value + stiff * summed
                speed_now[part, column, :, cut] = value
                field[part, REACH + column, middle, cut] += TIME_STEP * value

    for repeat in range(COUPLED):
        speeds = jnp.zeros((points, half), jnp.float32)
        for part in range(parts):
            outer = speed_now[part, :, :, half:width].reshape(count, half)
            picked = jnp.dot(
                pick[...], outer, precision=HIGHEST, preferred_element_type=jnp.float32
            )
            speeds = speeds + normal_cols[part] * picked
        own_speeds[...] = speeds
        packed_out[repeat] = pack(speeds).astype(packed_out.dtype)

        @pl.loop(1, col_count)
        def _(d):
            speed_copy(repeat, d).start()

        packed_in[repeat, col] = packed_out[repeat]

        if repeat == 0:

            @pl.loop(1, row_count)
            def _(d):
                geo_copy(1, d).wait_recv()

            @pl.loop(1, col_count)
            def _(d):
                geo_copy(0, d).wait_recv()

            @pl.loop(0, row_count)
            def _(r):
                for k in range(3):
                    target_cols[r, k] = as_column(targets[r, k : k + 1, :])

            tile(lax.rem(row + 1, row_count))

        @pl.loop(1, col_count)
        def _(d):
            speed_copy(repeat, d).wait_recv()

        @pl.loop(0, parts)
        def _(part):
            send_halos(repeat * SUBSTEPS, part)

        @pl.loop(0, col_count)
        def _(c):
            value = packed_in[repeat, c].astype(jnp.float32)
            unpacked[c, 0 : points // 2, :] = value.astype(jnp.bfloat16)
            unpacked[c, points // 2 : points, :] = pltpu.roll(value, half // 2, 1).astype(
                jnp.bfloat16
            )

        @pl.loop(1, row_count + 1)
        def _(d):
            r = lax.rem(row + d, row_count)
            total = jnp.zeros((points, half), jnp.float32)
            for c in range(col_count):
                total = total + jnp.dot(
                    tiles[r, c], unpacked[c], preferred_element_type=jnp.float32
                )
            partial_out[repeat, r] = pack(total)

            @pl.when(d < row_count)
            def _():
                part_copy(repeat, d).start()
                if repeat == 0:
                    tile(lax.rem(r + 1, row_count))

        received = partial_out[repeat, row]
        for d in range(1, row_count):
            part_copy(repeat, d).wait_recv()
            received = received + partial_in[repeat, d]
        low_points = jnp.concatenate([low_half, low_half], axis=0)
        both = jnp.concatenate([received, pltpu.roll(received, half // 2, 1)], axis=0)
        pressure = jnp.where(low_points, 0.0, 0.5 * own_speeds[...] + both)
        for part in range(parts):
            loading = jnp.dot(
                spread[...], -(normal_cols[part] * pressure),
                precision=HIGHEST, preferred_element_type=jnp.float32,
            )
            load[part] = loading.reshape(breadth, height, half)

            local(part)

        last = (repeat + 1) * SUBSTEPS - 1

        @pl.loop(repeat * SUBSTEPS, last + 1)
        def _(step):
            @pl.loop(0, parts)
            def _(part):
                complete(step, part)

                @pl.when(step < last)
                def _():
                    send_halos(step + 1, part)
                    local(part)

    for part in range(parts):
        for j in range(breadth):
            for lanes in range(2):
                lines = pl.ds(lanes * breadth + j, height, stride=2 * breadth)
                cut = pl.ds(lanes * half, half)
                u_out[part, lines, :] = field[part, REACH + j, middle, cut]
                v_out[part, lines, :] = speed_now[part, j, :, cut]

    @pl.loop(0, COUPLED * SUBSTEPS)
    def _(step):
        for side in range(4):

            @pl.when(present[side])
            def _():
                for part in range(parts):
                    halo_copy(step, side, part, False).wait_send()

    @pl.loop(1, col_count)
    def _(d):
        geo_copy(0, d).wait_send()
        for repeat in range(COUPLED):
            speed_copy(repeat, d).wait_send()

    @pl.loop(1, row_count)
    def _(d):
        geo_copy(1, d).wait_send()
        for repeat in range(COUPLED):
            part_copy(repeat, d).wait_send()


def on_device(shape, displacement, velocity, stiffness, wet_position, wet_normal, wet_area, wet_map):
    col_count, row_count, _ = shape
    parts, height, breadth, width = displacement.shape
    half = width // 2
    points = wet_map.shape[0]
    steps = COUPLED * SUBSTEPS
    stiff = jnp.broadcast_to(stiffness.T[:, :, None], (breadth, height, half))
    node = (wet_map % breadth) * height + wet_map // breadth

    def split(state):
        tiled = state.reshape(parts, height, breadth, 2, half).transpose(0, 1, 3, 2, 4)
        return tiled.reshape(parts, height * 2 * breadth, half)

    def joined(state):
        tiled = state.reshape(parts, height, 2, breadth, half).transpose(0, 1, 3, 2, 4)
        return tiled.reshape(parts, height, breadth, width)

    state = jax.ShapeDtypeStruct((parts, height * 2 * breadth, half), jnp.float32)
    cols = (steps, parts, 2, REACH, height, width)
    rows = (steps, parts, 2, breadth // 2, 8, width)
    f32, bf16 = jnp.float32, jnp.bfloat16
    dma = pltpu.SemaphoreType.DMA
    u_new, v_new = pl.pallas_call(
        functools.partial(coupled_kernel, shape),
        out_shape=(state, state),
        in_specs=[whole_spec()] * 7,
        out_specs=(whole_spec(), whole_spec()),
        scratch_shapes=[
            VMEM((parts, breadth + 2 * REACH, height + 2 * PAD, width), f32),
            VMEM((parts, breadth, height, width), f32),
            VMEM((parts, breadth, height, width), f32),
            VMEM((parts, breadth, height, half), f32),
            VMEM(cols, bf16),
            VMEM(cols, bf16),
            VMEM(rows, f32),
            VMEM(rows, f32),
            VMEM((8, points), f32),
            VMEM((col_count, 8, points), f32),
            VMEM((row_count, 8, points), f32),
            VMEM((row_count, 3, points, half), f32),
            VMEM((parts, points, half), f32),
            VMEM((points, height * breadth), f32),
            VMEM((height * breadth, points), f32),
            VMEM((points, half), f32),
            VMEM((COUPLED, points // 2, half), bf16),
            VMEM((COUPLED, col_count, points // 2, half), bf16),
            VMEM((col_count, points, half), bf16),
            VMEM((row_count, col_count, points, points), bf16),
            VMEM((COUPLED, row_count, points // 2, half), f32),
            VMEM((COUPLED, row_count, points // 2, half), f32),
            dma((steps, parts, 4)),
            dma((steps, parts, 4)),
            dma((2, max(col_count, row_count))),
            dma((2, max(col_count, row_count))),
            dma((COUPLED, col_count)),
            dma((COUPLED, col_count)),
            dma((COUPLED, row_count)),
            dma((COUPLED, row_count)),
        ],
        compiler_params=pltpu.CompilerParams(
            collective_id=0, has_side_effects=True, vmem_limit_bytes=67043328
        ),
        name="coupled_steps",
    )(
        split(displacement), split(velocity), stiff,
        wet_position, wet_normal, wet_area[None, :], node[None, :],
    )
    return (joined(u_new), joined(v_new))


PAIR = 2
LEVELS = 32767.0


def plane_kernel(
    shape, u_hbm, v_hbm, stiff_ref, position_ref, normal_ref, area_ref, map_ref, u_out, v_out,
    u_raw, v_raw, perm, eye, stencil, in_out, in_in, facts_out, facts, places, targets,
    source_cols, first_out, first_in, tiles, part_out, part_in, far_out, far_in, spoken,
    onehot, onehot_back, u_now, v_now, load, halves, summed, patched, stiff_now, own_speed,
    gathered_speeds, halo_out, halo_in, speed_out, speed_in, final_out, final_in, scale_out, scale_in,
    load_sem, facts_send, facts_recv, places_send, places_recv, first_send, first_recv,
    in_send, in_recv, part_send, part_recv, halo_send, halo_recv, speed_send, speed_recv,
    final_send, final_recv, scale_send, scale_recv,
):
    col_count, row_count, trow_count = shape
    depth_count = col_count // PAIR
    members = row_count * PAIR
    total = members * depth_count
    parts, _, half = u_raw.shape
    count, points = onehot.shape[1:]
    breadth, height = stiff_ref.shape
    width = perm.shape[1]
    own = LOADS // members
    layers = width // LOADS
    block = own * layers
    columns = PAIR * breadth
    last_step = COUPLED * SUBSTEPS - 1
    f32, bf16, i16, i32 = jnp.float32, jnp.bfloat16, jnp.int16, jnp.int32
    col = lax.axis_index("tcol")
    row = lax.axis_index("group") * trow_count + lax.axis_index("trow")
    z = col // PAIR
    me = row * PAIR + lax.rem(col, PAIR)

    def device(depth, member):
        return dict(
            row_device(member // PAIR, trow_count), tcol=depth * PAIR + lax.rem(member, PAIR)
        )

    def member_of(d):
        return lax.rem(me + d, members)

    def depth_of(d):
        return lax.rem(z + d, depth_count)

    def each(first, last, action):
        @pl.loop(first, last)
        def _(d):
            action(d)

    barrier = pltpu.get_barrier_semaphore()

    @pl.loop(1, total)
    def _(d):
        to = device(depth_of(d // members), member_of(lax.rem(d, members)))
        pl.semaphore_signal(barrier, inc=1, device_id=to, device_id_type=MESH)

    v_load = pltpu.make_async_copy(v_hbm, v_raw, load_sem.at[0])
    u_load = pltpu.make_async_copy(u_hbm, u_raw, load_sem.at[1])
    v_load.start()
    u_load.start()

    def iota(size, axis):
        return lax.broadcasted_iota(i32, size, axis)

    def ones_where(mask):
        return jnp.where(mask, 1.0, 0.0).astype(bf16)

    def dot(a, b):
        return jnp.dot(a, b, preferred_element_type=f32)

    def dot_turned(a, b):
        return lax.dot_general(a, b, (((1,), (1,)), ((), ())), preferred_element_type=f32)

    def lane_of(line):
        member, inner = line // block, line % block
        return (inner // own) * LOADS + member * own + inner % own

    square = (width, width)
    line, column = iota(square, 0), iota(square, 1)
    perm[0:width, :] = ones_where(lane_of(line) == column)
    outer = (LOADS, width)
    perm[width : width + LOADS, :] = ones_where(
        (layers - 1) * LOADS + iota(outer, 0) == iota(outer, 1)
    )
    eye[...] = ones_where(iota((count, count), 0) == iota((count, count), 1))

    src, dst = iota((count, count), 0), iota((count, count), 1)
    distance = jnp.abs(src - dst)
    taps = jnp.where(distance == 3, -2.0, jnp.where(distance < 3, -1.0, 0.0))
    taps = jnp.where(distance == 0, 16.0, taps)
    stencil[...] = jnp.where(src // half == dst // half, taps, 0.0).astype(bf16)

    spread = ones_where(iota((height, count), 0) == iota((height, count), 1) % height).astype(f32)
    wide = jnp.dot(stiff_ref[...], spread, precision=HIGHEST, preferred_element_type=f32)
    own_b = iota((breadth, count), 0) == iota((breadth, count), 1) // height
    places[0:3, :] = position_ref[...]
    places[3:8, :] = jnp.zeros((5, points), f32)
    facts_out[0:3, :] = position_ref[...]
    facts_out[3:6, :] = normal_ref[...] * (area_ref[...] * (1.0 / SPHERE_AREA))
    facts_out[6:9, :] = normal_ref[...]
    numbers = map_ref[...]
    facts_out[9:10, :] = ((numbers % breadth) * height + numbers // breadth).astype(f32)
    facts_out[10:11, :] = jnp.sum(jnp.where(own_b, wide, 0.0), axis=0, keepdims=True)
    facts_out[13:16, :] = jnp.zeros((3, points), f32)
    targets[z] = places[...]

    present = (z > 0, z < depth_count - 1)
    for side, first in ((0, 0), (1, columns + REACH)):

        @pl.when(jnp.logical_not(present[side]))
        def _():
            u_now[:, :, first : first + REACH] = jnp.zeros((2, parts, REACH, block, half), f32)

    def plane_copy(d, source, target, send, recv):
        return pltpu.make_async_remote_copy(
            src_ref=source, dst_ref=target.at[me], send_sem=send.at[d], recv_sem=recv.at[d],
            device_id=device(z, member_of(d)), device_id_type=MESH,
        )

    def facts_copy(d):
        return plane_copy(d, facts_out, facts, facts_send, facts_recv)

    def places_copy(d):
        return pltpu.make_async_remote_copy(
            src_ref=places, dst_ref=targets.at[z],
            send_sem=places_send.at[d], recv_sem=places_recv.at[d],
            device_id=device(depth_of(d), me), device_id_type=MESH,
        )

    def first_copy(d):
        return plane_copy(d, first_out, first_in, first_send, first_recv)

    def in_copy(d):
        return plane_copy(d, in_out.at[member_of(d)], in_in, in_send, in_recv)

    def speed_copy(d):
        return plane_copy(d, speed_out, speed_in, speed_send, speed_recv)

    def final_copy(part, f, d):
        return plane_copy(
            d, final_out.at[part, f, member_of(d)], final_in.at[part, f],
            final_send.at[part, f], final_recv.at[part, f],
        )

    def scale_copy(part, d):
        return plane_copy(
            d, scale_out.at[part], scale_in.at[part], scale_send.at[part], scale_recv.at[part]
        )

    def side_of(depth):
        return depth // (depth_count // 2)

    def part_copy(repeat, dz, dj, far):
        lines = pl.ds(pl.multiple_of(member_of(dj) * own, own), own)
        if far:
            source, target = far_out.at[repeat, depth_of(dz), member_of(dj)], far_in
        else:
            source, target = part_out.at[repeat, depth_of(dz), lines, :], part_in
        return pltpu.make_async_remote_copy(
            src_ref=source, dst_ref=target.at[repeat, z, me],
            send_sem=part_send.at[repeat, dz, dj], recv_sem=part_recv.at[repeat, dz, dj],
            device_id=device(depth_of(dz), member_of(dj)), device_id_type=MESH,
        )

    def near_or_far(depth, action):
        near = side_of(depth) == side_of(z)

        @pl.when(near)
        def _():
            action(False)

        @pl.when(jnp.logical_not(near))
        def _():
            action(True)

    def halo_copy(step, part, side, arriving):
        there = side if arriving else 1 - side
        step_z = jnp.maximum(z - 1, 0) if side == 0 else jnp.minimum(z + 1, depth_count - 1)
        return pltpu.make_async_remote_copy(
            src_ref=halo_out.at[step, part, side],
            dst_ref=halo_in.at[step, part, there],
            send_sem=halo_send.at[step, part, side], recv_sem=halo_recv.at[step, part, there],
            device_id=device(step_z, me), device_id_type=MESH,
        )

    def as_column(value):
        return jnp.broadcast_to(value, (half, value.shape[1])).T

    bunch = iota((8, half), 1) // height
    upper_half, odd = bunch >= 2, bunch % 2 == 1

    def exchange(values):
        rows = values[0].shape[0]

        def choose(mask, a, b):
            shape3 = (rows // 8, 8, half)
            return jnp.where(mask, b.reshape(shape3), a.reshape(shape3)).reshape(rows, half)

        def rolled(value, bunches):
            return pltpu.roll(value, bunches * height, 1)

        lows = [choose(upper_half, values[i], rolled(values[i + 2], 2)) for i in range(2)]
        highs = [choose(upper_half, rolled(values[i], 2), values[i + 2]) for i in range(2)]
        result = []
        for first, second in (lows, highs):
            result.append(choose(odd, first, rolled(second, 1)))
            result.append(choose(odd, rolled(first, 3), second))
        return result

    def tile_lanes(t):
        return slice(t * half, (t + 1) * half)

    def one_hot(s):
        onehot[s] = ones_where(iota((count, points), 0).astype(f32) == facts[s, 9:10, :])

    def one_hot_back(s):
        nodes = as_column(facts[s, 9:10, :])
        for lanes in range(2):
            numbers = (iota((points, half), 1) + lanes * half).astype(f32)
            onehot_back[s, :, lanes * half : (lanes + 1) * half] = ones_where(numbers == nodes)

    facts[me] = facts_out[...]
    one_hot(me)

    def largest(value):
        reduced = jnp.max(jnp.abs(value), axis=0)
        top = jnp.max(jnp.max(reduced, axis=1, keepdims=True), axis=0, keepdims=True)
        return jnp.maximum(top, 1e-30)

    def split(value):
        high = value.astype(bf16).astype(f32)
        return jnp.concatenate([high, value - high], axis=-2).astype(bf16)

    def turned(raw, part, inverse, lines):
        rows = []
        for j in range(breadth):
            picks = [
                raw[part, pl.ds(lanes * breadth + j, height, stride=2 * breadth), :]
                for lanes in range(2)
            ]
            rows.append(jnp.concatenate(picks, axis=1))
        value = jnp.round(jnp.concatenate(rows, axis=0) * inverse)
        high = jnp.round(value * (1.0 / 256.0))
        low = value - 256.0 * high
        return (
            dot_turned(perm[0:lines, :], high.astype(bf16)),
            dot_turned(perm[0:lines, :], low.astype(bf16)),
        )

    def top_of(raw):
        return largest(raw[...].reshape(raw.shape[0] * raw.shape[1] // 8, 8, half))

    v_load.wait()
    v_top = top_of(v_raw)
    v_scale, v_inverse = v_top * (1.0 / LEVELS), LEVELS / v_top
    facts_out[12:13, :] = jnp.broadcast_to(v_scale, (1, points))
    picked_all = jnp.zeros((LOADS, points), f32)
    for part in range(parts):
        high, low = turned(v_raw, part, v_inverse, width + LOADS)
        whole = high[0:width] * 256.0 + low[0:width]
        in_out[:, part, block : 2 * block, :] = (
            whole.reshape(members, block, count).astype(i32).astype(i16)
        )
        rows = jnp.concatenate([high[width:], low[width:]], axis=0).astype(bf16)
        both = dot(rows, onehot[me])
        picked = both[0:LOADS] * 256.0 + both[LOADS:]
        picked_all = picked_all + picked * (normal_ref[part : part + 1, :] * v_scale)
    own_speed[...] = picked_all
    first_out[...] = picked_all.astype(bf16)
    first_in[me] = first_out[...]

    u_load.wait()
    u_top = top_of(u_raw)
    u_scale, u_inverse = u_top * (1.0 / LEVELS), LEVELS / u_top
    facts_out[11:12, :] = jnp.broadcast_to(u_scale, (1, points))
    facts[me] = facts_out[...]
    for part in range(parts):
        high, low = turned(u_raw, part, u_inverse, width)
        whole = high * 256.0 + low
        in_out[:, part, 0:block, :] = whole.reshape(members, block, count).astype(i32).astype(i16)
    in_in[me] = in_out[me]

    pl.semaphore_wait(barrier, total - 1)
    each(1, members, lambda d: facts_copy(d).start())
    each(1, depth_count, lambda d: places_copy(d).start())
    each(1, members, lambda d: first_copy(d).start())
    each(1, members, lambda d: in_copy(d).start())

    each(1, members, lambda d: facts_copy(d).wait_recv())

    @pl.loop(0, members, unroll=4)
    def _(s):
        for k in range(6):
            source_cols[s, k] = as_column(facts[s, k : k + 1, :])

    group = 64

    def tile(depth):
        known = [
            [targets[depth, k : k + 1, lanes * half : (lanes + 1) * half] for k in range(3)]
            for lanes in range(2)
        ]

        def blocks(source, carry):
            def rows_of(g, inner):
                start = pl.multiple_of(g * group, group)
                rows = pl.ds(start, group)
                place_x, place_y, place_z, normal_x, normal_y, normal_z = [
                    source_cols[source, k, rows, :] for k in range(6)
                ]
                deep = pl.ds(pl.multiple_of(source * points + start, group), group)
                for lanes in range(2):
                    dx = known[lanes][0] - place_x
                    dy = known[lanes][1] - place_y
                    dz = known[lanes][2] - place_z
                    numerator = normal_x * dx + normal_y * dy + normal_z * dz
                    squared = dx * dx + dy * dy + dz * dz + SMOOTHING * SMOOTHING
                    inverse = lax.rsqrt(squared)
                    value = numerator * inverse * (inverse * inverse)
                    tiles[depth, deep, tile_lanes(lanes)] = value.astype(bf16)
                return inner

            return lax.fori_loop(0, points // group, rows_of, carry, unroll=2)

        lax.fori_loop(0, members, blocks, 0)

    def send_pressures(repeat, speeds):
        @pl.loop(1, depth_count + 1)
        def _(d):
            depth = depth_of(d)
            if repeat == 0:

                @pl.when(d < depth_count)
                def _():
                    places_copy(depth_count - d).wait_recv()

                tile(depth)

                @pl.when(d == 1)
                def _():
                    each(1, members, lambda d: first_copy(d).wait_recv())
                    for s in range(members):
                        speeds[:, s * points : (s + 1) * points] = first_in[s]

            value = dot(speeds[...], tiles[depth])
            if repeat == 0:
                value = value + jnp.where(depth == z, 0.5, 0.0) * own_speed[...]
            def pass_on(far):
                if far:
                    sides = [value[:, tile_lanes(t)].reshape(members, own, half) for t in range(2)]
                    far_out[repeat, depth] = jnp.concatenate(sides, axis=1).astype(bf16)
                else:
                    part_out[repeat, depth] = value

                @pl.when(d < depth_count)
                def _():
                    each(0, members, lambda dj: part_copy(repeat, d, dj, far).start())

            near_or_far(depth, pass_on)

            @pl.when(d == depth_count)
            def _():
                each(1, members, lambda dj: part_copy(repeat, 0, dj, False).start())

        part_in[repeat, z, me] = part_out[
            repeat, z, pl.ds(pl.multiple_of(me * own, own), own), :
        ]

    def parts_arrived(repeat):
        each(1, members, lambda dj: part_copy(repeat, 0, dj, False).wait_recv())

        @pl.loop(1, depth_count)
        def _(d):
            near_or_far(
                lax.rem(z + depth_count - d, depth_count),
                lambda far: each(
                    0, members, lambda dj: part_copy(repeat, d, dj, far).wait_recv()
                ),
            )

    def parts_sent(repeat):
        each(1, members, lambda dj: part_copy(repeat, 0, dj, False).wait_send())

        @pl.loop(1, depth_count)
        def _(d):
            near_or_far(
                depth_of(d),
                lambda far: each(
                    0, members, lambda dj: part_copy(repeat, d, dj, far).wait_send()
                ),
            )

    def interior(part, now):
        lines = halves[now, part].reshape(columns // 2 * 2 * block, 2 * half)
        summed[part] = dot(lines, stencil[...])

    def send_halos(step, part):
        for side in range(2):

            @pl.when(present[side])
            def _():
                halo_copy(step, part, side, False).start()

    def place(step, part, later, pair, j, value):
        c = pair * 2 + j
        u_now[later, part, REACH + c] = value
        high = value.astype(bf16)
        halves[later, part, pair, 0:block, tile_lanes(j)] = high
        halves[later, part, pair, block : 2 * block, tile_lanes(j)] = (
            value - high.astype(f32)
        ).astype(bf16)
        if isinstance(c, int):
            for side, first in ((0, 0), (1, columns - REACH)):
                if first <= c < first + REACH:
                    halo_out[step, part, side, c - first] = high

    send_pressures(0, gathered_speeds)

    @pl.loop(0, members, unroll=2)
    def _(s):
        one_hot(s)
        one_hot_back(s)

    for x in range(PAIR):
        for t in range(breadth // 4):
            given = [
                jnp.broadcast_to(facts[r * PAIR + x, 10:11, tile_lanes(t)], (8, half))
                for r in range(row_count)
            ]
            for g, value in enumerate(exchange(given)):
                stiff_now[x * breadth + t * 4 + g] = value * (-TIME_STEP / 12.0)

    each(1, members, lambda d: in_copy(d).wait_recv())

    @pl.loop(0, parts)
    def _(part):
        for x in range(PAIR):
            for t in range(breadth // 4):
                given = []
                for r in range(row_count):
                    value = in_in[r * PAIR + x, part, :, tile_lanes(t)].astype(i32).astype(f32)
                    scales = facts[r * PAIR + x, 11:13, tile_lanes(t)]
                    given.append(jnp.concatenate(
                        [value[0:block] * scales[0:1], value[block:] * scales[1:2]], axis=0
                    ))
                for g, value in enumerate(exchange(given)):
                    c = x * breadth + t * 4 + g
                    v_now[part, c] = value[block:]
                    place(0, part, 0, c // 2, c % 2, value[0:block])
        send_halos(0, part)
        interior(part, 0)

    def take_pressures(repeat):
        parts_arrived(repeat)
        near_first = side_of(z) * (depth_count // 2)
        far_first = depth_count // 2 - near_first

        @pl.loop(0, members, unroll=8)
        def _(s):
            value = part_in[repeat, near_first, s]
            for d in range(1, depth_count // 2):
                value = value + part_in[repeat, near_first + d, s]
            rest = far_in[repeat, far_first, s].astype(f32)
            for d in range(1, depth_count // 2):
                rest = rest + far_in[repeat, far_first + d, s].astype(f32)
            value = value + jnp.concatenate([rest[0:own], rest[own : 2 * own]], axis=1)
            if repeat > 0:
                value = value + 0.5 * spoken[s]
            pieces = [
                split(value * (facts[s, 6 + k : 7 + k, :] * (-TIME_STEP))) for k in range(parts)
            ]
            both = dot(jnp.concatenate(pieces, axis=0), onehot_back[s])
            patched[s] = jnp.concatenate(
                [
                    both[16 * k : 16 * k + 8] + both[16 * k + 8 : 16 * k + 16]
                    for k in range(parts)
                ], axis=0
            )

        for x in range(PAIR):
            for t in range(breadth // 4):
                given = [patched[r * PAIR + x, :, tile_lanes(t)] for r in range(row_count)]
                for g, value in enumerate(exchange(given)):
                    for k in range(parts):
                        load[k, x * breadth + t * 4 + g] = value[own * k : own * (k + 1)]

    def advance(part, step, final, later_interior=False):
        now = lax.rem(step, 2)
        later = 1 - now
        for side, first in ((0, 0), (1, columns + REACH)):

            @pl.when(present[side])
            def _():
                halo_copy(step, part, side, True).wait_recv()
                u_now[now, part, first : first + REACH] = halo_in[step, part, side].astype(f32)

        def update(pair, start):
            for j in range(2):
                c = pair * 2 + j
                both = summed[part, pl.ds(start, 2 * block), tile_lanes(j)]
                plane = both[0:block] + both[block : 2 * block]

                def near(offset):
                    return u_now[now, part, REACH + c + offset]

                beside = (near(-1) + near(1)) + (near(-2) + near(2))
                beside = beside + 2.0 * (near(-3) + near(3))
                plane = (plane - beside).reshape(layers, own, half)
                u_old = near(0).reshape(layers, own, half)
                under = jnp.concatenate([u_old[0:1], u_old[: layers - 1]], axis=0)
                above = jnp.concatenate([u_old[1:], u_old[layers - 1 :]], axis=0)
                v_new = (
                    v_now[part, c].reshape(layers, own, half)
                    + stiff_now[c] * plane
                    - (TIME_STEP * THICKNESS) * (2.0 * u_old - under - above)
                )
                v_new = jnp.concatenate(
                    [v_new[: layers - 1], v_new[layers - 1 :] + load[part, c]], axis=0
                )
                u_new = (u_old + TIME_STEP * v_new).reshape(block, half)
                v_now[part, c] = v_new.reshape(block, half)
                if final:
                    u_now[later, part, REACH + c] = u_new
                else:
                    place(step + 1, part, later, pair, j, u_new)

        edge = (REACH + 1) // 2
        for pair in list(range(edge)) + list(range(columns // 2 - edge, columns // 2)):
            update(pair, pair * 2 * block)
        if not final:
            send_halos(step + 1, part)

        @pl.loop(edge, columns // 2 - edge, unroll=4)
        def _(pair):
            update(pair, pl.multiple_of(pair * 2 * block, 2 * block))

        if not final and not later_interior:
            interior(part, later)

    take_pressures(0)

    @pl.loop(0, SUBSTEPS - 1)
    def _(step):
        @pl.loop(0, parts, unroll=parts)
        def _(part):
            advance(part, step, False)

    @pl.loop(0, parts)
    def _(part):
        advance(part, SUBSTEPS - 1, False, True)

    for x in range(PAIR):
        for t in range(breadth // 4):
            given = []
            for g in range(4):
                c = x * breadth + t * 4 + g
                given.append(jnp.concatenate(
                    [v_now[k, c, block - own : block] for k in range(parts)], axis=0
                ))
            for r, value in enumerate(exchange(given)):
                patched[r * PAIR + x, :, tile_lanes(t)] = value

    spoken_rows = []
    for s in range(members):
        pieces = [split(patched[s, own * k : own * (k + 1)]) for k in range(parts)]
        both = dot(jnp.concatenate(pieces, axis=0), onehot[s])
        value = jnp.zeros((own, points), f32)
        for k in range(parts):
            value = value + facts[s, 6 + k : 7 + k, :] * (
                both[16 * k : 16 * k + 8] + both[16 * k + 8 : 16 * k + 16]
            )
        spoken[s] = value
        spoken_rows.append(value)
    pairs = members // 2
    speed_out[...] = jnp.concatenate(
        [
            jnp.concatenate(spoken_rows[:pairs], axis=1),
            jnp.concatenate(spoken_rows[pairs:], axis=1),
        ], axis=0
    ).astype(bf16)
    each(1, members, lambda d: speed_copy(d).start())
    speed_in[me] = speed_out[...]

    @pl.loop(0, parts)
    def _(part):
        interior(part, SUBSTEPS % 2)

    each(1, members, lambda d: speed_copy(d).wait_recv())

    arrived = [speed_in[s].astype(f32) for s in range(members)]
    for part in range(2):
        pieces = [value[part * own : (part + 1) * own] for value in arrived]
        gathered_speeds[:, part * pairs * points : (part + 1) * pairs * points] = (
            jnp.concatenate(pieces, axis=0).astype(bf16)
        )
    send_pressures(1, gathered_speeds)
    take_pressures(1)

    @pl.loop(SUBSTEPS, last_step)
    def _(step):
        @pl.loop(0, parts, unroll=parts)
        def _(part):
            advance(part, step, False)

    @pl.loop(0, parts)
    def _(part):
        advance(part, last_step, True)
        done = 1 - last_step % 2
        states = (u_now.at[done, part, pl.ds(REACH, columns)], v_now.at[part])
        tops = [largest(state[...].reshape(columns * layers, own, half)) for state in states]
        for f, top in enumerate(tops):
            scale_out[part, :, f * (half // 2) : (f + 1) * (half // 2)] = jnp.broadcast_to(
                top * (1.0 / LEVELS), (1, half // 2)
            )
        each(1, members, lambda d: scale_copy(part, d).start())
        for f, state in enumerate(states):
            inverse = LEVELS / tops[f]
            for x in range(PAIR):
                for t in range(breadth // 4):
                    given = [state[x * breadth + t * 4 + g] * inverse for g in range(4)]
                    for r, value in enumerate(exchange(given)):
                        final_out[part, f, r * PAIR + x, :, tile_lanes(t)] = (
                            jnp.round(value).astype(i32).astype(i16)
                        )
            each(1, members, lambda d: final_copy(part, f, d).start())
            final_in[part, f, me] = final_out[part, f, me]
        scale_in[part, me] = scale_out[part]

    @pl.loop(0, parts)
    def _(part):
        each(1, members, lambda d: scale_copy(part, d).wait_recv())
        for f, result in enumerate((u_out, v_out)):
            each(1, members, lambda d: final_copy(part, f, d).wait_recv())
            scale = scale_in[part, :, :, f * (half // 2) : f * (half // 2) + 1]
            rows = final_in[part, f].astype(i32).astype(f32) * scale
            rows = jnp.concatenate(
                [
                    rows[:, layer * own : (layer + 1) * own].reshape(LOADS, count)
                    for layer in range(layers)
                ], axis=0
            )
            high = rows.astype(bf16)
            low = (rows - high.astype(f32)).astype(bf16)
            back = dot_turned(eye[...], high) + dot_turned(eye[...], low)
            for j in range(breadth):
                for lanes in range(2):
                    lines = pl.ds(lanes * breadth + j, height, stride=2 * breadth)
                    result[part, lines, :] = back[
                        j * height : (j + 1) * height, lanes * half : (lanes + 1) * half
                    ]

    each(1, members, lambda d: facts_copy(d).wait_send())
    each(1, depth_count, lambda d: places_copy(d).wait_send())
    each(1, members, lambda d: first_copy(d).wait_send())
    each(1, members, lambda d: in_copy(d).wait_send())
    each(1, members, lambda d: speed_copy(d).wait_send())
    for repeat in range(COUPLED):
        parts_sent(repeat)

    @pl.loop(0, parts)
    def _(part):
        for f in range(2):
            each(1, members, lambda d: final_copy(part, f, d).wait_send())
        each(1, members, lambda d: scale_copy(part, d).wait_send())

        @pl.loop(0, last_step + 1)
        def _(step):
            for side in range(2):

                @pl.when(present[side])
                def _():
                    halo_copy(step, part, side, False).wait_send()


def plane_on_device(shape, displacement, velocity, stiffness, wet_position, wet_normal, wet_area, wet_map):
    col_count, row_count, _ = shape
    depth_count = col_count // PAIR
    members = row_count * PAIR
    parts, height, breadth, width = displacement.shape
    half = width // 2
    points = wet_map.shape[0]
    count = height * breadth
    own = LOADS // members
    block = own * (width // LOADS)
    steps = COUPLED * SUBSTEPS
    f32, bf16, i16 = jnp.float32, jnp.bfloat16, jnp.int16
    dma = pltpu.SemaphoreType.DMA

    def separated(state):
        tiled = state.reshape(parts, height, breadth, 2, half).transpose(0, 1, 3, 2, 4)
        return tiled.reshape(parts, height * 2 * breadth, half)

    def joined(state):
        tiled = state.reshape(parts, height, 2, breadth, half).transpose(0, 1, 3, 2, 4)
        return tiled.reshape(parts, height, breadth, width)

    raw = (parts, height * 2 * breadth, half)
    state = jax.ShapeDtypeStruct(raw, f32)
    columns = PAIR * breadth
    anywhere = pl.BlockSpec(memory_space=pl.ANY)
    slab = (members, parts, 2 * block, count)
    final = (parts, 2, members, block, count)
    u_new, v_new = pl.pallas_call(
        functools.partial(plane_kernel, shape),
        out_shape=(state, state),
        in_specs=[anywhere] * 2 + [whole_spec()] * 5,
        out_specs=(whole_spec(), whole_spec()),
        scratch_shapes=[
            VMEM(raw, f32),
            VMEM(raw, f32),
            VMEM((width + LOADS, width), bf16),
            VMEM((count, count), bf16),
            VMEM((count, count), bf16),
            VMEM(slab, i16),
            VMEM(slab, i16),
            VMEM((16, points), f32),
            VMEM((members, 16, points), f32),
            VMEM((8, points), f32),
            VMEM((depth_count, 8, points), f32),
            VMEM((members, 6, points, half), f32),
            VMEM((LOADS, points), bf16),
            VMEM((members, LOADS, points), bf16),
            VMEM((depth_count, members * points, points), bf16),
            VMEM((COUPLED, depth_count, LOADS, points), f32),
            VMEM((COUPLED, depth_count, members, own, points), f32),
            VMEM((COUPLED, depth_count, members, 2 * own, half), bf16),
            VMEM((COUPLED, depth_count, members, 2 * own, half), bf16),
            VMEM((members, own, points), f32),
            VMEM((members, count, points), bf16),
            VMEM((members, points, count), bf16),
            VMEM((2, parts, columns + 2 * REACH, block, half), f32),
            VMEM((parts, columns, block, half), f32),
            VMEM((parts, columns, own, half), f32),
            VMEM((2, parts, columns // 2, 2 * block, 2 * half), bf16),
            VMEM((parts, columns * block, 2 * half), f32),
            VMEM((members, parts * own, count), f32),
            VMEM((columns, 8, half), f32),
            VMEM((LOADS, points), f32),
            VMEM((LOADS, members * points), bf16),
            VMEM((steps, parts, 2, REACH, block, half), bf16),
            VMEM((steps, parts, 2, REACH, block, half), bf16),
            VMEM((2 * own, members // 2 * points), bf16),
            VMEM((members, 2 * own, members // 2 * points), bf16),
            VMEM(final, i16),
            VMEM(final, i16),
            VMEM((parts, 1, half), f32),
            VMEM((parts, members, 1, half), f32),
            dma((2,)),
            dma((members,)),
            dma((members,)),
            dma((depth_count,)),
            dma((depth_count,)),
            dma((members,)),
            dma((members,)),
            dma((members,)),
            dma((members,)),
            dma((COUPLED, depth_count, members)),
            dma((COUPLED, depth_count, members)),
            dma((steps, parts, 2)),
            dma((steps, parts, 2)),
            dma((members,)),
            dma((members,)),
            dma((parts, 2, members)),
            dma((parts, 2, members)),
            dma((parts, members)),
            dma((parts, members)),
        ],
        compiler_params=pltpu.CompilerParams(
            collective_id=0, has_side_effects=True, vmem_limit_bytes=48000000
        ),
        name="plane_steps",
    )(
        pltpu.with_memory_space_constraint(separated(displacement), pltpu.HBM),
        pltpu.with_memory_space_constraint(separated(velocity), pltpu.HBM),
        stiffness.T, wet_position, wet_normal,
        wet_area[None, :], wet_map[None, :],
    )
    return (joined(u_new), joined(v_new))


def by_planes(shape, displacement, wet_map):
    col_count, row_count, _ = shape
    _, height, breadth, width = displacement.shape
    members = row_count * PAIR
    return (
        col_count % (2 * PAIR) == 0
        and LOADS % members == 0
        and LOADS // members == 8
        and height * breadth == wet_map.shape[0] == width == 256
        and row_count == 4
        and height == 32
    )


def either(shape, *arrays):
    chosen = plane_on_device if by_planes(shape, arrays[0], arrays[-1]) else on_device
    return chosen(shape, *arrays)


def solution(mesh):
    sizes = mesh.shape
    shape = (sizes["tcol"], sizes["group"] * sizes["trow"], sizes["trow"])
    state = P(None, ("group", "trow"), "tcol", None)
    wet = ("group", "trow", "tcol")
    return jax.shard_map(
        functools.partial(either, shape),
        mesh=mesh,
        in_specs=(
            state,
            state,
            P(("group", "trow"), "tcol"),
            P(None, wet),
            P(None, wet),
            P(wet),
            P(wet),
        ),
        out_specs=(state, state),
        check_vma=False,
    )
```
